32 devices in a mesh: docs: 8 (over z, y), anch: 4 (over x, core).
Axes of the slice: x: 2, y: 2, z: 4, core: 2. Of those that a mesh axis runs over, the one named last changes fastest.
Arguments:
- features: bfloat16 [65536, 128], P('docs'), may hold values from -6 to 6
- anchors: bfloat16 [1024, 128], P('anch'), may hold values from -6 to 6
- lab_index: int32 [128], P('docs'), may hold values from 0 to 65535, as said below
- lab_class: int32 [128], P('docs'), may hold values from 0 to 15
Outputs:
- anchor_scores: float32 [1024, 16], P('anch')
- doc_scores: float32 [16, 65536], P('anch', 'docs')
The draws below stay inside these ranges and needn't reach their ends.
Inputs may be any that keep to these rules, and one draw needn't show every extreme that they name: Entries k * 16 to (k + 1) * 16 - 1 of lab_index name documents k * 8192 to (k + 1) * 8192 - 1; an index may repeat.
All inputs are finite; a program needn't handle non-finite values.
Results may differ from the reference program's by a relative error of at most 0.0003.
Values may be sent and summed in bfloat16 or wider, within the bound.
No kernel may reach another device: no remote copies, remote signals or barrier semaphores. Data moves between devices by JAX's collectives and lax.ppermute only.
A program may use at most 64 MiB of HBM per device.

```python
import jax
import jax.numpy as jnp
from jax import lax

ANCHORS = 1024
FEAT = 128
CLASSES = 16
DOC_DEV = 8192
LAB_DEV = 16
ITERS = 2
DOCS = 65536
LABELED = 128
N_DOCS = 8


def draw_lab_index(key, part):
    offsets = jax.random.randint(key, (LABELED,), 0, DOC_DEV, dtype=jnp.int32)
    positions = jnp.arange(LABELED, dtype=jnp.int32)
    offsets = jnp.where(positions == 0, 0, offsets).astype(jnp.int32)
    offsets = jnp.where(positions == LABELED - 1, DOC_DEV - 1, offsets).astype(jnp.int32)
    blocks = positions // LAB_DEV
    return (blocks * DOC_DEV + offsets).astype(jnp.int32)


def place_ends(values, stream_key, smallest, largest):
    spot = [jax.random.randint(jax.random.fold_in(stream_key, axis), (), 0, length) for axis, length in enumerate(values.shape)]
    widest = values.shape.index(max(values.shape))
    neighbour = spot[:widest] + [(spot[widest] + 1) % values.shape[widest]] + spot[widest + 1:]
    return values.at[tuple(spot)].set(smallest).at[tuple(neighbour)].set(largest)


def block_scale(key, shape, split, smallest, high):
    level, own = 1.0, jax.random.fold_in(key, 6)
    for position, blocks in split:
        heights = jnp.exp(jax.random.uniform(jax.random.fold_in(own, position), (blocks,), jnp.float32, smallest / len(split), high / len(split)))
        level = level * jnp.repeat(heights, shape[position] // blocks).reshape([-1 if axis == position else 1 for axis in range(len(shape))])
    return level


def normal_values(key, shape, scale, bound, split=(), held_as=jnp.bfloat16):
    entries = jax.random.normal(key, shape, jnp.float32) * scale
    if len(split) > 0:
        entries = block_scale(key, shape, split, -0.22, 0.18) * entries
    return jnp.clip(entries, min=-bound, max=bound).astype(held_as)


def setup_inputs(seed: int = 0) -> dict:
    keys = jax.random.split(jax.random.key(seed), 5)
    return {
        "features": normal_values(keys[0], (DOCS, FEAT), 1.0, 6.0, ((0, 8),)),
        "anchors": normal_values(keys[1], (ANCHORS, FEAT), 1.0, 6.0, ((0, 4),)),
        "lab_index": draw_lab_index(jax.random.fold_in(keys[4], 71), 0),
        "lab_class": place_ends(jax.random.randint(keys[3], (LABELED,), 0, CLASSES), jax.random.fold_in(keys[3], 1), 0, CLASSES - 1).astype(jnp.int32),
    }


width_h = 0.25
ridge = 0.1


def kernel_rows(block, anchors):
    cross = jnp.dot(block, anchors.T, preferred_element_type=jnp.float32)
    row_sq = jnp.sum(jnp.square(block.astype(jnp.float32)), axis=1)
    col_sq = jnp.sum(jnp.square(anchors.astype(jnp.float32)), axis=1)
    dist = (row_sq[:, None] + col_sq[None, :] - 2.0 * cross) / FEAT
    ratio = width_h / (width_h + dist)
    square = ratio * ratio
    fourth = square * square
    kern = fourth * fourth
    return kern / jnp.sum(kern, axis=1, keepdims=True)


def reference(features, anchors, lab_index, lab_class):
    highest = lax.Precision.HIGHEST
    blocks = features.reshape(N_DOCS, DOC_DEV, FEAT)

    def col_sum(carry, block):
        return carry + jnp.sum(kernel_rows(block, anchors), axis=0), None

    degree, _ = lax.scan(col_sum, jnp.zeros((ANCHORS,), jnp.float32), blocks)
    zlab = kernel_rows(features[lab_index], anchors)
    onehot = (lab_class[:, None] == jnp.arange(CLASSES)[None, :]).astype(jnp.float32)
    rhs = (ANCHORS * CLASSES / LABELED) * jnp.dot(zlab.T, onehot, precision=highest)

    def gram(vec):
        def step(carry, block):
            zmat = kernel_rows(block, anchors)
            spread = jnp.dot(zmat, vec, precision=highest)
            return carry + jnp.dot(zmat.T, spread, precision=highest), None
        total, _ = lax.scan(step, jnp.zeros((ANCHORS, CLASSES), jnp.float32), blocks)
        return total

    def operate(vec):
        first = gram(vec)
        labeled = jnp.dot(zlab.T, jnp.dot(zlab, vec, precision=highest), precision=highest)
        back = gram(first / degree[:, None])
        return (ANCHORS / LABELED) * labeled + (ANCHORS * ANCHORS / DOCS) * (first - back) + ridge * vec

    solution = jnp.zeros((ANCHORS, CLASSES), jnp.float32)
    resid = rhs
    direc = rhs
    norm_now = jnp.sum(resid * resid)
    for step in range(ITERS):
        image = operate(direc)
        alpha = norm_now / jnp.sum(direc * image)
        solution = solution + alpha * direc
        resid = resid - alpha * image
        norm_next = jnp.sum(resid * resid)
        direc = resid + (norm_next / norm_now) * direc
        norm_now = norm_next

    def score_step(carry, block):
        return carry, jnp.dot(kernel_rows(block, anchors), solution, precision=highest)

    _, scores = lax.scan(score_step, jnp.zeros((), jnp.float32), blocks)
    return solution, scores.reshape(DOCS, CLASSES).T
```

```python
import functools

import jax
import jax.numpy as jnp
from jax import lax
from jax.experimental import pallas as pl
from jax.experimental.pallas import tpu as pltpu
from jax.sharding import PartitionSpec as P

CLASSES = 16
HALF = CLASSES // 2

width_h = 0.25
ridge = 0.1
highest = lax.Precision.HIGHEST
f32 = jnp.float32
bf16 = jnp.bfloat16
EVERY = ("docs", "anch")
LANES = 128

NT = (((1,), (1,)), ((), ()))
NN = (((1,), (0,)), ((), ()))


def mm(left, right, dims=NN, precision=None):
    return lax.dot_general(left, right, dims, precision=precision, preferred_element_type=f32)


def split2(value):
    high = value.astype(bf16)
    return high, (value - high.astype(f32)).astype(bf16)


def swap(value, mask):
    count = lax.axis_size("docs") * lax.axis_size("anch")
    return lax.ppermute(value, EVERY, [(i, i ^ mask) for i in range(count)])


def bit_groups(bits):
    groups = []
    while bits:
        part, bits = bits[:2], bits[2:]
        masks = [1 << part[0]]
        if len(part) == 2:
            masks += [1 << part[1], (1 << part[0]) | (1 << part[1])]
        groups.append(masks)
    return groups


def sum_stage(held, masks):
    got = [swap(held, mask) for mask in masks]
    if len(got) == 1:
        return held + got[0]
    return (held + got[0]) + (got[1] + got[2])


def reduce_all(mine, send, n_bits):
    held = mine + swap(send, 1)
    for masks in bit_groups(list(range(1, n_bits))):
        held = sum_stage(held, masks)
    return held, swap(held, 1)


def aug_columns(first, second, rows):
    lane = lax.broadcasted_iota(jnp.int32, (rows, LANES), 1)
    out = jnp.zeros((rows, LANES), f32)
    for base, column in ((0, first), (3, second)):
        if column is None:
            out = jnp.where((lane >= base) & (lane < base + 3), 1.0, out)
        else:
            rest = column
            for piece in range(3):
                part = rest.astype(bf16).astype(f32)
                out = jnp.where(lane == base + piece, part, out)
                rest = rest - part
    return out.astype(bf16)


def eighth(value):
    square = value * value
    fourth = square * square
    return 1.0 / (fourth * fourth)


def label_kernel(docs_dev, na, me_ref, idx_ref, cls_ref, feat_ref, out_ref, rows, sems):
    base = (me_ref[0] // na) * docs_dev
    count = idx_ref.shape[0]
    copies = []
    for k in range(count):
        local = idx_ref[k] - base
        start = pl.multiple_of((local >> 4) << 4, 16)
        copy = pltpu.make_async_copy(feat_ref.at[pl.ds(start, 16), :], rows.at[k], sems.at[k])
        copy.start()
        copies.append(copy)
    sub = lax.broadcasted_iota(jnp.int32, (16, LANES), 0)
    lane = lax.broadcasted_iota(jnp.int32, (1, LANES), 1)
    for k in range(count):
        out_ref[count + k : count + k + 1, :] = jnp.where(lane == cls_ref[k], 1.0, 0.0)
    for k in range(count):
        copies[k].wait()
        inside = (idx_ref[k] - base) & 15
        chosen = jnp.where(sub == inside, rows[k].astype(f32), 0.0)
        out_ref[k : k + 1, :] = jnp.sum(chosen, axis=0, keepdims=True)


def build_kernel(na, chunk, me_ref, a0, a1, a2, a3, x_ref, khi_ref, klo_ref, tinv_ref, aug_ref, xaug):
    feat = x_ref.shape[1]
    quarter = a0.shape[0]
    scale = 1.0 / (feat * width_h)
    me = me_ref[0] % na

    @pl.when(pl.program_id(0) == 0)
    def _():
        for mask, piece in enumerate((a0, a1, a2, a3)):
            at = pl.ds(pl.multiple_of((me ^ mask) * quarter, quarter), quarter)
            value = piece[...].astype(f32)
            size = jnp.sum(value * value, axis=1, keepdims=True) * scale + 1.0
            aug_ref[at, 0:feat] = (value * (-2.0 * scale)).astype(bf16)
            aug_ref[at, feat : feat + LANES] = aug_columns(size, None, quarter)

    value = x_ref[...].astype(f32)
    size = jnp.sum(value * value, axis=1, keepdims=True) * scale
    xaug[:, 0:feat] = x_ref[...]
    xaug[:, feat : feat + LANES] = aug_columns(None, size, x_ref.shape[0])
    right = xaug[...]
    total = jnp.zeros((8, x_ref.shape[0]), f32)
    for at in range(0, aug_ref.shape[0], chunk):
        kern = eighth(mm(aug_ref[at : at + chunk, :], right, NT))
        high, low = split2(kern)
        khi_ref[at : at + chunk, :] = high
        klo_ref[at : at + chunk, :] = low
        total = total + jnp.sum(kern.reshape(chunk // 8, 8, -1), axis=0)
    tinv_ref[...] = 1.0 / jnp.sum(total, axis=0, keepdims=True)


def apply_block(vec, khi_ref, klo_ref, tinv_ref):
    both = mm(vec[...], khi_ref[...])
    low = mm(vec[0:CLASSES, :], klo_ref[...])
    return (both[0:CLASSES] + (both[CLASSES:] + low)) * tinv_ref[...]


def gather_block(spread, khi_ref, klo_ref, tinv_ref, with_degree):
    tinv = tinv_ref[...]
    high, low = split2(spread * tinv)
    parts, second = [high, low], [high]
    if with_degree:
        row = lax.broadcasted_iota(jnp.int32, (CLASSES, tinv.shape[1]), 0)
        thigh = tinv.astype(bf16).astype(f32)
        ones = jnp.where(row == 0, thigh, jnp.where(row == 1, tinv - thigh, 0.0)).astype(bf16)
        parts.append(ones)
        second.append(ones)
    one = mm(jnp.concatenate(parts, axis=0), khi_ref[...], NT)
    two = mm(jnp.concatenate(second, axis=0), klo_ref[...], NT)
    out = one[0:CLASSES] + (one[CLASSES : 2 * CLASSES] + two[0:CLASSES])
    if not with_degree:
        return out, None
    deg = one[2 * CLASSES :] + two[CLASSES:]
    return out, deg[0:1] + deg[1:2]


def set_vec(vec, value):
    high, low = split2(value)
    vec[0:CLASSES, :] = high
    vec[CLASSES:, :] = low


def put_halves(acc, me, mine_ref, send_ref):
    core = me & 1
    mine_ref[...] = acc[pl.ds(pl.multiple_of(core * HALF, HALF), HALF), :]
    send_ref[...] = acc[pl.ds(pl.multiple_of((1 - core) * HALF, HALF), HALF), :]


def take_halves(acc, me, mine_ref, got_ref):
    core = me & 1
    acc[pl.ds(pl.multiple_of(core * HALF, HALF), HALF), :] = mine_ref[...]
    acc[pl.ds(pl.multiple_of((1 - core) * HALF, HALF), HALF), :] = got_ref[...]


def centred(value):
    return value - jnp.mean(value, axis=1, keepdims=True)


def first_kernel(
    na, labs, slots, gain, me_ref, *refs
):
    lab_refs = refs[: len(slots)]
    (aug_ref, khi_ref, klo_ref, tinv_ref, mine_ref, send_ref, rhs_ref, zlab_ref, spread_ref,
     laug, hot, vec, acc, mean) = refs[len(slots) :]
    step = pl.program_id(0)
    anchors = aug_ref.shape[0]
    feat = laug.shape[1] - LANES

    @pl.when(step == 0)
    def _():
        docs = me_ref[0] // na
        for masks, ref in zip(slots, lab_refs):
            for k, mask in enumerate(masks):
                at = pl.ds(pl.multiple_of((docs ^ mask) * labs, labs), labs)
                laug[at, 0:feat] = ref[2 * labs * k : 2 * labs * k + labs, :].astype(bf16)
                hot[at, :] = ref[2 * labs * k + labs : 2 * labs * (k + 1), :].astype(f32)
        value = laug[:, 0:feat].astype(f32)
        scale = 1.0 / (feat * width_h)
        size = jnp.sum(value * value, axis=1, keepdims=True) * scale
        laug[:, feat:] = aug_columns(None, size, laug.shape[0])
        kern = eighth(mm(aug_ref[...], laug[...], NT))
        zlab = kern / jnp.sum(kern, axis=0, keepdims=True)
        zlab_ref[...] = zlab
        onehot = hot[...].T[0:CLASSES, :]
        rhs = gain * mm(onehot, zlab, NT, highest)
        rhs_ref[...] = rhs
        middle = jnp.mean(rhs, axis=1, keepdims=True)
        mean[...] = jnp.broadcast_to(middle, mean.shape)
        set_vec(vec, rhs - middle)
        acc[...] = jnp.zeros_like(acc)

    spread = apply_block(vec, khi_ref, klo_ref, tinv_ref)
    spread_ref[...] = spread + mean[:, 0:1]
    out, deg = gather_block(spread, khi_ref, klo_ref, tinv_ref, True)
    acc[:, 0:anchors] += out
    for k in range(anchors // LANES):
        acc[k : k + 1, anchors:] += deg[:, k * LANES : (k + 1) * LANES]

    @pl.when(step == pl.num_programs(0) - 1)
    def _():
        put_halves(acc, me_ref[0], mine_ref, send_ref)


def second_kernel(me_ref, held_ref, got_ref, rhs_ref, khi_ref, klo_ref, tinv_ref,
                  mine_ref, send_ref, dinv_ref, vec, whole, acc):
    step = pl.program_id(0)
    anchors = rhs_ref.shape[1]

    @pl.when(step == 0)
    def _():
        take_halves(whole, me_ref[0], held_ref, got_ref)
        for k in range(anchors // LANES):
            dinv_ref[:, k * LANES : (k + 1) * LANES] = 1.0 / whole[k : k + 1, anchors:]
        set_vec(vec, centred(rhs_ref[...]) - whole[:, 0:anchors] * dinv_ref[...])
        acc[...] = jnp.zeros_like(acc)

    spread = apply_block(vec, khi_ref, klo_ref, tinv_ref)
    out, _ = gather_block(spread, khi_ref, klo_ref, tinv_ref, False)
    acc[...] += out

    @pl.when(step == pl.num_programs(0) - 1)
    def _():
        put_halves(acc, me_ref[0], mine_ref, send_ref)


def total_of(value):
    return jnp.sum(jnp.sum(value, axis=1, keepdims=True), axis=0, keepdims=True)


def third_kernel(na, lab_scale, graph_scale, me_ref, held_ref, got_ref, rhs_ref, lab_ref, spread0_ref,
                 khi_ref, klo_ref, tinv_ref, *refs):
    (mine_ref, send_ref, direc_ref, part_ref, next_ref), outs, (vec, acc, stats, slots) = (
        refs[0:5], refs[5 : 5 + na], refs[5 + na :]
    )
    step = pl.program_id(0)
    quarter = CLASSES // na
    me = me_ref[0]

    @pl.when(step == 0)
    def _():
        take_halves(acc, me, held_ref, got_ref)
        rhs = rhs_ref[...]
        image = lab_scale * lab_ref[...] + graph_scale * acc[...] + ridge * rhs
        norm = total_of(rhs * rhs)
        alpha = norm / total_of(rhs * image)
        resid = rhs - alpha * image
        after = total_of(resid * resid)
        direc = resid + (after / norm) * rhs
        direc_ref[...] = direc
        part_ref[...] = alpha * rhs
        next_ref[...] = jnp.broadcast_to(after, next_ref.shape)
        middle = jnp.mean(direc, axis=1, keepdims=True)
        stats[0:CLASSES, :] = jnp.broadcast_to(middle, (CLASSES, LANES))
        stats[CLASSES:, :] = jnp.broadcast_to(alpha, (8, LANES))
        set_vec(vec, direc - middle)
        acc[...] = jnp.zeros_like(acc)

    spread = apply_block(vec, khi_ref, klo_ref, tinv_ref)
    out, _ = gather_block(spread, khi_ref, klo_ref, tinv_ref, False)
    acc[...] += out
    full = spread + stats[0:CLASSES, 0:1]
    part = stats[CLASSES : CLASSES + 1, 0:1] * spread0_ref[...]
    for k in range(na):
        slots[k, 0:quarter, :] = part[k * quarter : (k + 1) * quarter]
        slots[k, quarter : 2 * quarter, :] = full[k * quarter : (k + 1) * quarter]
    for mask in range(na):
        outs[mask][...] = slots[(me % na) ^ mask]

    @pl.when(step == pl.num_programs(0) - 1)
    def _():
        put_halves(acc, me, mine_ref, send_ref)


def label_image_kernel(vec_ref, zlab_ref, out_ref):
    seen = mm(vec_ref[...], zlab_ref[...], NN, highest)
    out_ref[...] = mm(seen, zlab_ref[...], NT, highest)


def label_norm_kernel(lab_scale, vec_ref, zlab_ref, out_ref):
    vec = vec_ref[...]
    seen = mm(vec, zlab_ref[...], NN, highest)
    out_ref[...] = jnp.broadcast_to(lab_scale * total_of(seen * seen) + ridge * total_of(vec * vec), out_ref.shape)


def last_kernel(na, graph_scale, me_ref, held_ref, got_ref, direc_ref, part_ref, next_ref, base_ref, dinv_ref, *refs):
    pieces, (anchor_ref, doc_ref, whole) = refs[0:na], refs[na:]
    me = me_ref[0]
    mine = me % na
    take_halves(whole, me, held_ref, got_ref)
    prod = whole[...]
    direc = direc_ref[...]
    quad = total_of(prod * (centred(direc) - prod * dinv_ref[...]))
    alpha = next_ref[0:1, 0:1] / (base_ref[0:1, 0:1] + graph_scale * quad)
    whole[...] = part_ref[...] + alpha * direc
    rows = anchor_ref.shape[1]
    anchor_ref[...] = whole[:, pl.ds(pl.multiple_of(mine * rows, rows), rows)]
    quarter, docs = doc_ref.shape[0], pieces[0].shape[1]
    for mask in range(na):
        at = pl.ds(pl.multiple_of((mine ^ mask) * docs, docs), docs)
        doc_ref[:, at] = pieces[mask][0:quarter, :] + alpha * pieces[mask][quarter:, :]


def call(kernel, grid, in_specs, out_specs, out_shape, scratch, name, flops=0, moved=0):
    return pl.pallas_call(
        kernel,
        grid_spec=pltpu.PrefetchScalarGridSpec(
            num_scalar_prefetch=1, grid=grid, in_specs=in_specs, out_specs=out_specs, scratch_shapes=scratch
        ),
        out_shape=out_shape,
        name=name,
        compiler_params=pltpu.CompilerParams(dimension_semantics=("arbitrary",) * len(grid)),
        cost_estimate=pl.CostEstimate(flops=flops, bytes_accessed=moved, transcendentals=0),
    )


def whole_spec(shape):
    return pl.BlockSpec(shape, lambda i, me: (0,) * len(shape))


def per_device(features, anchors, lab_index, lab_class):
    docs_dev, feat = features.shape
    nd, na = lax.axis_size("docs"), lax.axis_size("anch")
    n_bits = (nd * na).bit_length() - 1
    a_bits = na.bit_length() - 1
    labs = lab_index.shape[0]
    labeled = labs * nd
    quarter = anchors.shape[0]
    total = quarter * na
    docs = docs_dev // na
    lab_scale = total / labeled
    graph_scale = total * total / (docs_dev * nd)
    assert na == 4 and nd * na == 1 << n_bits and total // LANES <= CLASSES
    sds = jax.ShapeDtypeStruct

    me = lax.axis_index(EVERY).astype(jnp.int32).reshape(1)

    own = pl.pallas_call(
        functools.partial(label_kernel, docs_dev, na),
        grid_spec=pltpu.PrefetchScalarGridSpec(
            num_scalar_prefetch=3,
            grid=(1,),
            in_specs=[pl.BlockSpec(memory_space=pl.ANY)],
            out_specs=pl.BlockSpec((2 * labs, LANES), lambda i, *_: (0, 0)),
            scratch_shapes=[pltpu.VMEM((labs, 16, LANES), bf16), pltpu.SemaphoreType.DMA((labs,))],
        ),
        out_shape=sds((2 * labs, feat), f32),
        name="label_rows",
    )(me, lab_index, lab_class, features).astype(bf16)

    piece = [anchors, swap(anchors, 1), swap(anchors, 2), None]
    piece[3] = swap(piece[2], 1)

    held, masks, stages = own, [0], []
    bits = list(range(a_bits, n_bits))
    stages = bit_groups(bits[:1]) + bit_groups(bits[1:])
    for at, stage in enumerate(stages):
        got = [swap(held, mask) for mask in stage]
        if at < len(stages) - 1:
            masks = masks + [m ^ mask for mask in stage for m in masks]
            held = jnp.concatenate([held] + got, axis=0)
    lab_arrays = [held] + got
    slots = [[m >> a_bits for m in masks]] + [[(m ^ mask) >> a_bits for m in masks] for mask in stages[-1]]

    block = min(256, docs)
    steps = docs // block
    khi, klo, tinv, aug = call(
        functools.partial(build_kernel, na, 128),
        (steps,),
        [whole_spec((quarter, feat))] * 4
        + [pl.BlockSpec((block, feat), lambda i, me: ((me[0] % na) * steps + i, 0))],
        [
            pl.BlockSpec((total, block), lambda i, me: (0, i)),
            pl.BlockSpec((total, block), lambda i, me: (0, i)),
            pl.BlockSpec((1, block), lambda i, me: (0, i)),
            whole_spec((total, feat + LANES)),
        ],
        [sds((total, docs), bf16), sds((total, docs), bf16), sds((1, docs), f32), sds((total, feat + LANES), bf16)],
        [pltpu.VMEM((block, feat + LANES), bf16)],
        "kernel_matrix",
        flops=2 * total * docs * 256,
        moved=4 * total * docs,
    )(me, *piece, features)

    wide = min(512, docs)
    grid = (docs // wide,)
    k_specs = [
        pl.BlockSpec((total, wide), lambda i, me: (0, i)),
        pl.BlockSpec((total, wide), lambda i, me: (0, i)),
        pl.BlockSpec((1, wide), lambda i, me: (0, i)),
    ]
    doc_spec = pl.BlockSpec((CLASSES, wide), lambda i, me: (0, i))
    flat = whole_spec((CLASSES, total))
    half = whole_spec((HALF, total))
    half_sds = sds((HALF, total), f32)
    long = total + LANES
    vec = pltpu.VMEM((2 * CLASSES, total), bf16)
    acc = pltpu.VMEM((CLASSES, total), f32)
    work = dict(flops=8 * total * docs * 64, moved=4 * total * docs)

    mine, send, rhs, zlab, spread = call(
        functools.partial(first_kernel, na, labs, slots, CLASSES * lab_scale),
        grid,
        [whole_spec(arr.shape) for arr in lab_arrays] + [whole_spec((total, feat + LANES))] + k_specs,
        [whole_spec((HALF, long))] * 2 + [flat, whole_spec((total, labeled)), doc_spec],
        [sds((HALF, long), f32)] * 2 + [sds((CLASSES, total), f32), sds((total, labeled), f32), sds((CLASSES, docs), f32)],
        [
            pltpu.VMEM((labeled, feat + LANES), bf16),
            pltpu.VMEM((labeled, LANES), f32),
            vec,
            pltpu.VMEM((CLASSES, long), f32),
            pltpu.VMEM((CLASSES, LANES), f32),
        ],
        "first_gram",
        **work,
    )(me, *lab_arrays, aug, khi, klo, tinv)

    image_lab = pl.pallas_call(
        label_image_kernel, out_shape=sds((CLASSES, total), f32), name="label_image",
        cost_estimate=pl.CostEstimate(flops=1 << 26, bytes_accessed=1 << 20, transcendentals=0),
    )(rhs, zlab)

    held, got = reduce_all(mine, send, n_bits)
    mine, send, dinv = call(
        second_kernel,
        grid,
        [whole_spec((HALF, long))] * 2 + [flat] + k_specs,
        [half, half, whole_spec((1, total))],
        [half_sds, half_sds, sds((1, total), f32)],
        [vec, pltpu.VMEM((CLASSES, long), f32), acc],
        "second_gram",
        **work,
    )(me, held, got, rhs, khi, klo, tinv)

    held, got = reduce_all(mine, send, n_bits)
    part_rows = 2 * CLASSES // na
    mine, send, direc, part, norm, *docs_out = call(
        functools.partial(third_kernel, na, lab_scale, graph_scale),
        grid,
        [half, half, flat, flat, doc_spec] + k_specs,
        [half, half, flat, flat, whole_spec((1, LANES))] + [pl.BlockSpec((part_rows, wide), lambda i, me: (0, i))] * na,
        [half_sds, half_sds, sds((CLASSES, total), f32), sds((CLASSES, total), f32), sds((1, LANES), f32)]
        + [sds((part_rows, docs), f32)] * na,
        [vec, acc, pltpu.VMEM((CLASSES + 8, LANES), f32), pltpu.VMEM((na, part_rows, wide), f32)],
        "third_gram",
        **work,
    )(me, held, got, rhs, image_lab, spread, khi, klo, tinv)

    base = pl.pallas_call(
        functools.partial(label_norm_kernel, lab_scale), out_shape=sds((1, LANES), f32), name="label_norm",
        cost_estimate=pl.CostEstimate(flops=1 << 26, bytes_accessed=1 << 20, transcendentals=0),
    )(direc, zlab)

    held, got = reduce_all(mine, send, n_bits)
    pieces = [docs_out[0]] + [swap(docs_out[mask], mask) for mask in range(1, na)]
    anchor_scores, doc_scores = call(
        functools.partial(last_kernel, na, graph_scale),
        (1,),
        [half, half, flat, flat, whole_spec((1, LANES)), whole_spec((1, LANES)), whole_spec((1, total))]
        + [whole_spec((part_rows, docs))] * na,
        [whole_spec((CLASSES, quarter)), whole_spec((CLASSES // na, docs_dev))],
        [sds((CLASSES, quarter), f32), sds((CLASSES // na, docs_dev), f32)],
        [acc],
        "scores",
    )(me, held, got, direc, part, norm, base, dinv, *pieces)
    return anchor_scores.T, doc_scores


def solution(mesh):
    in_specs = (P("docs", None), P("anch", None), P("docs"), P("docs"))
    out_specs = (P("anch", None), P("anch", "docs"))
    return jax.shard_map(per_device, mesh=mesh, in_specs=in_specs, out_specs=out_specs, check_vma=False)
```

```python
import functools

import jax
import jax.numpy as jnp
from jax import lax
from jax.experimental import pallas as pl
from jax.experimental.pallas import tpu as pltpu
from jax.sharding import PartitionSpec as P

CLASSES = 16
HALF = CLASSES // 2

width_h = 0.25
ridge = 0.1
highest = lax.Precision.HIGHEST
f32 = jnp.float32
bf16 = jnp.bfloat16
EVERY = ("docs", "anch")
LANES = 128

NT = (((1,), (1,)), ((), ()))
NN = (((1,), (0,)), ((), ()))


def mm(left, right, dims=NN, precision=None):
    return lax.dot_general(left, right, dims, precision=precision, preferred_element_type=f32)


def split2(value):
    high = value.astype(bf16)
    return high, (value - high.astype(f32)).astype(bf16)


def swap(value, mask):
    count = lax.axis_size("docs") * lax.axis_size("anch")
    return lax.ppermute(value, EVERY, [(i, i ^ mask) for i in range(count)])


def bit_groups(bits):
    groups = []
    while bits:
        part, bits = bits[:2], bits[2:]
        masks = [1 << part[0]]
        if len(part) == 2:
            masks += [1 << part[1], (1 << part[0]) | (1 << part[1])]
        groups.append(masks)
    return groups


def sum_stage(held, masks):
    got = [swap(held, mask) for mask in masks]
    if len(got) == 1:
        return held + got[0]
    return (held + got[0]) + (got[1] + got[2])


def reduce_all(mine, send, n_bits):
    held = mine + swap(send, 1)
    for masks in bit_groups(list(range(1, n_bits))):
        held = sum_stage(held, masks)
    return held, swap(held, 1)


def aug_columns(first, second, rows):
    lane = lax.broadcasted_iota(jnp.int32, (rows, LANES), 1)
    out = jnp.zeros((rows, LANES), f32)
    for base, column in ((0, first), (3, second)):
        if column is None:
            out = jnp.where((lane >= base) & (lane < base + 3), 1.0, out)
        else:
            rest = column
            for piece in range(3):
                part = rest.astype(bf16).astype(f32)
                out = jnp.where(lane == base + piece, part, out)
                rest = rest - part
    return out.astype(bf16)


def row_sizes(value):
    return jnp.sum(value * value, axis=1, keepdims=True)


def eighth(value):
    square = value * value
    fourth = square * square
    return 1.0 / (fourth * fourth)


def label_kernel(na, me_ref, idx_ref, cls_ref, feat_ref, out_ref, x_ref, rows, picked, sems, xsem):
    docs_dev = feat_ref.shape[0]
    docs = x_ref.shape[0]
    base = (me_ref[0] // na) * docs_dev
    count = idx_ref.shape[0]
    copies = []
    for k in range(count):
        start = pl.multiple_of(((idx_ref[k] - base) >> 4) << 4, 16)
        copy = pltpu.make_async_copy(feat_ref.at[pl.ds(start, 16), :], rows.at[k], sems.at[k])
        copy.start()
        copies.append(copy)
    own = pl.ds(pl.multiple_of((me_ref[0] % na) * docs, docs), docs)
    bulk = pltpu.make_async_copy(feat_ref.at[own, :], x_ref, xsem)
    bulk.start()
    sub = lax.broadcasted_iota(jnp.int32, (16, LANES), 0)
    lane = lax.broadcasted_iota(jnp.int32, (1, LANES), 1)
    for k in range(count):
        picked[count + k : count + k + 1, :] = jnp.where(lane == cls_ref[k], 1.0, 0.0)
    for k in range(count):
        copies[k].wait()
        chosen = jnp.where(sub == ((idx_ref[k] - base) & 15), rows[k].astype(f32), 0.0)
        picked[k : k + 1, :] = jnp.sum(chosen, axis=0, keepdims=True)
    out_ref[...] = picked[...].astype(bf16)
    bulk.wait()


def build_kernel(na, me_ref, a0, a1, a2, a3, x_ref, khi_ref, klo_ref, tinv_ref, aug_ref):
    docs, feat = x_ref.shape
    quarter = a0.shape[0]
    scale = 1.0 / (feat * width_h)
    me = me_ref[0] % na
    for mask, piece in enumerate((a0, a1, a2, a3)):
        at = pl.ds(pl.multiple_of((me ^ mask) * quarter, quarter), quarter)
        value = piece[...].astype(f32)
        aug_ref[at, 0:feat] = (value * (-2.0 * scale)).astype(bf16)
        aug_ref[at, feat:] = aug_columns(row_sizes(value) * scale + 1.0, None, quarter)
    tile = min(256, docs)
    for col in range(0, docs, tile):
        raw = x_ref[col : col + tile, :]
        right = jnp.concatenate([raw, aug_columns(None, row_sizes(raw.astype(f32)) * scale, tile)], axis=1)
        total = jnp.zeros((8, tile), f32)
        for at in range(0, aug_ref.shape[0], 256):
            kern = eighth(mm(aug_ref[at : at + 256, :], right, NT))
            high, low = split2(kern)
            khi_ref[at : at + 256, col : col + tile] = high
            klo_ref[at : at + 256, col : col + tile] = low
            total = total + jnp.sum(kern.reshape(32, 8, tile), axis=0)
        tinv_ref[:, col : col + tile] = 1.0 / jnp.sum(total, axis=0, keepdims=True)


def times(vec, khi, klo):
    both = mm(vec, khi)
    return both[0:CLASSES] + (both[CLASSES:] + mm(vec[0:CLASSES], klo))


def times_back(value, khi, klo):
    high, low = split2(value)
    both = mm(jnp.concatenate([high, low], axis=0), khi, NT)
    return both[0:CLASSES] + (both[CLASSES:] + mm(high, klo, NT))


def pieces(value):
    return jnp.concatenate(split2(value), axis=0)


def gram(vec, khi_ref, klo_ref, tinv_ref, with_degree=False):
    khi, klo, tinv = khi_ref[...], klo_ref[...], tinv_ref[...]
    spread = times(vec, khi, klo) * tinv
    high, low = split2(spread * tinv)
    parts, second = [high, low], [high]
    if with_degree:
        row = lax.broadcasted_iota(jnp.int32, (CLASSES, tinv.shape[1]), 0)
        thigh = tinv.astype(bf16).astype(f32)
        ones = jnp.where(row == 0, thigh, jnp.where(row == 1, tinv - thigh, 0.0)).astype(bf16)
        parts.append(ones)
        second.append(ones)
    one = mm(jnp.concatenate(parts, axis=0), khi, NT)
    two = mm(jnp.concatenate(second, axis=0), klo, NT)
    out = one[0:CLASSES] + (one[CLASSES : 2 * CLASSES] + two[0:CLASSES])
    if not with_degree:
        return spread, out
    deg = one[2 * CLASSES :] + two[CLASSES:]
    return spread, out, deg[0:1] + deg[1:2]


def put_halves(acc, me, mine_ref, send_ref):
    core = me & 1
    mine_ref[...] = acc[pl.ds(pl.multiple_of(core * HALF, HALF), HALF), :]
    send_ref[...] = acc[pl.ds(pl.multiple_of((1 - core) * HALF, HALF), HALF), :]


def take_halves(acc, me, mine_ref, got_ref):
    core = me & 1
    acc[pl.ds(pl.multiple_of(core * HALF, HALF), HALF), :] = mine_ref[...]
    acc[pl.ds(pl.multiple_of((1 - core) * HALF, HALF), HALF), :] = got_ref[...]


def mean_of(value):
    return jnp.mean(value, axis=1, keepdims=True)


def total_of(value):
    return jnp.sum(jnp.sum(value, axis=1, keepdims=True), axis=0, keepdims=True)


def first_kernel(na, labs, slots, gain, me_ref, *refs):
    lab_refs = refs[: len(slots)]
    (aug_ref, khi_ref, klo_ref, tinv_ref, mine_ref, send_ref, rhs_ref, zhi_ref, zlo_ref, spread_ref,
     laug, hot, acc) = refs[len(slots) :]
    anchors = aug_ref.shape[0]
    feat = laug.shape[1] - LANES
    docs = me_ref[0] // na
    for masks, ref in zip(slots, lab_refs):
        for k, mask in enumerate(masks):
            at = pl.ds(pl.multiple_of((docs ^ mask) * labs, labs), labs)
            laug[at, 0:feat] = ref[2 * labs * k : 2 * labs * k + labs, :]
            hot[at, :] = ref[2 * labs * k + labs : 2 * labs * (k + 1), :].astype(f32)
    size = row_sizes(laug[:, 0:feat].astype(f32)) * (1.0 / (feat * width_h))
    laug[:, feat:] = aug_columns(None, size, laug.shape[0])
    kern = eighth(mm(aug_ref[...], laug[...], NT))
    zlab = kern / jnp.sum(kern, axis=0, keepdims=True)
    zhi_ref[...], zlo_ref[...] = split2(zlab)
    onehot = hot[...].T[0:CLASSES, :]
    rhs = gain * mm(onehot, zlab, NT, highest)
    rhs_ref[...] = rhs
    middle = mean_of(rhs)
    spread, out, deg = gram(pieces(rhs - middle), khi_ref, klo_ref, tinv_ref, True)
    spread_ref[...] = spread + middle
    acc[:, 0:anchors] = out
    acc[:, anchors:] = jnp.zeros((CLASSES, LANES), f32)
    for k in range(anchors // LANES):
        acc[k : k + 1, anchors:] = deg[:, k * LANES : (k + 1) * LANES]
    put_halves(acc, me_ref[0], mine_ref, send_ref)


def second_kernel(me_ref, held_ref, got_ref, rhs_ref, zhi_ref, zlo_ref, khi_ref, klo_ref, tinv_ref,
                  mine_ref, send_ref, dinv_ref, lab_ref, whole, acc):
    anchors = rhs_ref.shape[1]
    take_halves(whole, me_ref[0], held_ref, got_ref)
    for k in range(anchors // LANES):
        dinv_ref[:, k * LANES : (k + 1) * LANES] = 1.0 / whole[k : k + 1, anchors:]
    rhs = rhs_ref[...]
    vec = rhs - mean_of(rhs) - whole[:, 0:anchors] * dinv_ref[...]
    acc[...] = gram(pieces(vec), khi_ref, klo_ref, tinv_ref)[1]
    put_halves(acc, me_ref[0], mine_ref, send_ref)
    zhi, zlo = zhi_ref[...], zlo_ref[...]
    lab_ref[...] = times_back(times(pieces(rhs), zhi, zlo), zhi, zlo)


def third_kernel(na, lab_scale, graph_scale, me_ref, held_ref, got_ref, rhs_ref, lab_ref, spread0_ref,
                 zhi_ref, zlo_ref, khi_ref, klo_ref, tinv_ref, *refs):
    (mine_ref, send_ref, direc_ref, part_ref, next_ref), outs, (acc, slots) = refs[0:5], refs[5 : 5 + na], refs[5 + na :]
    quarter = CLASSES // na
    me = me_ref[0]
    take_halves(acc, me, held_ref, got_ref)
    rhs = rhs_ref[...]
    image = lab_scale * lab_ref[...] + graph_scale * acc[...] + ridge * rhs
    norm = total_of(rhs * rhs)
    alpha = norm / total_of(rhs * image)
    resid = rhs - alpha * image
    after = total_of(resid * resid)
    direc = resid + (after / norm) * rhs
    direc_ref[...] = direc
    part_ref[...] = alpha * rhs
    middle = mean_of(direc)
    spread, out = gram(pieces(direc - middle), khi_ref, klo_ref, tinv_ref)
    acc[...] = out
    put_halves(acc, me, mine_ref, send_ref)
    full = spread + middle
    part = alpha * spread0_ref[...]
    for k in range(na):
        slots[k, 0:quarter, :] = part[k * quarter : (k + 1) * quarter]
        slots[k, quarter : 2 * quarter, :] = full[k * quarter : (k + 1) * quarter]
    for mask in range(na):
        outs[mask][...] = slots[(me % na) ^ mask]
    seen = times(pieces(direc), zhi_ref[...], zlo_ref[...])
    base = lab_scale * total_of(seen * seen) + ridge * total_of(direc * direc)
    next_ref[0:8, :] = jnp.broadcast_to(after, (8, LANES))
    next_ref[8:, :] = jnp.broadcast_to(base, (8, LANES))


def last_kernel(na, graph_scale, me_ref, held_ref, got_ref, direc_ref, part_ref, next_ref, dinv_ref, *refs):
    parts, (anchor_ref, doc_ref, whole) = refs[0:na], refs[na:]
    me = me_ref[0]
    mine = me % na
    take_halves(whole, me, held_ref, got_ref)
    prod = whole[...]
    direc = direc_ref[...]
    quad = total_of(prod * (direc - mean_of(direc) - prod * dinv_ref[...]))
    alpha = next_ref[0:1, 0:1] / (next_ref[8:9, 0:1] + graph_scale * quad)
    whole[...] = part_ref[...] + alpha * direc
    rows = anchor_ref.shape[1]
    anchor_ref[...] = whole[:, pl.ds(pl.multiple_of(mine * rows, rows), rows)]
    quarter, docs = doc_ref.shape[0], parts[0].shape[1]
    for mask in range(na):
        at = pl.ds(pl.multiple_of((mine ^ mask) * docs, docs), docs)
        doc_ref[:, at] = parts[mask][0:quarter, :] + alpha * parts[mask][quarter:, :]


VMEM = pl.BlockSpec(memory_space=pltpu.MemorySpace.VMEM)
SMEM = pl.BlockSpec(memory_space=pltpu.MemorySpace.SMEM)


def call(kernel, in_specs, out_shape, scratch, name, flops=1 << 20, moved=1 << 18):
    return pl.pallas_call(
        kernel,
        in_specs=in_specs,
        out_specs=[VMEM] * len(out_shape),
        out_shape=out_shape,
        scratch_shapes=scratch,
        name=name,
        compiler_params=pltpu.CompilerParams(vmem_limit_bytes=24 << 20),
        cost_estimate=pl.CostEstimate(flops=flops, bytes_accessed=moved, transcendentals=0),
    )


def per_device(features, anchors, lab_index, lab_class):
    docs_dev, feat = features.shape
    nd, na = lax.axis_size("docs"), lax.axis_size("anch")
    n_bits = (nd * na).bit_length() - 1
    a_bits = na.bit_length() - 1
    labs = lab_index.shape[0]
    labeled = labs * nd
    quarter = anchors.shape[0]
    total = quarter * na
    docs = docs_dev // na
    lab_scale = total / labeled
    graph_scale = total * total / (docs_dev * nd)
    assert na == 4 and nd * na == 1 << n_bits and total // LANES <= CLASSES and feat == LANES
    sds = jax.ShapeDtypeStruct

    me = lax.axis_index(EVERY).astype(jnp.int32).reshape(1)

    own, mine_x = call(
        functools.partial(label_kernel, na),
        [SMEM, SMEM, SMEM, pl.BlockSpec(memory_space=pl.ANY)],
        [sds((2 * labs, feat), bf16), sds((docs, feat), bf16)],
        [
            pltpu.VMEM((labs, 16, LANES), bf16),
            pltpu.VMEM((2 * labs, LANES), f32),
            pltpu.SemaphoreType.DMA((labs,)),
            pltpu.SemaphoreType.DMA,
        ],
        "label_rows",
    )(me, lab_index, lab_class, features)

    piece = [anchors, swap(anchors, 1), swap(anchors, 2), None]
    piece[3] = swap(piece[2], 1)

    held, masks = own, [0]
    bits = list(range(a_bits, n_bits))
    stages = bit_groups(bits[:1]) + bit_groups(bits[1:])
    for at, stage in enumerate(stages):
        got = [swap(held, mask) for mask in stage]
        if at < len(stages) - 1:
            masks = masks + [m ^ mask for mask in stage for m in masks]
            held = jnp.concatenate([held] + got, axis=0)
    lab_arrays = [held] + got
    slots = [[m >> a_bits for m in masks]] + [[(m ^ mask) >> a_bits for m in masks] for mask in stages[-1]]

    k_sds = sds((total, docs), bf16)
    khi, klo, tinv, aug = call(
        functools.partial(build_kernel, na),
        [SMEM] + [VMEM] * 5,
        [k_sds, k_sds, sds((1, docs), f32), sds((total, feat + LANES), bf16)],
        [],
        "kernel_matrix",
        flops=2 * total * docs * 256,
        moved=4 * total * docs,
    )(me, *piece, mine_x)

    long = total + LANES
    flat_sds = sds((CLASSES, total), f32)
    half_sds = sds((HALF, total), f32)
    z_sds = sds((total, labeled), bf16)
    acc = pltpu.VMEM((CLASSES, total), f32)
    work = dict(flops=8 * total * docs * 64, moved=4 * total * docs)

    mine, send, rhs, zhi, zlo, spread = call(
        functools.partial(first_kernel, na, labs, slots, CLASSES * lab_scale),
        [SMEM] + [VMEM] * (len(lab_arrays) + 4),
        [sds((HALF, long), f32)] * 2 + [flat_sds, z_sds, z_sds, sds((CLASSES, docs), f32)],
        [
            pltpu.VMEM((labeled, feat + LANES), bf16),
            pltpu.VMEM((labeled, LANES), f32),
            pltpu.VMEM((CLASSES, long), f32),
        ],
        "first_gram",
        **work,
    )(me, *lab_arrays, aug, khi, klo, tinv)

    held, got = reduce_all(mine, send, n_bits)
    mine, send, dinv, lab = call(
        second_kernel,
        [SMEM] + [VMEM] * 8,
        [half_sds, half_sds, sds((1, total), f32), flat_sds],
        [pltpu.VMEM((CLASSES, long), f32), acc],
        "second_gram",
        **work,
    )(me, held, got, rhs, zhi, zlo, khi, klo, tinv)

    held, got = reduce_all(mine, send, n_bits)
    part_rows = 2 * CLASSES // na
    mine, send, direc, part, stats, *docs_out = call(
        functools.partial(third_kernel, na, lab_scale, graph_scale),
        [SMEM] + [VMEM] * 10,
        [half_sds, half_sds, flat_sds, flat_sds, sds((16, LANES), f32)] + [sds((part_rows, docs), f32)] * na,
        [acc, pltpu.VMEM((na, part_rows, docs), f32)],
        "third_gram",
        **work,
    )(me, held, got, rhs, lab, spread, zhi, zlo, khi, klo, tinv)

    held, got = reduce_all(mine, send, n_bits)
    parts = [docs_out[0]] + [swap(docs_out[mask], mask) for mask in range(1, na)]
    anchor_scores, doc_scores = call(
        functools.partial(last_kernel, na, graph_scale),
        [SMEM] + [VMEM] * (6 + na),
        [sds((CLASSES, quarter), f32), sds((CLASSES // na, docs_dev), f32)],
        [acc],
        "scores",
    )(me, held, got, direc, part, stats, dinv, *parts)
    return anchor_scores.T, doc_scores


def solution(mesh):
    in_specs = (P("docs", None), P("anch", None), P("docs"), P("docs"))
    out_specs = (P("anch", None), P("anch", "docs"))
    return jax.shard_map(per_device, mesh=mesh, in_specs=in_specs, out_specs=out_specs, check_vma=False)
```

```python
import functools

import jax
import jax.numpy as jnp
from jax import lax
from jax.experimental import pallas as pl
from jax.experimental.pallas import tpu as pltpu
from jax.sharding import PartitionSpec as P


CLASSES = 16
HALF = CLASSES // 2

width_h = 0.25
ridge = 0.1
highest = lax.Precision.HIGHEST
f32 = jnp.float32
bf16 = jnp.bfloat16
EVERY = ("docs", "anch")
LANES = 128

NT = (((1,), (1,)), ((), ()))
NN = (((1,), (0,)), ((), ()))


def mm(left, right, dims=NN, precision=None):
    return lax.dot_general(left, right, dims, precision=precision, preferred_element_type=f32)


def split2(value):
    high = value.astype(bf16)
    return high, (value - high.astype(f32)).astype(bf16)


def swap(value, mask):
    count = lax.axis_size("docs") * lax.axis_size("anch")
    return lax.ppermute(value, EVERY, [(i, i ^ mask) for i in range(count)])


def bit_groups(bits):
    groups = []
    while bits:
        part, bits = bits[:2], bits[2:]
        masks = [1 << part[0]]
        if len(part) == 2:
            masks += [1 << part[1], (1 << part[0]) | (1 << part[1])]
        groups.append(masks)
    return groups


def sum_stage(held, masks):
    got = [swap(held, mask) for mask in masks]
    if len(got) == 1:
        return held + got[0]
    return (held + got[0]) + (got[1] + got[2])


def reduce_all(mine, send, n_bits):
    held = mine + swap(send, 1)
    for masks in bit_groups(list(range(1, n_bits))):
        held = sum_stage(held, masks)
    return held, swap(held, 1)


def aug_columns(first, second, rows):
    lane = lax.broadcasted_iota(jnp.int32, (rows, LANES), 1)
    out = jnp.zeros((rows, LANES), f32)
    for base, column in ((0, first), (3, second)):
        if column is None:
            out = jnp.where((lane >= base) & (lane < base + 3), 1.0, out)
        else:
            rest = column
            for piece in range(3):
                part = rest.astype(bf16).astype(f32)
                out = jnp.where(lane == base + piece, part, out)
                rest = rest - part
    return out.astype(bf16)


def row_sizes(value):
    return jnp.sum(value * value, axis=1, keepdims=True)


def eighth(value):
    square = value * value
    fourth = square * square
    return 1.0 / (fourth * fourth)


def label_kernel(na, me_ref, idx_ref, cls_ref, feat_ref, anch_ref, out_ref, x_ref, a_ref, rows, picked, sems, xsem, asem):
    docs_dev = feat_ref.shape[0]
    docs = x_ref.shape[0]
    base = (me_ref[0] // na) * docs_dev
    count = idx_ref.shape[0]
    copies = []
    for k in range(count):
        start = pl.multiple_of(((idx_ref[k] - base) >> 4) << 4, 16)
        copy = pltpu.make_async_copy(feat_ref.at[pl.ds(start, 16), :], rows.at[k], sems.at[k])
        copy.start()
        copies.append(copy)
    own = pl.ds(pl.multiple_of((me_ref[0] % na) * docs, docs), docs)
    bulk = pltpu.make_async_copy(feat_ref.at[own, :], x_ref, xsem)
    bulk.start()
    points = pltpu.make_async_copy(anch_ref, a_ref, asem)
    points.start()
    sub = lax.broadcasted_iota(jnp.int32, (16, LANES), 0)
    lane = lax.broadcasted_iota(jnp.int32, (1, LANES), 1)
    for k in range(count):
        picked[count + k : count + k + 1, :] = jnp.where(lane == cls_ref[k], 1.0, 0.0)
    for k in range(count):
        copies[k].wait()
        chosen = jnp.where(sub == ((idx_ref[k] - base) & 15), rows[k].astype(f32), 0.0)
        picked[k : k + 1, :] = jnp.sum(chosen, axis=0, keepdims=True)
    out_ref[...] = picked[...].astype(bf16)
    bulk.wait()
    points.wait()


def build_rows(at_rows, value, x_ref, khi_ref, klo_ref, aug_ref, sums):
    docs, feat = x_ref.shape
    scale = 1.0 / (feat * width_h)
    tile = min(256, docs)
    lefts = []
    for at, piece in zip(at_rows, value):
        wide = piece[...].astype(f32)
        left = jnp.concatenate(
            [(wide * (-2.0 * scale)).astype(bf16), aug_columns(row_sizes(wide) * scale + 1.0, None, wide.shape[0])], axis=1
        )
        aug_ref[at, :] = left
        lefts.append(left)
    for k, col in enumerate(range(0, docs, tile)):
        raw = x_ref[col : col + tile, :]
        right = jnp.concatenate([raw, aug_columns(None, row_sizes(raw.astype(f32)) * scale, tile)], axis=1)
        for at, left in zip(at_rows, lefts):
            kern = eighth(mm(left, right, NT))
            high, low = split2(kern)
            khi_ref[at, col : col + tile] = high
            klo_ref[at, col : col + tile] = low
            part = jnp.sum(kern.reshape(-1, 8, tile), axis=0)
            sums[k] = part if sums[k] is None else sums[k] + part
    return sums


def rows_of(me_ref, na, quarter, masks):
    mine = me_ref[0] % na
    return [pl.ds(pl.multiple_of((mine ^ mask) * quarter, quarter), quarter) for mask in masks]


def build_near(na, me_ref, a0, a1, x_ref, khi_ref, klo_ref, aug_ref, sum_ref):
    tile = min(256, x_ref.shape[0])
    sums = [None] * (x_ref.shape[0] // tile)
    build_rows(rows_of(me_ref, na, a0.shape[0], (0, 1)), (a0, a1), x_ref, khi_ref, klo_ref, aug_ref, sums)
    for k, part in enumerate(sums):
        sum_ref[:, k * tile : (k + 1) * tile] = part


def build_far(na, me_ref, a2, a3, x_ref, sum_ref, kh0, kl0, aug0, khi_ref, klo_ref, aug_ref, tinv_ref):
    tile = min(256, x_ref.shape[0])
    sums = [sum_ref[:, k * tile : (k + 1) * tile] for k in range(x_ref.shape[0] // tile)]
    build_rows(rows_of(me_ref, na, a2.shape[0], (2, 3)), (a2, a3), x_ref, khi_ref, klo_ref, aug_ref, sums)
    for k, part in enumerate(sums):
        tinv_ref[:, k * tile : (k + 1) * tile] = 1.0 / jnp.sum(part, axis=0, keepdims=True)


def times(vec, khi, klo):
    both = mm(vec, khi)
    return both[0:CLASSES] + (both[CLASSES:] + mm(vec[0:CLASSES], klo))


def times_back(value, khi, klo):
    high, low = split2(value)
    both = mm(jnp.concatenate([high, low], axis=0), khi, NT)
    return both[0:CLASSES] + (both[CLASSES:] + mm(high, klo, NT))


def pieces(value):
    return jnp.concatenate(split2(value), axis=0)


def gram(vec, khi_ref, klo_ref, tinv_ref, with_degree=False):
    khi, klo, tinv = khi_ref[...], klo_ref[...], tinv_ref[...]
    spread = times(vec, khi, klo) * tinv
    high, low = split2(spread * tinv)
    parts, second = [high, low], [high]
    if with_degree:
        row = lax.broadcasted_iota(jnp.int32, (CLASSES, tinv.shape[1]), 0)
        thigh = tinv.astype(bf16).astype(f32)
        ones = jnp.where(row == 0, thigh, jnp.where(row == 1, tinv - thigh, 0.0)).astype(bf16)
        parts.append(ones)
        second.append(ones)
    one = mm(jnp.concatenate(parts, axis=0), khi, NT)
    two = mm(jnp.concatenate(second, axis=0), klo, NT)
    out = one[0:CLASSES] + (one[CLASSES : 2 * CLASSES] + two[0:CLASSES])
    if not with_degree:
        return spread, out
    deg = one[2 * CLASSES :] + two[CLASSES:]
    return spread, out, deg[0:1] + deg[1:2]


def put_halves(acc, me, mine_ref, send_ref):
    core = me & 1
    mine_ref[...] = acc[pl.ds(pl.multiple_of(core * HALF, HALF), HALF), :]
    send_ref[...] = acc[pl.ds(pl.multiple_of((1 - core) * HALF, HALF), HALF), :]


def take_halves(acc, me, mine_ref, got_ref):
    core = me & 1
    acc[pl.ds(pl.multiple_of(core * HALF, HALF), HALF), :] = mine_ref[...]
    acc[pl.ds(pl.multiple_of((1 - core) * HALF, HALF), HALF), :] = got_ref[...]


def mean_of(value):
    return jnp.mean(value, axis=1, keepdims=True)


def total_of(value):
    return jnp.sum(jnp.sum(value, axis=1, keepdims=True), axis=0, keepdims=True)


def first_kernel(na, labs, slots, gain, me_ref, *refs):
    lab_refs = refs[: len(slots)]
    (aug_ref, khi_ref, klo_ref, tinv_ref, mine_ref, send_ref, rhs_ref, zhi_ref, zlo_ref, spread_ref,
     laug, hot, acc) = refs[len(slots) :]
    anchors = aug_ref.shape[0]
    feat = laug.shape[1] - LANES
    docs = me_ref[0] // na
    for masks, ref in zip(slots, lab_refs):
        for k, mask in enumerate(masks):
            at = pl.ds(pl.multiple_of((docs ^ mask) * labs, labs), labs)
            laug[at, 0:feat] = ref[2 * labs * k : 2 * labs * k + labs, :]
            hot[at, :] = ref[2 * labs * k + labs : 2 * labs * (k + 1), :].astype(f32)
    size = row_sizes(laug[:, 0:feat].astype(f32)) * (1.0 / (feat * width_h))
    laug[:, feat:] = aug_columns(None, size, laug.shape[0])
    kern = eighth(mm(aug_ref[...], laug[...], NT))
    zlab = kern / jnp.sum(kern, axis=0, keepdims=True)
    zhi_ref[...], zlo_ref[...] = split2(zlab)
    onehot = hot[...].T[0:CLASSES, :]
    rhs = gain * mm(onehot, zlab, NT, highest)
    rhs_ref[...] = rhs
    middle = mean_of(rhs)
    spread, out, deg = gram(pieces(rhs - middle), khi_ref, klo_ref, tinv_ref, True)
    spread_ref[...] = spread + middle
    acc[:, 0:anchors] = out
    acc[:, anchors:] = jnp.zeros((CLASSES, LANES), f32)
    for k in range(anchors // LANES):
        acc[k : k + 1, anchors:] = deg[:, k * LANES : (k + 1) * LANES]
    put_halves(acc, me_ref[0], mine_ref, send_ref)


def second_kernel(me_ref, held_ref, got_ref, rhs_ref, zhi_ref, zlo_ref, khi_ref, klo_ref, tinv_ref,
                  mine_ref, send_ref, dinv_ref, lab_ref, whole, acc):
    anchors = rhs_ref.shape[1]
    take_halves(whole, me_ref[0], held_ref, got_ref)
    for k in range(anchors // LANES):
        dinv_ref[:, k * LANES : (k + 1) * LANES] = 1.0 / whole[k : k + 1, anchors:]
    rhs = rhs_ref[...]
    vec = rhs - mean_of(rhs) - whole[:, 0:anchors] * dinv_ref[...]
    acc[...] = gram(pieces(vec), khi_ref, klo_ref, tinv_ref)[1]
    put_halves(acc, me_ref[0], mine_ref, send_ref)
    zhi, zlo = zhi_ref[...], zlo_ref[...]
    lab_ref[...] = times_back(times(pieces(rhs), zhi, zlo), zhi, zlo)


def third_kernel(na, lab_scale, graph_scale, me_ref, held_ref, got_ref, rhs_ref, lab_ref, spread0_ref,
                 zhi_ref, zlo_ref, khi_ref, klo_ref, tinv_ref, *refs):
    (mine_ref, send_ref, direc_ref, part_ref, next_ref), outs, (acc, slots) = refs[0:5], refs[5 : 5 + na], refs[5 + na :]
    quarter = CLASSES // na
    me = me_ref[0]
    take_halves(acc, me, held_ref, got_ref)
    rhs = rhs_ref[...]
    image = lab_scale * lab_ref[...] + graph_scale * acc[...] + ridge * rhs
    norm = total_of(rhs * rhs)
    alpha = norm / total_of(rhs * image)
    resid = rhs - alpha * image
    after = total_of(resid * resid)
    direc = resid + (after / norm) * rhs
    direc_ref[...] = direc
    part_ref[...] = alpha * rhs
    middle = mean_of(direc)
    spread, out = gram(pieces(direc - middle), khi_ref, klo_ref, tinv_ref)
    acc[...] = out
    put_halves(acc, me, mine_ref, send_ref)
    full = spread + middle
    part = alpha * spread0_ref[...]
    for k in range(na):
        slots[k, 0:quarter, :] = part[k * quarter : (k + 1) * quarter]
        slots[k, quarter : 2 * quarter, :] = full[k * quarter : (k + 1) * quarter]
    for mask in range(na):
        outs[mask][...] = slots[(me % na) ^ mask]
    seen = times(pieces(direc), zhi_ref[...], zlo_ref[...])
    base = lab_scale * total_of(seen * seen) + ridge * total_of(direc * direc)
    next_ref[0:8, :] = jnp.broadcast_to(after, (8, LANES))
    next_ref[8:, :] = jnp.broadcast_to(base, (8, LANES))


def last_kernel(na, graph_scale, me_ref, held_ref, got_ref, direc_ref, part_ref, next_ref, dinv_ref, *refs):
    parts, (anchor_ref, doc_ref, whole) = refs[0:na], refs[na:]
    me = me_ref[0]
    mine = me % na
    take_halves(whole, me, held_ref, got_ref)
    prod = whole[...]
    direc = direc_ref[...]
    quad = total_of(prod * (direc - mean_of(direc) - prod * dinv_ref[...]))
    alpha = next_ref[0:1, 0:1] / (next_ref[8:9, 0:1] + graph_scale * quad)
    whole[...] = part_ref[...] + alpha * direc
    rows = anchor_ref.shape[1]
    anchor_ref[...] = whole[:, pl.ds(pl.multiple_of(mine * rows, rows), rows)]
    quarter, docs = doc_ref.shape[0], parts[0].shape[1]
    for mask in range(na):
        at = pl.ds(pl.multiple_of((mine ^ mask) * docs, docs), docs)
        doc_ref[:, at] = parts[mask][0:quarter, :] + alpha * parts[mask][quarter:, :]


VMEM = pl.BlockSpec(memory_space=pltpu.MemorySpace.VMEM)
SMEM = pl.BlockSpec(memory_space=pltpu.MemorySpace.SMEM)


def in_hbm(value):
    return pltpu.with_memory_space_constraint(value, pltpu.MemorySpace.HBM)


def call(kernel, in_specs, out_shape, scratch, flops=1 << 20, moved=1 << 18, aliases={}):
    return pl.pallas_call(
        kernel,
        in_specs=in_specs,
        out_specs=[VMEM] * len(out_shape),
        out_shape=out_shape,
        scratch_shapes=scratch,
        input_output_aliases=aliases,
        compiler_params=pltpu.CompilerParams(vmem_limit_bytes=24 << 20),
        cost_estimate=pl.CostEstimate(flops=flops, bytes_accessed=moved, transcendentals=0),
    )


def run(features, anchors, lab_index, lab_class):
    docs_dev, feat = features.shape
    nd, na = lax.axis_size("docs"), lax.axis_size("anch")
    n_bits = (nd * na).bit_length() - 1
    a_bits = na.bit_length() - 1
    labs = lab_index.shape[0]
    labeled = labs * nd
    quarter = anchors.shape[0]
    total = quarter * na
    docs = docs_dev // na
    lab_scale = total / labeled
    graph_scale = total * total / (docs_dev * nd)
    assert na == 4 and nd * na == 1 << n_bits and total // LANES <= CLASSES and feat == LANES
    sds = jax.ShapeDtypeStruct

    me = lax.axis_index(EVERY).astype(jnp.int32).reshape(1)

    own, mine_x, near = pl.pallas_call(
        functools.partial(label_kernel, na),
        grid_spec=pltpu.PrefetchScalarGridSpec(
            num_scalar_prefetch=3,
            grid=(1,),
            in_specs=[pl.BlockSpec(memory_space=pltpu.MemorySpace.HBM)] * 2,
            out_specs=[VMEM] * 3,
            scratch_shapes=[
                pltpu.VMEM((labs, 16, LANES), bf16),
                pltpu.VMEM((2 * labs, LANES), f32),
                pltpu.SemaphoreType.DMA((labs,)),
                pltpu.SemaphoreType.DMA,
                pltpu.SemaphoreType.DMA,
            ],
        ),
        out_shape=[sds((2 * labs, feat), bf16), sds((docs, feat), bf16), sds((quarter, feat), bf16)],
        name="label_rows",
        compiler_params=pltpu.CompilerParams(vmem_limit_bytes=4 << 20),
    )(me, in_hbm(lab_index), in_hbm(lab_class), in_hbm(features), in_hbm(anchors))

    piece = [near, swap(anchors, 1), swap(anchors, 2), None]
    piece[3] = swap(piece[2], 1)

    held, masks = own, [0]
    bits = list(range(a_bits, n_bits))
    stages = bit_groups(bits[:1]) + bit_groups(bits[1:])
    for at, stage in enumerate(stages):
        got = [swap(held, mask) for mask in stage]
        if at < len(stages) - 1:
            masks = masks + [m ^ mask for mask in stage for m in masks]
            held = jnp.concatenate([held] + got, axis=0)
    lab_arrays = [held] + got
    slots = [[m >> a_bits for m in masks]] + [[(m ^ mask) >> a_bits for m in masks] for mask in stages[-1]]

    k_sds = sds((total, docs), bf16)
    a_sds = sds((total, feat + LANES), bf16)
    build = dict(flops=total * docs * 256, moved=2 * total * docs)
    khi, klo, aug, sums = call(
        functools.partial(build_near, na), [SMEM] + [VMEM] * 3, [k_sds, k_sds, a_sds, sds((8, docs), f32)], [], **build
    )(me, piece[0], piece[1], mine_x)
    khi, klo, aug, tinv = call(
        functools.partial(build_far, na),
        [SMEM] + [VMEM] * 7,
        [k_sds, k_sds, a_sds, sds((1, docs), f32)],
        [],
        aliases={5: 0, 6: 1, 7: 2},
        **build,
    )(me, piece[2], piece[3], mine_x, sums, khi, klo, aug)

    long = total + LANES
    flat_sds = sds((CLASSES, total), f32)
    half_sds = sds((HALF, total), f32)
    z_sds = sds((total, labeled), bf16)
    acc = pltpu.VMEM((CLASSES, total), f32)
    work = dict(flops=8 * total * docs * 64, moved=4 * total * docs)

    mine, send, rhs, zhi, zlo, spread = call(
        functools.partial(first_kernel, na, labs, slots, CLASSES * lab_scale),
        [SMEM] + [VMEM] * (len(lab_arrays) + 4),
        [sds((HALF, long), f32)] * 2 + [flat_sds, z_sds, z_sds, sds((CLASSES, docs), f32)],
        [
            pltpu.VMEM((labeled, feat + LANES), bf16),
            pltpu.VMEM((labeled, LANES), f32),
            pltpu.VMEM((CLASSES, long), f32),
        ],
        **work,
    )(me, *lab_arrays, aug, khi, klo, tinv)

    held, got = reduce_all(mine, send, n_bits)
    mine, send, dinv, lab = call(
        second_kernel,
        [SMEM] + [VMEM] * 8,
        [half_sds, half_sds, sds((1, total), f32), flat_sds],
        [pltpu.VMEM((CLASSES, long), f32), acc],
        **work,
    )(me, held, got, rhs, zhi, zlo, khi, klo, tinv)

    held, got = reduce_all(mine, send, n_bits)
    part_rows = 2 * CLASSES // na
    mine, send, direc, part, stats, *docs_out = call(
        functools.partial(third_kernel, na, lab_scale, graph_scale),
        [SMEM] + [VMEM] * 10,
        [half_sds, half_sds, flat_sds, flat_sds, sds((16, LANES), f32)] + [sds((part_rows, docs), f32)] * na,
        [acc, pltpu.VMEM((na, part_rows, docs), f32)],
        **work,
    )(me, held, got, rhs, lab, spread, zhi, zlo, khi, klo, tinv)

    held, got = reduce_all(mine, send, n_bits)
    parts = [docs_out[0]] + [swap(docs_out[mask], mask) for mask in range(1, na)]
    anchor_scores, doc_scores = call(
        functools.partial(last_kernel, na, graph_scale),
        [SMEM] + [VMEM] * (6 + na),
        [sds((CLASSES, quarter), f32), sds((CLASSES // na, docs_dev), f32)],
        [acc],
    )(me, held, got, direc, part, stats, dinv, *parts)
    return anchor_scores.T, doc_scores


def solution(mesh):
    in_specs = (P("docs", None), P("anch", None), P("docs"), P("docs"))
    out_specs = (P("anch", None), P("anch", "docs"))
    return jax.shard_map(run, mesh=mesh, in_specs=in_specs, out_specs=out_specs, check_vma=False)
```

```python
import functools

import jax
import jax.numpy as jnp
from jax import lax
from jax.experimental import pallas as pl
from jax.experimental.pallas import tpu as pltpu
from jax.sharding import PartitionSpec as P


CLASSES = 16
HALF = CLASSES // 2

width_h = 0.25
ridge = 0.1
highest = lax.Precision.HIGHEST
f32 = jnp.float32
bf16 = jnp.bfloat16
EVERY = ("docs", "anch")
LANES = 128

NT = (((1,), (1,)), ((), ()))
NN = (((1,), (0,)), ((), ()))


def mm(left, right, dims=NN, precision=None):
    return lax.dot_general(left, right, dims, precision=precision, preferred_element_type=f32)


def split2(value):
    high = value.astype(bf16)
    return high, (value - high.astype(f32)).astype(bf16)


def swap(value, mask):
    count = lax.axis_size("docs") * lax.axis_size("anch")
    return lax.ppermute(value, EVERY, [(i, i ^ mask) for i in range(count)])


def bit_groups(bits):
    groups = []
    while bits:
        part, bits = bits[:2], bits[2:]
        masks = [1 << part[0]]
        if len(part) == 2:
            masks += [1 << part[1], (1 << part[0]) | (1 << part[1])]
        groups.append(masks)
    return groups


def exchange(value, masks):
    got = []
    for mask in masks:
        got.append(swap(value, mask))
    return got


def sum_stage(held, masks):
    got = exchange(held, masks)
    if len(got) == 1:
        return held + got[0]
    return (held + got[0]) + (got[1] + got[2])


def reduce_all(mine, send, n_bits):
    held = mine + swap(send, 1)
    for masks in bit_groups(list(range(1, n_bits))):
        held = sum_stage(held, masks)
    return held, swap(held, 1)


def aug_columns(first, second, rows):
    lane = lax.broadcasted_iota(jnp.int32, (rows, LANES), 1)
    out = jnp.zeros((rows, LANES), f32)
    for base, column in ((0, first), (3, second)):
        if column is None:
            out = jnp.where((lane >= base) & (lane < base + 3), 1.0, out)
        else:
            rest = column
            for piece in range(3):
                part = rest.astype(bf16).astype(f32)
                out = jnp.where(lane == base + piece, part, out)
                rest = rest - part
    return out.astype(bf16)


def row_sizes(value):
    return jnp.sum(value * value, axis=1, keepdims=True)


def eighth(value):
    square = value * value
    fourth = square * square
    return 1.0 / (fourth * fourth)


def label_kernel(na, me_ref, idx_ref, cls_ref, feat_ref, anch_ref, out_ref, x_ref, a_ref, rows, picked, sems, xsem, asem):
    docs_dev = feat_ref.shape[0]
    docs = x_ref.shape[0]
    base = (me_ref[0] // na) * docs_dev
    count = idx_ref.shape[0]
    copies = []
    for k in range(count):
        start = pl.multiple_of(((idx_ref[k] - base) >> 4) << 4, 16)
        copy = pltpu.make_async_copy(feat_ref.at[pl.ds(start, 16), :], rows.at[k], sems.at[k])
        copy.start()
        copies.append(copy)
    own = pl.ds(pl.multiple_of((me_ref[0] % na) * docs, docs), docs)
    bulk = pltpu.make_async_copy(feat_ref.at[own, :], x_ref, xsem)
    bulk.start()
    points = pltpu.make_async_copy(anch_ref, a_ref, asem)
    points.start()
    sub = lax.broadcasted_iota(jnp.int32, (16, LANES), 0)
    lane = lax.broadcasted_iota(jnp.int32, (1, LANES), 1)
    for k in range(count):
        picked[count + k : count + k + 1, :] = jnp.where(lane == cls_ref[k], 1.0, 0.0)
    for k in range(count):
        copies[k].wait()
        chosen = jnp.where(sub == ((idx_ref[k] - base) & 15), rows[k].astype(f32), 0.0)
        picked[k : k + 1, :] = jnp.sum(chosen, axis=0, keepdims=True)
    out_ref[...] = picked[...].astype(bf16)
    bulk.wait()
    points.wait()


def build_rows(at_rows, value, x_ref, khi_ref, klo_ref, aug_ref, sums):
    docs, feat = x_ref.shape
    scale = 1.0 / (feat * width_h)
    tile = min(256, docs)
    lefts = []
    for at, piece in zip(at_rows, value):
        wide = piece[...].astype(f32)
        left = jnp.concatenate(
            [(wide * (-2.0 * scale)).astype(bf16), aug_columns(row_sizes(wide) * scale + 1.0, None, wide.shape[0])], axis=1
        )
        aug_ref[at, :] = left
        lefts.append(left)
    for k, col in enumerate(range(0, docs, tile)):
        raw = x_ref[col : col + tile, :]
        right = jnp.concatenate([raw, aug_columns(None, row_sizes(raw.astype(f32)) * scale, tile)], axis=1)
        for at, left in zip(at_rows, lefts):
            kern = eighth(mm(left, right, NT))
            high, low = split2(kern)
            khi_ref[at, col : col + tile] = high
            klo_ref[at, col : col + tile] = low
            part = jnp.sum(kern.reshape(-1, 8, tile), axis=0)
            sums[k] = part if sums[k] is None else sums[k] + part
    return sums


def rows_of(me_ref, na, quarter, masks):
    mine = me_ref[0] % na
    return [pl.ds(pl.multiple_of((mine ^ mask) * quarter, quarter), quarter) for mask in masks]


def build_near(na, me_ref, a0, a1, x_ref, khi_ref, klo_ref, aug_ref, sum_ref):
    tile = min(256, x_ref.shape[0])
    sums = [None] * (x_ref.shape[0] // tile)
    build_rows(rows_of(me_ref, na, a0.shape[0], (0, 1)), (a0, a1), x_ref, khi_ref, klo_ref, aug_ref, sums)
    for k, part in enumerate(sums):
        sum_ref[:, k * tile : (k + 1) * tile] = part


def build_far(na, me_ref, a2, a3, x_ref, sum_ref, kh0, kl0, aug0, khi_ref, klo_ref, aug_ref, tinv_ref):
    tile = min(256, x_ref.shape[0])
    sums = [sum_ref[:, k * tile : (k + 1) * tile] for k in range(x_ref.shape[0] // tile)]
    build_rows(rows_of(me_ref, na, a2.shape[0], (2, 3)), (a2, a3), x_ref, khi_ref, klo_ref, aug_ref, sums)
    for k, part in enumerate(sums):
        tinv_ref[:, k * tile : (k + 1) * tile] = 1.0 / jnp.sum(part, axis=0, keepdims=True)


def times(vec, khi, klo):
    both = mm(vec, khi)
    return both[0:CLASSES] + (both[CLASSES:] + mm(vec[0:CLASSES], klo))


def times_back(value, khi, klo):
    high, low = split2(value)
    both = mm(jnp.concatenate([high, low], axis=0), khi, NT)
    return both[0:CLASSES] + (both[CLASSES:] + mm(high, klo, NT))


def pieces(value):
    return jnp.concatenate(split2(value), axis=0)


def gram(vec, khi_ref, klo_ref, tinv_ref, with_degree=False):
    khi, klo, tinv = khi_ref[...], klo_ref[...], tinv_ref[...]
    spread = times(vec, khi, klo) * tinv
    high, low = split2(spread * tinv)
    parts, second = [high, low], [high]
    if with_degree:
        row = lax.broadcasted_iota(jnp.int32, (CLASSES, tinv.shape[1]), 0)
        thigh = tinv.astype(bf16).astype(f32)
        ones = jnp.where(row == 0, thigh, jnp.where(row == 1, tinv - thigh, 0.0)).astype(bf16)
        parts.append(ones)
        second.append(ones)
    one = mm(jnp.concatenate(parts, axis=0), khi, NT)
    two = mm(jnp.concatenate(second, axis=0), klo, NT)
    out = one[0:CLASSES] + (one[CLASSES : 2 * CLASSES] + two[0:CLASSES])
    if not with_degree:
        return spread, out
    deg = one[2 * CLASSES :] + two[CLASSES:]
    return spread, out, deg[0:1] + deg[1:2]


def put_halves(acc, me, mine_ref, send_ref):
    core = me & 1
    mine_ref[...] = acc[pl.ds(pl.multiple_of(core * HALF, HALF), HALF), :]
    send_ref[...] = acc[pl.ds(pl.multiple_of((1 - core) * HALF, HALF), HALF), :]


def take_halves(acc, me, mine_ref, got_ref):
    core = me & 1
    acc[pl.ds(pl.multiple_of(core * HALF, HALF), HALF), :] = mine_ref[...]
    acc[pl.ds(pl.multiple_of((1 - core) * HALF, HALF), HALF), :] = got_ref[...]


def mean_of(value):
    return jnp.mean(value, axis=1, keepdims=True)


def total_of(value):
    return jnp.sum(jnp.sum(value, axis=1, keepdims=True), axis=0, keepdims=True)


def first_kernel(na, labs, slots, gain, me_ref, *refs):
    lab_refs = refs[: len(slots)]
    (aug_ref, khi_ref, klo_ref, tinv_ref, mine_ref, send_ref, rhs_ref, zhi_ref, zlo_ref, spread_ref,
     laug, hot, acc) = refs[len(slots) :]
    anchors = aug_ref.shape[0]
    feat = laug.shape[1] - LANES
    docs = me_ref[0] // na
    for masks, ref in zip(slots, lab_refs):
        for k, mask in enumerate(masks):
            at = pl.ds(pl.multiple_of((docs ^ mask) * labs, labs), labs)
            laug[at, 0:feat] = ref[2 * labs * k : 2 * labs * k + labs, :]
            hot[at, :] = ref[2 * labs * k + labs : 2 * labs * (k + 1), :].astype(f32)
    size = row_sizes(laug[:, 0:feat].astype(f32)) * (1.0 / (feat * width_h))
    laug[:, feat:] = aug_columns(None, size, laug.shape[0])
    kern = eighth(mm(aug_ref[...], laug[...], NT))
    zlab = kern / jnp.sum(kern, axis=0, keepdims=True)
    zhi_ref[...], zlo_ref[...] = split2(zlab)
    onehot = hot[...].T[0:CLASSES, :]
    rhs = gain * mm(onehot, zlab, NT, highest)
    rhs_ref[...] = rhs
    middle = mean_of(rhs)
    spread, out, deg = gram(pieces(rhs - middle), khi_ref, klo_ref, tinv_ref, True)
    spread_ref[...] = spread + middle
    acc[:, 0:anchors] = out
    acc[:, anchors:] = jnp.zeros((CLASSES, LANES), f32)
    for k in range(anchors // LANES):
        acc[k : k + 1, anchors:] = deg[:, k * LANES : (k + 1) * LANES]
    put_halves(acc, me_ref[0], mine_ref, send_ref)


def second_kernel(me_ref, held_ref, got_ref, rhs_ref, zhi_ref, zlo_ref, khi_ref, klo_ref, tinv_ref,
                  mine_ref, send_ref, dinv_ref, lab_ref, whole, acc):
    anchors = rhs_ref.shape[1]
    take_halves(whole, me_ref[0], held_ref, got_ref)
    for k in range(anchors // LANES):
        dinv_ref[:, k * LANES : (k + 1) * LANES] = 1.0 / whole[k : k + 1, anchors:]
    rhs = rhs_ref[...]
    vec = rhs - mean_of(rhs) - whole[:, 0:anchors] * dinv_ref[...]
    acc[...] = gram(pieces(vec), khi_ref, klo_ref, tinv_ref)[1]
    put_halves(acc, me_ref[0], mine_ref, send_ref)
    zhi, zlo = zhi_ref[...], zlo_ref[...]
    lab_ref[...] = times_back(times(pieces(rhs), zhi, zlo), zhi, zlo)


def third_kernel(na, lab_scale, graph_scale, me_ref, held_ref, got_ref, rhs_ref, lab_ref, spread0_ref,
                 zhi_ref, zlo_ref, khi_ref, klo_ref, tinv_ref, *refs):
    (mine_ref, send_ref, direc_ref, part_ref, next_ref), outs, (acc, slots) = refs[0:5], refs[5 : 5 + na], refs[5 + na :]
    quarter = CLASSES // na
    me = me_ref[0]
    take_halves(acc, me, held_ref, got_ref)
    rhs = rhs_ref[...]
    image = lab_scale * lab_ref[...] + graph_scale * acc[...] + ridge * rhs
    norm = total_of(rhs * rhs)
    alpha = norm / total_of(rhs * image)
    resid = rhs - alpha * image
    after = total_of(resid * resid)
    direc = resid + (after / norm) * rhs
    direc_ref[...] = direc
    part_ref[...] = alpha * rhs
    middle = mean_of(direc)
    spread, out = gram(pieces(direc - middle), khi_ref, klo_ref, tinv_ref)
    acc[...] = out
    put_halves(acc, me, mine_ref, send_ref)
    full = spread + middle
    part = alpha * spread0_ref[...]
    for k in range(na):
        slots[k, 0:quarter, :] = part[k * quarter : (k + 1) * quarter]
        slots[k, quarter : 2 * quarter, :] = full[k * quarter : (k + 1) * quarter]
    for mask in range(na):
        outs[mask][...] = slots[(me % na) ^ mask]
    seen = times(pieces(direc), zhi_ref[...], zlo_ref[...])
    base = lab_scale * total_of(seen * seen) + ridge * total_of(direc * direc)
    next_ref[0:8, :] = jnp.broadcast_to(after, (8, LANES))
    next_ref[8:, :] = jnp.broadcast_to(base, (8, LANES))


def last_kernel(na, graph_scale, me_ref, held_ref, got_ref, direc_ref, part_ref, next_ref, dinv_ref, *refs):
    parts, (anchor_ref, doc_ref, whole) = refs[0:na], refs[na:]
    me = me_ref[0]
    mine = me % na
    take_halves(whole, me, held_ref, got_ref)
    prod = whole[...]
    direc = direc_ref[...]
    quad = total_of(prod * (direc - mean_of(direc) - prod * dinv_ref[...]))
    alpha = next_ref[0:1, 0:1] / (next_ref[8:9, 0:1] + graph_scale * quad)
    whole[...] = part_ref[...] + alpha * direc
    rows = anchor_ref.shape[1]
    anchor_ref[...] = whole[:, pl.ds(pl.multiple_of(mine * rows, rows), rows)]
    quarter, docs = doc_ref.shape[0], parts[0].shape[1]
    for mask in range(na):
        at = pl.ds(pl.multiple_of((mine ^ mask) * docs, docs), docs)
        doc_ref[:, at] = parts[mask][0:quarter, :] + alpha * parts[mask][quarter:, :]


VMEM = pl.BlockSpec(memory_space=pltpu.MemorySpace.VMEM)
SMEM = pl.BlockSpec(memory_space=pltpu.MemorySpace.SMEM)


def in_hbm(value):
    return pltpu.with_memory_space_constraint(value, pltpu.MemorySpace.HBM)


def call(kernel, in_specs, out_shape, scratch, flops=1 << 20, moved=1 << 18, aliases={}):
    return pl.pallas_call(
        kernel,
        in_specs=in_specs,
        out_specs=[VMEM] * len(out_shape),
        out_shape=out_shape,
        scratch_shapes=scratch,
        input_output_aliases=aliases,
        compiler_params=pltpu.CompilerParams(vmem_limit_bytes=24 << 20),
        cost_estimate=pl.CostEstimate(flops=flops, bytes_accessed=moved, transcendentals=0),
    )


def run(features, anchors, lab_index, lab_class):
    docs_dev, feat = features.shape
    nd, na = lax.axis_size("docs"), lax.axis_size("anch")
    n_bits = (nd * na).bit_length() - 1
    a_bits = na.bit_length() - 1
    labs = lab_index.shape[0]
    labeled = labs * nd
    quarter = anchors.shape[0]
    total = quarter * na
    docs = docs_dev // na
    lab_scale = total / labeled
    graph_scale = total * total / (docs_dev * nd)
    assert na == 4 and nd * na == 1 << n_bits and total // LANES <= CLASSES and feat == LANES
    sds = jax.ShapeDtypeStruct

    me = lax.axis_index(EVERY).astype(jnp.int32).reshape(1)

    own, mine_x, near = pl.pallas_call(
        functools.partial(label_kernel, na),
        grid_spec=pltpu.PrefetchScalarGridSpec(
            num_scalar_prefetch=3,
            grid=(1,),
            in_specs=[pl.BlockSpec(memory_space=pltpu.MemorySpace.HBM)] * 2,
            out_specs=[VMEM] * 3,
            scratch_shapes=[
                pltpu.VMEM((labs, 16, LANES), bf16),
                pltpu.VMEM((2 * labs, LANES), f32),
                pltpu.SemaphoreType.DMA((labs,)),
                pltpu.SemaphoreType.DMA,
                pltpu.SemaphoreType.DMA,
            ],
        ),
        out_shape=[sds((2 * labs, feat), bf16), sds((docs, feat), bf16), sds((quarter, feat), bf16)],
        name="label_rows",
        compiler_params=pltpu.CompilerParams(vmem_limit_bytes=4 << 20),
    )(me, in_hbm(lab_index), in_hbm(lab_class), in_hbm(features), in_hbm(anchors))

    piece = [near, swap(anchors, 1), swap(anchors, 2), None]
    piece[3] = swap(piece[2], 1)

    held, masks = own, [0]
    bits = list(range(a_bits, n_bits))
    stages = bit_groups(bits[:1]) + bit_groups(bits[1:])
    for at, stage in enumerate(stages):
        got = exchange(held, stage)
        if at < len(stages) - 1:
            masks = masks + [m ^ mask for mask in stage for m in masks]
            held = jnp.concatenate([held] + got, axis=0)
    lab_arrays = [held] + got
    slots = [[m >> a_bits for m in masks]] + [[(m ^ mask) >> a_bits for m in masks] for mask in stages[-1]]

    k_sds = sds((total, docs), bf16)
    a_sds = sds((total, feat + LANES), bf16)
    build = dict(flops=total * docs * 256, moved=2 * total * docs)
    khi, klo, aug, sums = call(
        functools.partial(build_near, na), [SMEM] + [VMEM] * 3, [k_sds, k_sds, a_sds, sds((8, docs), f32)], [], **build
    )(me, piece[0], piece[1], mine_x)
    khi, klo, aug, tinv = call(
        functools.partial(build_far, na),
        [SMEM] + [VMEM] * 7,
        [k_sds, k_sds, a_sds, sds((1, docs), f32)],
        [],
        aliases={5: 0, 6: 1, 7: 2},
        **build,
    )(me, piece[2], piece[3], mine_x, sums, khi, klo, aug)

    long = total + LANES
    flat_sds = sds((CLASSES, total), f32)
    half_sds = sds((HALF, total), f32)
    z_sds = sds((total, labeled), bf16)
    acc = pltpu.VMEM((CLASSES, total), f32)
    work = dict(flops=8 * total * docs * 64, moved=4 * total * docs)

    mine, send, rhs, zhi, zlo, spread = call(
        functools.partial(first_kernel, na, labs, slots, CLASSES * lab_scale),
        [SMEM] + [VMEM] * (len(lab_arrays) + 4),
        [sds((HALF, long), f32)] * 2 + [flat_sds, z_sds, z_sds, sds((CLASSES, docs), f32)],
        [
            pltpu.VMEM((labeled, feat + LANES), bf16),
            pltpu.VMEM((labeled, LANES), f32),
            pltpu.VMEM((CLASSES, long), f32),
        ],
        **work,
    )(me, *lab_arrays, aug, khi, klo, tinv)

    held, got = reduce_all(mine, send, n_bits)
    mine, send, dinv, lab = call(
        second_kernel,
        [SMEM] + [VMEM] * 8,
        [half_sds, half_sds, sds((1, total), f32), flat_sds],
        [pltpu.VMEM((CLASSES, long), f32), acc],
        **work,
    )(me, held, got, rhs, zhi, zlo, khi, klo, tinv)

    held, got = reduce_all(mine, send, n_bits)
    part_rows = 2 * CLASSES // na
    mine, send, direc, part, stats, *docs_out = call(
        functools.partial(third_kernel, na, lab_scale, graph_scale),
        [SMEM] + [VMEM] * 10,
        [half_sds, half_sds, flat_sds, flat_sds, sds((16, LANES), f32)] + [sds((part_rows, docs), f32)] * na,
        [acc, pltpu.VMEM((na, part_rows, docs), f32)],
        **work,
    )(me, held, got, rhs, lab, spread, zhi, zlo, khi, klo, tinv)

    held, got = reduce_all(mine, send, n_bits)
    parts = [docs_out[0]]
    for mask in range(1, na):
        parts.append(swap(docs_out[mask], mask))
    anchor_scores, doc_scores = call(
        functools.partial(last_kernel, na, graph_scale),
        [SMEM] + [VMEM] * (6 + na),
        [sds((CLASSES, quarter), f32), sds((CLASSES // na, docs_dev), f32)],
        [acc],
    )(me, held, got, direc, part, stats, dinv, *parts)
    return anchor_scores.T, doc_scores


def solution(mesh):
    in_specs = (P("docs", None), P("anch", None), P("docs"), P("docs"))
    out_specs = (P("anch", None), P("anch", "docs"))
    return jax.shard_map(run, mesh=mesh, in_specs=in_specs, out_specs=out_specs, check_vma=False)
```

```python
import functools

import jax
import jax.numpy as jnp
from jax import lax
from jax.experimental import pallas as pl
from jax.experimental.pallas import tpu as pltpu
from jax.sharding import PartitionSpec as P


CLASSES = 16

width_h = 0.25
ridge = 0.1
f32 = jnp.float32
bf16 = jnp.bfloat16
EVERY = ("docs", "anch")
LANES = 128

NT = (((1,), (1,)), ((), ()))
NN = (((1,), (0,)), ((), ()))


def mm(left, right, dims=NN, precision=None):
    return lax.dot_general(left, right, dims, precision=precision, preferred_element_type=f32)


def split2(value):
    high = value.astype(bf16)
    return high, (value - high.astype(f32)).astype(bf16)


def swap(value, mask):
    count = lax.axis_size("docs") * lax.axis_size("anch")
    return lax.ppermute(value, EVERY, [(i, i ^ mask) for i in range(count)])


def bit_groups(bits):
    groups = []
    while bits:
        part, bits = bits[:2], bits[2:]
        masks = [1 << part[0]]
        if len(part) == 2:
            masks += [1 << part[1], (1 << part[0]) | (1 << part[1])]
        groups.append(masks)
    return groups


def exchange(value, masks):
    got = []
    for mask in masks:
        got.append(swap(value, mask))
    return got


def sum_stage(held, masks):
    got = exchange(held, masks)
    if len(got) == 1:
        return held + got[0]
    return (held + got[0]) + (got[1] + got[2])


def reduce_chips(held, n_bits):
    for masks in bit_groups(list(range(1, n_bits))):
        held = sum_stage(held, masks)
    return held


def swap_core(value):
    return swap(value, 1)


def aug_columns(first, second, rows):
    lane = lax.broadcasted_iota(jnp.int32, (rows, LANES), 1)
    out = jnp.zeros((rows, LANES), f32)
    for base, column in ((0, first), (3, second)):
        if column is None:
            out = jnp.where((lane >= base) & (lane < base + 3), 1.0, out)
        else:
            rest = column
            for piece in range(3):
                part = rest.astype(bf16).astype(f32)
                out = jnp.where(lane == base + piece, part, out)
                rest = rest - part
    return out.astype(bf16)


def row_sizes(value):
    return jnp.sum(value * value, axis=1, keepdims=True)


def eighth(value):
    square = value * value
    fourth = square * square
    return 1.0 / (fourth * fourth)


def label_kernel(na, me_ref, idx_ref, cls_ref, feat_ref, anch_ref, out_ref, x_ref, a_ref, rows, picked, sems, xsem, asem):
    docs_dev = feat_ref.shape[0]
    docs = x_ref.shape[0]
    base = (me_ref[0] // na) * docs_dev
    count = idx_ref.shape[0]
    copies = []
    for k in range(count):
        start = pl.multiple_of(((idx_ref[k] - base) >> 4) << 4, 16)
        copy = pltpu.make_async_copy(feat_ref.at[pl.ds(start, 16), :], rows.at[k], sems.at[k])
        copy.start()
        copies.append(copy)
    own = pl.ds(pl.multiple_of((me_ref[0] % na) * docs, docs), docs)
    bulk = pltpu.make_async_copy(feat_ref.at[own, :], x_ref, xsem)
    bulk.start()
    points = pltpu.make_async_copy(anch_ref, a_ref, asem)
    points.start()
    sub = lax.broadcasted_iota(jnp.int32, (16, LANES), 0)
    lane = lax.broadcasted_iota(jnp.int32, (1, LANES), 1)
    for k in range(count):
        picked[count + k : count + k + 1, :] = jnp.where(lane == cls_ref[k], 1.0, 0.0)
    for k in range(count):
        copies[k].wait()
        chosen = jnp.where(sub == ((idx_ref[k] - base) & 15), rows[k].astype(f32), 0.0)
        picked[k : k + 1, :] = jnp.sum(chosen, axis=0, keepdims=True)
    out_ref[...] = picked[...].astype(bf16)
    bulk.wait()
    points.wait()


def build_rows(at_rows, value, x_ref, khi_ref, klo_ref, aug_ref, sums):
    docs, feat = x_ref.shape
    scale = 1.0 / (feat * width_h)
    tile = min(256, docs)
    lefts = []
    for at, piece in zip(at_rows, value):
        wide = piece[...].astype(f32)
        left = jnp.concatenate(
            [(wide * (-2.0 * scale)).astype(bf16), aug_columns(row_sizes(wide) * scale + 1.0, None, wide.shape[0])], axis=1
        )
        aug_ref[at, :] = left
        lefts.append(left)
    for k, col in enumerate(range(0, docs, tile)):
        raw = x_ref[col : col + tile, :]
        right = jnp.concatenate([raw, aug_columns(None, row_sizes(raw.astype(f32)) * scale, tile)], axis=1)
        for at, left in zip(at_rows, lefts):
            kern = eighth(mm(left, right, NT))
            high, low = split2(kern)
            khi_ref[at, col : col + tile] = high
            klo_ref[at, col : col + tile] = low
            part = jnp.sum(kern.reshape(-1, 8, tile), axis=0)
            sums[k] = part if sums[k] is None else sums[k] + part
    return sums


def rows_of(me_ref, na, quarter, masks):
    mine = me_ref[0] % na
    return [pl.ds(pl.multiple_of((mine ^ mask) * quarter, quarter), quarter) for mask in masks]


def build_near(na, me_ref, a0, a1, x_ref, khi_ref, klo_ref, aug_ref, sum_ref):
    tile = min(256, x_ref.shape[0])
    sums = [None] * (x_ref.shape[0] // tile)
    build_rows(rows_of(me_ref, na, a0.shape[0], (0, 1)), (a0, a1), x_ref, khi_ref, klo_ref, aug_ref, sums)
    for k, part in enumerate(sums):
        sum_ref[:, k * tile : (k + 1) * tile] = part


def build_far(na, me_ref, a2, a3, x_ref, sum_ref, kh0, kl0, aug0, khi_ref, klo_ref, aug_ref, tinv_ref):
    tile = min(256, x_ref.shape[0])
    sums = [sum_ref[:, k * tile : (k + 1) * tile] for k in range(x_ref.shape[0] // tile)]
    build_rows(rows_of(me_ref, na, a2.shape[0], (2, 3)), (a2, a3), x_ref, khi_ref, klo_ref, aug_ref, sums)
    for k, part in enumerate(sums):
        tinv_ref[:, k * tile : (k + 1) * tile] = 1.0 / jnp.sum(part, axis=0, keepdims=True)


def times(vec, khi, klo):
    both = mm(vec, khi)
    return both[0:CLASSES] + (both[CLASSES:] + mm(vec[0:CLASSES], klo))


def times_back(value, khi, klo):
    high, low = split2(value)
    both = mm(jnp.concatenate([high, low], axis=0), khi, NT)
    return both[0:CLASSES] + (both[CLASSES:] + mm(high, klo, NT))


def pieces(value):
    return jnp.concatenate(split2(value), axis=0)


def halves(me_ref, size):
    core = me_ref[0] & 1
    return [pl.ds(pl.multiple_of(part * size, size), size) for part in (core, 1 - core)]


def put_weights(w_ref, spread, tinv):
    high, low = split2(spread * tinv)
    w_ref[0:CLASSES, :] = high
    w_ref[CLASSES:, :] = low


def back_rows(w_ref, khi, klo):
    one = mm(w_ref[...], khi, NT)
    return one[0:CLASSES] + (one[CLASSES:] + mm(w_ref[0:CLASSES, :], klo, NT))


def back_degree(w_ref, khi, klo, out_ref):
    one = mm(w_ref[...], khi, NT)
    two = mm(w_ref[0 : 2 * CLASSES, :], klo, NT)
    size = one.shape[1]
    out_ref[:, 0:size] = one[0:CLASSES] + (one[2 * CLASSES :] + two[0:CLASSES])
    deg = one[CLASSES : 2 * CLASSES] + two[CLASSES:]
    deg = deg[0:1] + deg[1:2]
    out_ref[:, size:] = jnp.zeros((CLASSES, LANES), f32)
    for k in range(size // LANES):
        out_ref[k : k + 1, size:] = deg[:, k * LANES : (k + 1) * LANES]


def mean_of(value):
    return jnp.mean(value, axis=1, keepdims=True)


def total_of(value):
    return jnp.sum(jnp.sum(value, axis=1, keepdims=True), axis=0, keepdims=True)


def first_send(na, labs, slots, gain, me_ref, *refs):
    lab_refs = refs[: len(slots)]
    (aug_ref, khi_ref, klo_ref, tinv_ref, send_ref, w_ref, rhs_ref, mid_ref, zhi_ref, zlo_ref, spread_ref,
     laug, hot) = refs[len(slots) :]
    feat = laug.shape[1] - LANES
    docs = me_ref[0] // na
    for masks, ref in zip(slots, lab_refs):
        for k, mask in enumerate(masks):
            at = pl.ds(pl.multiple_of((docs ^ mask) * labs, labs), labs)
            laug[at, 0:feat] = ref[2 * labs * k : 2 * labs * k + labs, :]
            hot[at, :] = ref[2 * labs * k + labs : 2 * labs * (k + 1), :].astype(f32)
    size = row_sizes(laug[:, 0:feat].astype(f32)) * (1.0 / (feat * width_h))
    laug[:, feat:] = aug_columns(None, size, laug.shape[0])
    kern = eighth(mm(aug_ref[...], laug[...], NT))
    zhi, zlo = split2(kern / jnp.sum(kern, axis=0, keepdims=True))
    zhi_ref[...], zlo_ref[...] = zhi, zlo
    onehot = hot[...].T[0:CLASSES, :].astype(bf16)
    rhs = gain * (mm(onehot, zhi, NT) + mm(onehot, zlo, NT))
    rhs_ref[...] = rhs
    middle = rhs - mean_of(rhs)
    mid_ref[...] = middle
    tinv = tinv_ref[...]
    spread = times(pieces(middle), khi_ref[...], klo_ref[...]) * tinv
    spread_ref[...] = spread
    high, low = split2(spread * tinv)
    row = lax.broadcasted_iota(jnp.int32, (CLASSES, tinv.shape[1]), 0)
    thigh = tinv.astype(bf16).astype(f32)
    w_ref[0:CLASSES, :] = high
    w_ref[CLASSES : 2 * CLASSES, :] = jnp.where(row == 0, thigh, jnp.where(row == 1, tinv - thigh, 0.0)).astype(bf16)
    w_ref[2 * CLASSES :, :] = low
    _, other = halves(me_ref, khi_ref.shape[0] // 2)
    back_degree(w_ref, khi_ref[other, :], klo_ref[other, :], send_ref)


def first_own(me_ref, w_ref, khi_ref, klo_ref, mine_ref):
    own, _ = halves(me_ref, khi_ref.shape[0] // 2)
    back_degree(w_ref, khi_ref[own, :], klo_ref[own, :], mine_ref)


def product_own(me_ref, w_ref, khi_ref, klo_ref, mine_ref):
    own, _ = halves(me_ref, khi_ref.shape[0] // 2)
    mine_ref[...] = back_rows(w_ref, khi_ref[own, :], klo_ref[own, :])


def residual_part(sums_ref, mid_ref, at, dinv_ref):
    size = sums_ref.shape[1] - LANES
    for k in range(size // LANES):
        dinv_ref[:, k * LANES : (k + 1) * LANES] = 1.0 / sums_ref[k : k + 1, size:]
    return mid_ref[:, at] - sums_ref[:, 0:size] * dinv_ref[...]


def second_own(me_ref, held_ref, mid_ref, khi_ref, klo_ref, part_ref, dinv_ref):
    own, _ = halves(me_ref, khi_ref.shape[0] // 2)
    part_ref[...] = times(pieces(residual_part(held_ref, mid_ref, own, dinv_ref)), khi_ref[own, :], klo_ref[own, :])


def second_send(me_ref, got_ref, mid_ref, khi_ref, klo_ref, tinv_ref, part_ref, dinv_own, send_ref, w_ref, dinv_ref, dinv_other):
    own, other = halves(me_ref, khi_ref.shape[0] // 2)
    rest = times(pieces(residual_part(got_ref, mid_ref, other, dinv_other)), khi_ref[other, :], klo_ref[other, :])
    dinv_ref[:, own] = dinv_own[...]
    dinv_ref[:, other] = dinv_other[...]
    tinv = tinv_ref[...]
    put_weights(w_ref, (part_ref[...] + rest) * tinv, tinv)
    send_ref[...] = back_rows(w_ref, khi_ref[other, :], klo_ref[other, :])


def label_image(rhs_ref, zhi_ref, zlo_ref, lab_ref):
    zhi, zlo = zhi_ref[...], zlo_ref[...]
    lab_ref[...] = times_back(times(pieces(rhs_ref[...]), zhi, zlo), zhi, zlo)


def image_shift(lab_scale, lab, rhs):
    return lab_scale * mean_of(lab) + ridge * mean_of(rhs)


def third_own(lab_scale, graph_scale, me_ref, held_ref, rhs_ref, lab_ref, khi_ref, klo_ref, part_ref):
    own, _ = halves(me_ref, khi_ref.shape[0] // 2)
    shift = image_shift(lab_scale, lab_ref[...], rhs_ref[...])
    image = lab_scale * lab_ref[:, own] + graph_scale * held_ref[...] + ridge * rhs_ref[:, own]
    part_ref[...] = times(pieces(image - shift), khi_ref[own, :], klo_ref[own, :])


def third_send(lab_scale, graph_scale, me_ref, held_ref, got_ref, rhs_ref, lab_ref, part_ref, spread0_ref, khi_ref, klo_ref, tinv_ref,
               send_ref, w_ref, spread_ref, direc_ref, mid_ref, first_ref, stats_ref, whole):
    own, other = halves(me_ref, khi_ref.shape[0] // 2)
    rhs, lab = rhs_ref[...], lab_ref[...]
    whole[:, own] = held_ref[...]
    whole[:, other] = got_ref[...]
    image = lab_scale * lab + graph_scale * whole[...] + ridge * rhs
    shift = image_shift(lab_scale, lab, rhs)
    whole[...] = image - shift
    rest = times(pieces(whole[:, other]), khi_ref[other, :], klo_ref[other, :])
    norm = total_of(rhs * rhs)
    alpha = norm / total_of(rhs * image)
    resid = rhs - alpha * image
    after = total_of(resid * resid)
    beta = after / norm
    direc = resid + beta * rhs
    base = mean_of(rhs)
    level = (1.0 + beta) * base - alpha * shift
    direc_ref[...] = direc
    mid_ref[...] = direc - level
    first_ref[...] = alpha * rhs
    tinv = tinv_ref[...]
    spread = (1.0 + beta) * spread0_ref[...] - alpha * ((part_ref[...] + rest) * tinv)
    put_weights(w_ref, spread, tinv)
    send_ref[...] = back_rows(w_ref, khi_ref[other, :], klo_ref[other, :])
    spread_ref[...] = spread
    stats_ref[0:CLASSES, :] = jnp.broadcast_to(level, (CLASSES, LANES))
    stats_ref[CLASSES : 2 * CLASSES, :] = jnp.broadcast_to(alpha * base, (CLASSES, LANES))
    stats_ref[2 * CLASSES : 2 * CLASSES + 8, :] = jnp.broadcast_to(alpha, (8, LANES))
    stats_ref[2 * CLASSES + 8 :, :] = jnp.broadcast_to(after, (8, LANES))


def doc_parts(na, lab_scale, me_ref, spread0_ref, spread_ref, stats_ref, direc_ref, zhi_ref, zlo_ref, *refs):
    outs, (base_ref, slots) = refs[0:na], refs[na:]
    quarter = CLASSES // na
    part = stats_ref[2 * CLASSES : 2 * CLASSES + 1, 0:1] * spread0_ref[...] + stats_ref[CLASSES : 2 * CLASSES, 0:1]
    full = spread_ref[...] + stats_ref[0:CLASSES, 0:1]
    for k in range(na):
        slots[k, 0:quarter, :] = part[k * quarter : (k + 1) * quarter]
        slots[k, quarter : 2 * quarter, :] = full[k * quarter : (k + 1) * quarter]
    for mask in range(na):
        outs[mask][...] = slots[(me_ref[0] % na) ^ mask]
    direc = direc_ref[...]
    seen = times(pieces(direc), zhi_ref[...], zlo_ref[...])
    base_ref[...] = jnp.broadcast_to(lab_scale * total_of(seen * seen) + ridge * total_of(direc * direc), base_ref.shape)


def last_kernel(na, graph_scale, me_ref, held_ref, got_ref, direc_ref, mid_ref, first_ref, stats_ref, base_ref, dinv_ref, *refs):
    parts, (anchor_ref, doc_ref, whole) = refs[0:na], refs[na:]
    mine = me_ref[0] % na
    own, other = halves(me_ref, whole.shape[1] // 2)
    whole[:, own] = held_ref[...]
    whole[:, other] = got_ref[...]
    prod = whole[...]
    quad = total_of(prod * (mid_ref[...] - prod * dinv_ref[...]))
    alpha = stats_ref[2 * CLASSES + 8 : 2 * CLASSES + 9, 0:1] / (base_ref[0:1, 0:1] + graph_scale * quad)
    whole[...] = first_ref[...] + alpha * direc_ref[...]
    rows = anchor_ref.shape[1]
    anchor_ref[...] = whole[:, pl.ds(pl.multiple_of(mine * rows, rows), rows)]
    quarter, docs = doc_ref.shape[0], parts[0].shape[1]
    for mask in range(na):
        at = pl.ds(pl.multiple_of((mine ^ mask) * docs, docs), docs)
        doc_ref[:, at] = parts[mask][0:quarter, :] + alpha * parts[mask][quarter:, :]


VMEM = pl.BlockSpec(memory_space=pltpu.MemorySpace.VMEM)
SMEM = pl.BlockSpec(memory_space=pltpu.MemorySpace.SMEM)


def in_hbm(value):
    return pltpu.with_memory_space_constraint(value, pltpu.MemorySpace.HBM)


def call(kernel, in_specs, out_shape, scratch, flops=1 << 20, moved=1 << 18, aliases={}):
    return pl.pallas_call(
        kernel,
        in_specs=in_specs,
        out_specs=[VMEM] * len(out_shape),
        out_shape=out_shape,
        scratch_shapes=scratch,
        input_output_aliases=aliases,
        compiler_params=pltpu.CompilerParams(vmem_limit_bytes=24 << 20),
        cost_estimate=pl.CostEstimate(flops=flops, bytes_accessed=moved, transcendentals=0),
    )


def run(features, anchors, lab_index, lab_class):
    docs_dev, feat = features.shape
    nd, na = lax.axis_size("docs"), lax.axis_size("anch")
    n_bits = (nd * na).bit_length() - 1
    a_bits = na.bit_length() - 1
    labs = lab_index.shape[0]
    labeled = labs * nd
    quarter = anchors.shape[0]
    total = quarter * na
    docs = docs_dev // na
    lab_scale = total / labeled
    graph_scale = total * total / (docs_dev * nd)
    assert na == 4 and nd * na == 1 << n_bits and total // LANES <= CLASSES and feat == LANES
    sds = jax.ShapeDtypeStruct

    me = lax.axis_index(EVERY).astype(jnp.int32).reshape(1)

    own, mine_x, near = pl.pallas_call(
        functools.partial(label_kernel, na),
        grid_spec=pltpu.PrefetchScalarGridSpec(
            num_scalar_prefetch=3,
            grid=(1,),
            in_specs=[pl.BlockSpec(memory_space=pltpu.MemorySpace.HBM)] * 2,
            out_specs=[VMEM] * 3,
            scratch_shapes=[
                pltpu.VMEM((labs, 16, LANES), bf16),
                pltpu.VMEM((2 * labs, LANES), f32),
                pltpu.SemaphoreType.DMA((labs,)),
                pltpu.SemaphoreType.DMA,
                pltpu.SemaphoreType.DMA,
            ],
        ),
        out_shape=[sds((2 * labs, feat), bf16), sds((docs, feat), bf16), sds((quarter, feat), bf16)],
        name="label_rows",
        compiler_params=pltpu.CompilerParams(vmem_limit_bytes=4 << 20),
    )(me, in_hbm(lab_index), in_hbm(lab_class), in_hbm(features), in_hbm(anchors))

    piece = [near, swap(anchors, 1), swap(anchors, 2), None]
    piece[3] = swap(piece[2], 1)

    held, masks = own, [0]
    bits = list(range(a_bits, n_bits))
    stages = bit_groups(bits[:1]) + bit_groups(bits[1:])
    for at, stage in enumerate(stages):
        got = exchange(held, stage)
        if at < len(stages) - 1:
            masks = masks + [m ^ mask for mask in stage for m in masks]
            held = jnp.concatenate([held] + got, axis=0)
    lab_arrays = [held] + got
    slots = [[m >> a_bits for m in masks]] + [[(m ^ mask) >> a_bits for m in masks] for mask in stages[-1]]

    k_sds = sds((total, docs), bf16)
    a_sds = sds((total, feat + LANES), bf16)
    build = dict(flops=total * docs * 256, moved=2 * total * docs)
    khi, klo, aug, sums = call(
        functools.partial(build_near, na), [SMEM] + [VMEM] * 3, [k_sds, k_sds, a_sds, sds((8, docs), f32)], [], **build
    )(me, piece[0], piece[1], mine_x)
    khi, klo, aug, tinv = call(
        functools.partial(build_far, na),
        [SMEM] + [VMEM] * 7,
        [k_sds, k_sds, a_sds, sds((1, docs), f32)],
        [],
        aliases={5: 0, 6: 1, 7: 2},
        **build,
    )(me, piece[2], piece[3], mine_x, sums, khi, klo, aug)

    half = total // 2
    flat_sds = sds((CLASSES, total), f32)
    half_sds = sds((CLASSES, half), f32)
    long_sds = sds((CLASSES, half + LANES), f32)
    docs_sds = sds((CLASSES, docs), f32)
    z_sds = sds((total, labeled), bf16)
    w_sds = sds((2 * CLASSES, docs), bf16)
    work = dict(flops=4 * total * docs * 64, moved=2 * total * docs)

    send, w, rhs, middle, zhi, zlo, spread0 = call(
        functools.partial(first_send, na, labs, slots, CLASSES * lab_scale),
        [SMEM] + [VMEM] * (len(lab_arrays) + 4),
        [long_sds, sds((3 * CLASSES, docs), bf16), flat_sds, flat_sds, z_sds, z_sds, docs_sds],
        [pltpu.VMEM((labeled, feat + LANES), bf16), pltpu.VMEM((labeled, LANES), f32)],
        **work,
    )(me, *lab_arrays, aug, khi, klo, tinv)
    got = swap_core(send)
    mine = call(first_own, [SMEM] + [VMEM] * 3, [long_sds], [], **work)(me, w, khi, klo)[0]
    held = reduce_chips(mine + got, n_bits)
    lab = call(label_image, [VMEM] * 3, [flat_sds], [])(rhs, zhi, zlo)[0]

    got = swap_core(held)
    part, dinv_own = call(
        second_own, [SMEM] + [VMEM] * 4, [docs_sds, sds((1, half), f32)], [], **work
    )(me, held, middle, khi, klo)
    send, w, dinv = call(
        second_send, [SMEM] + [VMEM] * 7, [half_sds, w_sds, sds((1, total), f32)], [pltpu.VMEM((1, half), f32)], **work
    )(me, got, middle, khi, klo, tinv, part, dinv_own)
    got = swap_core(send)
    mine = call(product_own, [SMEM] + [VMEM] * 3, [half_sds], [], **work)(me, w, khi, klo)[0]
    held = reduce_chips(mine + got, n_bits)

    got = swap_core(held)
    part = call(
        functools.partial(third_own, lab_scale, graph_scale), [SMEM] + [VMEM] * 5, [docs_sds], [], **work
    )(me, held, rhs, lab, khi, klo)[0]
    send, w, spread, direc, middle, first, stats = call(
        functools.partial(third_send, lab_scale, graph_scale),
        [SMEM] + [VMEM] * 9,
        [half_sds, w_sds, docs_sds, flat_sds, flat_sds, flat_sds, sds((2 * CLASSES + 16, LANES), f32)],
        [pltpu.VMEM((CLASSES, total), f32)],
        **work,
    )(me, held, got, rhs, lab, part, spread0, khi, klo, tinv)
    got = swap_core(send)
    mine = call(product_own, [SMEM] + [VMEM] * 3, [half_sds], [], **work)(me, w, khi, klo)[0]
    part_rows = 2 * CLASSES // na
    *docs_out, base = call(
        functools.partial(doc_parts, na, lab_scale),
        [SMEM] + [VMEM] * 6,
        [sds((part_rows, docs), f32)] * na + [sds((8, LANES), f32)],
        [pltpu.VMEM((na, part_rows, docs), f32)],
    )(me, spread0, spread, stats, direc, zhi, zlo)
    held = reduce_chips(mine + got, n_bits)
    got = swap_core(held)

    parts = [docs_out[0]]
    for mask in range(1, na):
        parts.append(swap(docs_out[mask], mask))
    anchor_scores, doc_scores = call(
        functools.partial(last_kernel, na, graph_scale),
        [SMEM] + [VMEM] * (8 + na),
        [sds((CLASSES, quarter), f32), sds((CLASSES // na, docs_dev), f32)],
        [pltpu.VMEM((CLASSES, total), f32)],
    )(me, held, got, direc, middle, first, stats, base, dinv, *parts)
    return anchor_scores.T, doc_scores


def solution(mesh):
    in_specs = (P("docs", None), P("anch", None), P("docs"), P("docs"))
    out_specs = (P("anch", None), P("anch", "docs"))
    return jax.shard_map(run, mesh=mesh, in_specs=in_specs, out_specs=out_specs, check_vma=False)
```

```python
import functools

import jax
import jax.numpy as jnp
from jax import lax
from jax.experimental import pallas as pl
from jax.experimental.pallas import tpu as pltpu
from jax.sharding import PartitionSpec as P


CLASSES = 16

width_h = 0.25
ridge = 0.1
f32 = jnp.float32
bf16 = jnp.bfloat16
EVERY = ("docs", "anch")
LANES = 128

NT = (((1,), (1,)), ((), ()))
NN = (((1,), (0,)), ((), ()))


def mm(left, right, dims=NN, precision=None):
    return lax.dot_general(left, right, dims, precision=precision, preferred_element_type=f32)


def split2(value):
    high = value.astype(bf16)
    return high, (value - high.astype(f32)).astype(bf16)


def swap(value, mask):
    count = lax.axis_size("docs") * lax.axis_size("anch")
    return lax.ppermute(value, EVERY, [(i, i ^ mask) for i in range(count)])


def bit_groups(bits):
    groups = []
    while bits:
        part, bits = bits[:2], bits[2:]
        masks = [1 << part[0]]
        if len(part) == 2:
            masks += [1 << part[1], (1 << part[0]) | (1 << part[1])]
        groups.append(masks)
    return groups


def exchange(value, masks):
    got = []
    for mask in masks:
        got.append(swap(value, mask))
    return got


def sum_stage(held, masks):
    got = exchange(held, masks)
    if len(got) == 1:
        return held + got[0]
    return (held + got[0]) + (got[1] + got[2])


def reduce_chips(held, n_bits):
    for masks in bit_groups(list(range(1, n_bits))):
        held = sum_stage(held, masks)
    return held


def swap_core(value):
    return swap(value, 1)


def aug_columns(first, second, rows):
    lane = lax.broadcasted_iota(jnp.int32, (rows, LANES), 1)
    out = jnp.zeros((rows, LANES), f32)
    for base, column in ((0, first), (3, second)):
        if column is None:
            out = jnp.where((lane >= base) & (lane < base + 3), 1.0, out)
        else:
            rest = column
            for piece in range(3):
                part = rest.astype(bf16).astype(f32)
                out = jnp.where(lane == base + piece, part, out)
                rest = rest - part
    return out.astype(bf16)


def row_sizes(value):
    return jnp.sum(value * value, axis=1, keepdims=True)


def eighth(value):
    square = value * value
    fourth = square * square
    return 1.0 / (fourth * fourth)


def label_kernel(na, me_ref, idx_ref, cls_ref, feat_ref, anch_ref, out_ref, x_ref, a_ref, rows, picked, sems, xsem, asem):
    docs_dev = feat_ref.shape[0]
    docs = x_ref.shape[0]
    base = (me_ref[0] // na) * docs_dev
    count = idx_ref.shape[0]
    copies = []
    for k in range(count):
        start = pl.multiple_of(((idx_ref[k] - base) >> 4) << 4, 16)
        copy = pltpu.make_async_copy(feat_ref.at[pl.ds(start, 16), :], rows.at[k], sems.at[k])
        copy.start()
        copies.append(copy)
    own = pl.ds(pl.multiple_of((me_ref[0] % na) * docs, docs), docs)
    bulk = pltpu.make_async_copy(feat_ref.at[own, :], x_ref, xsem)
    bulk.start()
    points = pltpu.make_async_copy(anch_ref, a_ref, asem)
    points.start()
    sub = lax.broadcasted_iota(jnp.int32, (16, LANES), 0)
    lane = lax.broadcasted_iota(jnp.int32, (1, LANES), 1)
    for k in range(count):
        picked[count + k : count + k + 1, :] = jnp.where(lane == cls_ref[k], 1.0, 0.0)
    for k in range(count):
        copies[k].wait()
        chosen = jnp.where(sub == ((idx_ref[k] - base) & 15), rows[k].astype(f32), 0.0)
        picked[k : k + 1, :] = jnp.sum(chosen, axis=0, keepdims=True)
    out_ref[...] = picked[...].astype(bf16)
    bulk.wait()
    points.wait()


def build_kernel(na, me_ref, a0, a1, a2, a3, x_ref, khi_ref, klo_ref, tinv_ref, aug_ref):
    docs, feat = x_ref.shape
    quarter = a0.shape[0]
    scale = 1.0 / (feat * width_h)
    me = me_ref[0] % na
    for mask, piece in enumerate((a0, a1, a2, a3)):
        at = pl.ds(pl.multiple_of((me ^ mask) * quarter, quarter), quarter)
        value = piece[...].astype(f32)
        aug_ref[at, 0:feat] = (value * (-2.0 * scale)).astype(bf16)
        aug_ref[at, feat:] = aug_columns(row_sizes(value) * scale + 1.0, None, quarter)
    tile = min(256, docs)
    for col in range(0, docs, tile):
        raw = x_ref[col : col + tile, :]
        right = jnp.concatenate([raw, aug_columns(None, row_sizes(raw.astype(f32)) * scale, tile)], axis=1)
        total = jnp.zeros((8, tile), f32)
        for at in range(0, aug_ref.shape[0], 256):
            kern = eighth(mm(aug_ref[at : at + 256, :], right, NT))
            high, low = split2(kern)
            khi_ref[at : at + 256, col : col + tile] = high
            klo_ref[at : at + 256, col : col + tile] = low
            total = total + jnp.sum(kern.reshape(32, 8, tile), axis=0)
        tinv_ref[:, col : col + tile] = 1.0 / jnp.sum(total, axis=0, keepdims=True)


def times(vec, khi, klo):
    both = mm(vec, khi)
    return both[0:CLASSES] + (both[CLASSES:] + mm(vec[0:CLASSES], klo))


def times_back(value, khi, klo):
    high, low = split2(value)
    both = mm(jnp.concatenate([high, low], axis=0), khi, NT)
    return both[0:CLASSES] + (both[CLASSES:] + mm(high, klo, NT))


def pieces(value):
    return jnp.concatenate(split2(value), axis=0)


def halves(me_ref, size):
    core = me_ref[0] & 1
    return [pl.ds(pl.multiple_of(part * size, size), size) for part in (core, 1 - core)]


def put_weights(w_ref, spread, tinv):
    high, low = split2(spread * tinv)
    w_ref[0:CLASSES, :] = high
    w_ref[CLASSES:, :] = low


def back_rows(w_ref, khi, klo):
    one = mm(w_ref[...], khi, NT)
    return one[0:CLASSES] + (one[CLASSES:] + mm(w_ref[0:CLASSES, :], klo, NT))


def back_degree(w_ref, khi, klo, out_ref):
    one = mm(w_ref[...], khi, NT)
    two = mm(w_ref[0 : 2 * CLASSES, :], klo, NT)
    size = one.shape[1]
    out_ref[:, 0:size] = one[0:CLASSES] + (one[2 * CLASSES :] + two[0:CLASSES])
    deg = one[CLASSES : 2 * CLASSES] + two[CLASSES:]
    deg = deg[0:1] + deg[1:2]
    out_ref[:, size:] = jnp.zeros((CLASSES, LANES), f32)
    for k in range(size // LANES):
        out_ref[k : k + 1, size:] = deg[:, k * LANES : (k + 1) * LANES]


def mean_of(value):
    return jnp.mean(value, axis=1, keepdims=True)


def total_of(value):
    return jnp.sum(jnp.sum(value, axis=1, keepdims=True), axis=0, keepdims=True)


def first_send(na, labs, slots, gain, me_ref, *refs):
    lab_refs = refs[: len(slots)]
    (aug_ref, khi_ref, klo_ref, tinv_ref, send_ref, w_ref, rhs_ref, mid_ref, zhi_ref, zlo_ref, spread_ref,
     laug, hot) = refs[len(slots) :]
    feat = laug.shape[1] - LANES
    docs = me_ref[0] // na
    for masks, ref in zip(slots, lab_refs):
        for k, mask in enumerate(masks):
            at = pl.ds(pl.multiple_of((docs ^ mask) * labs, labs), labs)
            laug[at, 0:feat] = ref[2 * labs * k : 2 * labs * k + labs, :]
            hot[at, :] = ref[2 * labs * k + labs : 2 * labs * (k + 1), :].astype(f32)
    size = row_sizes(laug[:, 0:feat].astype(f32)) * (1.0 / (feat * width_h))
    laug[:, feat:] = aug_columns(None, size, laug.shape[0])
    kern = eighth(mm(aug_ref[...], laug[...], NT))
    zhi, zlo = split2(kern / jnp.sum(kern, axis=0, keepdims=True))
    zhi_ref[...], zlo_ref[...] = zhi, zlo
    onehot = hot[...].T[0:CLASSES, :].astype(bf16)
    rhs = gain * (mm(onehot, zhi, NT) + mm(onehot, zlo, NT))
    rhs_ref[...] = rhs
    middle = rhs - mean_of(rhs)
    mid_ref[...] = middle
    tinv = tinv_ref[...]
    spread = times(pieces(middle), khi_ref[...], klo_ref[...]) * tinv
    spread_ref[...] = spread
    high, low = split2(spread * tinv)
    row = lax.broadcasted_iota(jnp.int32, (CLASSES, tinv.shape[1]), 0)
    thigh = tinv.astype(bf16).astype(f32)
    w_ref[0:CLASSES, :] = high
    w_ref[CLASSES : 2 * CLASSES, :] = jnp.where(row == 0, thigh, jnp.where(row == 1, tinv - thigh, 0.0)).astype(bf16)
    w_ref[2 * CLASSES :, :] = low
    _, other = halves(me_ref, khi_ref.shape[0] // 2)
    back_degree(w_ref, khi_ref[other, :], klo_ref[other, :], send_ref)


def first_own(me_ref, w_ref, khi_ref, klo_ref, mine_ref):
    own, _ = halves(me_ref, khi_ref.shape[0] // 2)
    back_degree(w_ref, khi_ref[own, :], klo_ref[own, :], mine_ref)


def product_own(me_ref, w_ref, khi_ref, klo_ref, mine_ref):
    own, _ = halves(me_ref, khi_ref.shape[0] // 2)
    mine_ref[...] = back_rows(w_ref, khi_ref[own, :], klo_ref[own, :])


def residual_part(sums_ref, mid_ref, at, dinv_ref):
    size = sums_ref.shape[1] - LANES
    for k in range(size // LANES):
        dinv_ref[:, k * LANES : (k + 1) * LANES] = 1.0 / sums_ref[k : k + 1, size:]
    return mid_ref[:, at] - sums_ref[:, 0:size] * dinv_ref[...]


def second_own(me_ref, held_ref, mid_ref, khi_ref, klo_ref, part_ref, dinv_ref):
    own, _ = halves(me_ref, khi_ref.shape[0] // 2)
    part_ref[...] = times(pieces(residual_part(held_ref, mid_ref, own, dinv_ref)), khi_ref[own, :], klo_ref[own, :])


def second_send(me_ref, got_ref, mid_ref, khi_ref, klo_ref, tinv_ref, part_ref, dinv_own, send_ref, w_ref, dinv_ref, dinv_other):
    own, other = halves(me_ref, khi_ref.shape[0] // 2)
    rest = times(pieces(residual_part(got_ref, mid_ref, other, dinv_other)), khi_ref[other, :], klo_ref[other, :])
    dinv_ref[:, own] = dinv_own[...]
    dinv_ref[:, other] = dinv_other[...]
    tinv = tinv_ref[...]
    put_weights(w_ref, (part_ref[...] + rest) * tinv, tinv)
    send_ref[...] = back_rows(w_ref, khi_ref[other, :], klo_ref[other, :])


def label_image(rhs_ref, zhi_ref, zlo_ref, lab_ref):
    zhi, zlo = zhi_ref[...], zlo_ref[...]
    lab_ref[...] = times_back(times(pieces(rhs_ref[...]), zhi, zlo), zhi, zlo)


def image_shift(lab_scale, lab, rhs):
    return lab_scale * mean_of(lab) + ridge * mean_of(rhs)


def third_own(lab_scale, graph_scale, me_ref, held_ref, rhs_ref, lab_ref, khi_ref, klo_ref, part_ref):
    own, _ = halves(me_ref, khi_ref.shape[0] // 2)
    shift = image_shift(lab_scale, lab_ref[...], rhs_ref[...])
    image = lab_scale * lab_ref[:, own] + graph_scale * held_ref[...] + ridge * rhs_ref[:, own]
    part_ref[...] = times(pieces(image - shift), khi_ref[own, :], klo_ref[own, :])


def third_send(lab_scale, graph_scale, me_ref, held_ref, got_ref, rhs_ref, lab_ref, part_ref, spread0_ref, khi_ref, klo_ref, tinv_ref,
               send_ref, w_ref, spread_ref, direc_ref, mid_ref, first_ref, stats_ref, whole):
    own, other = halves(me_ref, khi_ref.shape[0] // 2)
    rhs, lab = rhs_ref[...], lab_ref[...]
    whole[:, own] = held_ref[...]
    whole[:, other] = got_ref[...]
    image = lab_scale * lab + graph_scale * whole[...] + ridge * rhs
    shift = image_shift(lab_scale, lab, rhs)
    whole[...] = image - shift
    rest = times(pieces(whole[:, other]), khi_ref[other, :], klo_ref[other, :])
    norm = total_of(rhs * rhs)
    alpha = norm / total_of(rhs * image)
    resid = rhs - alpha * image
    after = total_of(resid * resid)
    beta = after / norm
    direc = resid + beta * rhs
    base = mean_of(rhs)
    level = (1.0 + beta) * base - alpha * shift
    direc_ref[...] = direc
    mid_ref[...] = direc - level
    first_ref[...] = alpha * rhs
    tinv = tinv_ref[...]
    spread = (1.0 + beta) * spread0_ref[...] - alpha * ((part_ref[...] + rest) * tinv)
    put_weights(w_ref, spread, tinv)
    send_ref[...] = back_rows(w_ref, khi_ref[other, :], klo_ref[other, :])
    spread_ref[...] = spread
    stats_ref[0:CLASSES, :] = jnp.broadcast_to(level, (CLASSES, LANES))
    stats_ref[CLASSES : 2 * CLASSES, :] = jnp.broadcast_to(alpha * base, (CLASSES, LANES))
    stats_ref[2 * CLASSES : 2 * CLASSES + 8, :] = jnp.broadcast_to(alpha, (8, LANES))
    stats_ref[2 * CLASSES + 8 :, :] = jnp.broadcast_to(after, (8, LANES))


def doc_parts(na, lab_scale, me_ref, spread0_ref, spread_ref, stats_ref, direc_ref, zhi_ref, zlo_ref, *refs):
    outs, (base_ref, slots) = refs[0:na], refs[na:]
    quarter = CLASSES // na
    part = stats_ref[2 * CLASSES : 2 * CLASSES + 1, 0:1] * spread0_ref[...] + stats_ref[CLASSES : 2 * CLASSES, 0:1]
    full = spread_ref[...] + stats_ref[0:CLASSES, 0:1]
    for k in range(na):
        slots[k, 0:quarter, :] = part[k * quarter : (k + 1) * quarter]
        slots[k, quarter : 2 * quarter, :] = full[k * quarter : (k + 1) * quarter]
    for mask in range(na):
        outs[mask][...] = slots[(me_ref[0] % na) ^ mask]
    direc = direc_ref[...]
    seen = times(pieces(direc), zhi_ref[...], zlo_ref[...])
    base_ref[...] = jnp.broadcast_to(lab_scale * total_of(seen * seen) + ridge * total_of(direc * direc), base_ref.shape)


def last_kernel(na, graph_scale, me_ref, held_ref, got_ref, direc_ref, mid_ref, first_ref, stats_ref, base_ref, dinv_ref, *refs):
    parts, (anchor_ref, doc_ref, whole) = refs[0:na], refs[na:]
    mine = me_ref[0] % na
    own, other = halves(me_ref, whole.shape[1] // 2)
    whole[:, own] = held_ref[...]
    whole[:, other] = got_ref[...]
    prod = whole[...]
    quad = total_of(prod * (mid_ref[...] - prod * dinv_ref[...]))
    alpha = stats_ref[2 * CLASSES + 8 : 2 * CLASSES + 9, 0:1] / (base_ref[0:1, 0:1] + graph_scale * quad)
    whole[...] = first_ref[...] + alpha * direc_ref[...]
    rows = anchor_ref.shape[1]
    anchor_ref[...] = whole[:, pl.ds(pl.multiple_of(mine * rows, rows), rows)]
    quarter, docs = doc_ref.shape[0], parts[0].shape[1]
    for mask in range(na):
        at = pl.ds(pl.multiple_of((mine ^ mask) * docs, docs), docs)
        doc_ref[:, at] = parts[mask][0:quarter, :] + alpha * parts[mask][quarter:, :]


VMEM = pl.BlockSpec(memory_space=pltpu.MemorySpace.VMEM)
SMEM = pl.BlockSpec(memory_space=pltpu.MemorySpace.SMEM)


def in_hbm(value):
    return pltpu.with_memory_space_constraint(value, pltpu.MemorySpace.HBM)


def call(kernel, in_specs, out_shape, scratch, flops=1 << 20, moved=1 << 18):
    return pl.pallas_call(
        kernel,
        in_specs=in_specs,
        out_specs=[VMEM] * len(out_shape),
        out_shape=out_shape,
        scratch_shapes=scratch,
        compiler_params=pltpu.CompilerParams(vmem_limit_bytes=24 << 20),
        cost_estimate=pl.CostEstimate(flops=flops, bytes_accessed=moved, transcendentals=0),
    )


def run(features, anchors, lab_index, lab_class):
    docs_dev, feat = features.shape
    nd, na = lax.axis_size("docs"), lax.axis_size("anch")
    n_bits = (nd * na).bit_length() - 1
    a_bits = na.bit_length() - 1
    labs = lab_index.shape[0]
    labeled = labs * nd
    quarter = anchors.shape[0]
    total = quarter * na
    docs = docs_dev // na
    lab_scale = total / labeled
    graph_scale = total * total / (docs_dev * nd)
    assert na == 4 and nd * na == 1 << n_bits and total // LANES <= CLASSES and feat == LANES
    sds = jax.ShapeDtypeStruct

    me = lax.axis_index(EVERY).astype(jnp.int32).reshape(1)

    own, mine_x, near = pl.pallas_call(
        functools.partial(label_kernel, na),
        grid_spec=pltpu.PrefetchScalarGridSpec(
            num_scalar_prefetch=3,
            grid=(1,),
            in_specs=[pl.BlockSpec(memory_space=pltpu.MemorySpace.HBM)] * 2,
            out_specs=[VMEM] * 3,
            scratch_shapes=[
                pltpu.VMEM((labs, 16, LANES), bf16),
                pltpu.VMEM((2 * labs, LANES), f32),
                pltpu.SemaphoreType.DMA((labs,)),
                pltpu.SemaphoreType.DMA,
                pltpu.SemaphoreType.DMA,
            ],
        ),
        out_shape=[sds((2 * labs, feat), bf16), sds((docs, feat), bf16), sds((quarter, feat), bf16)],
        name="label_rows",
        compiler_params=pltpu.CompilerParams(vmem_limit_bytes=4 << 20),
    )(me, in_hbm(lab_index), in_hbm(lab_class), in_hbm(features), in_hbm(anchors))

    piece = [near, swap_core(anchors), None, None]
    piece[2] = swap(anchors, 2)
    piece[3] = swap_core(piece[2])

    held, masks = own, [0]
    bits = list(range(a_bits, n_bits))
    stages = bit_groups(bits[:1]) + bit_groups(bits[1:])
    for at, stage in enumerate(stages):
        got = exchange(held, stage)
        if at < len(stages) - 1:
            masks = masks + [m ^ mask for mask in stage for m in masks]
            held = jnp.concatenate([held] + got, axis=0)
    lab_arrays = [held] + got
    slots = [[m >> a_bits for m in masks]] + [[(m ^ mask) >> a_bits for m in masks] for mask in stages[-1]]

    k_sds = sds((total, docs), bf16)
    khi, klo, tinv, aug = call(
        functools.partial(build_kernel, na),
        [SMEM] + [VMEM] * 5,
        [k_sds, k_sds, sds((1, docs), f32), sds((total, feat + LANES), bf16)],
        [],
        flops=2 * total * docs * 256,
        moved=4 * total * docs,
    )(me, *piece, mine_x)

    half = total // 2
    flat_sds = sds((CLASSES, total), f32)
    half_sds = sds((CLASSES, half), f32)
    long_sds = sds((CLASSES, half + LANES), f32)
    docs_sds = sds((CLASSES, docs), f32)
    z_sds = sds((total, labeled), bf16)
    w_sds = sds((2 * CLASSES, docs), bf16)
    work = dict(flops=4 * total * docs * 64, moved=2 * total * docs)

    send, w, rhs, middle, zhi, zlo, spread0 = call(
        functools.partial(first_send, na, labs, slots, CLASSES * lab_scale),
        [SMEM] + [VMEM] * (len(lab_arrays) + 4),
        [long_sds, sds((3 * CLASSES, docs), bf16), flat_sds, flat_sds, z_sds, z_sds, docs_sds],
        [pltpu.VMEM((labeled, feat + LANES), bf16), pltpu.VMEM((labeled, LANES), f32)],
        **work,
    )(me, *lab_arrays, aug, khi, klo, tinv)
    got = swap_core(send)
    mine = call(first_own, [SMEM] + [VMEM] * 3, [long_sds], [], **work)(me, w, khi, klo)[0]
    held = reduce_chips(mine + got, n_bits)
    lab = call(label_image, [VMEM] * 3, [flat_sds], [])(rhs, zhi, zlo)[0]

    got = swap_core(held)
    part, dinv_own = call(
        second_own, [SMEM] + [VMEM] * 4, [docs_sds, sds((1, half), f32)], [], **work
    )(me, held, middle, khi, klo)
    send, w, dinv = call(
        second_send, [SMEM] + [VMEM] * 7, [half_sds, w_sds, sds((1, total), f32)], [pltpu.VMEM((1, half), f32)], **work
    )(me, got, middle, khi, klo, tinv, part, dinv_own)
    got = swap_core(send)
    mine = call(product_own, [SMEM] + [VMEM] * 3, [half_sds], [], **work)(me, w, khi, klo)[0]
    held = reduce_chips(mine + got, n_bits)

    got = swap_core(held)
    part = call(
        functools.partial(third_own, lab_scale, graph_scale), [SMEM] + [VMEM] * 5, [docs_sds], [], **work
    )(me, held, rhs, lab, khi, klo)[0]
    send, w, spread, direc, middle, first, stats = call(
        functools.partial(third_send, lab_scale, graph_scale),
        [SMEM] + [VMEM] * 9,
        [half_sds, w_sds, docs_sds, flat_sds, flat_sds, flat_sds, sds((2 * CLASSES + 16, LANES), f32)],
        [pltpu.VMEM((CLASSES, total), f32)],
        **work,
    )(me, held, got, rhs, lab, part, spread0, khi, klo, tinv)
    got = swap_core(send)
    mine = call(product_own, [SMEM] + [VMEM] * 3, [half_sds], [], **work)(me, w, khi, klo)[0]
    part_rows = 2 * CLASSES // na
    *docs_out, base = call(
        functools.partial(doc_parts, na, lab_scale),
        [SMEM] + [VMEM] * 6,
        [sds((part_rows, docs), f32)] * na + [sds((8, LANES), f32)],
        [pltpu.VMEM((na, part_rows, docs), f32)],
    )(me, spread0, spread, stats, direc, zhi, zlo)
    held = reduce_chips(mine + got, n_bits)
    got = swap_core(held)

    parts = [docs_out[0]]
    for mask in range(1, na):
        parts.append(swap(docs_out[mask], mask))
    anchor_scores, doc_scores = call(
        functools.partial(last_kernel, na, graph_scale),
        [SMEM] + [VMEM] * (8 + na),
        [sds((CLASSES, quarter), f32), sds((CLASSES // na, docs_dev), f32)],
        [pltpu.VMEM((CLASSES, total), f32)],
    )(me, held, got, direc, middle, first, stats, base, dinv, *parts)
    return anchor_scores.T, doc_scores


def solution(mesh):
    in_specs = (P("docs", None), P("anch", None), P("docs"), P("docs"))
    out_specs = (P("anch", None), P("anch", "docs"))
    return jax.shard_map(run, mesh=mesh, in_specs=in_specs, out_specs=out_specs, check_vma=False)
```

```python
import functools

import jax
import jax.numpy as jnp
from jax import lax
from jax.experimental import pallas as pl
from jax.experimental.pallas import tpu as pltpu
from jax.sharding import PartitionSpec as P


CLASSES = 16

width_h = 0.25
ridge = 0.1
f32 = jnp.float32
bf16 = jnp.bfloat16
EVERY = ("docs", "anch")
LANES = 128

NT = (((1,), (1,)), ((), ()))
NN = (((1,), (0,)), ((), ()))


def mm(left, right, dims=NN, precision=None):
    return lax.dot_general(left, right, dims, precision=precision, preferred_element_type=f32)


def split2(value):
    high = value.astype(bf16)
    return high, (value - high.astype(f32)).astype(bf16)


def swap(value, mask):
    count = lax.axis_size("docs") * lax.axis_size("anch")
    return lax.ppermute(value, EVERY, [(i, i ^ mask) for i in range(count)])


def bit_groups(bits):
    groups = []
    while bits:
        part, bits = bits[:2], bits[2:]
        masks = [1 << part[0]]
        if len(part) == 2:
            masks += [1 << part[1], (1 << part[0]) | (1 << part[1])]
        groups.append(masks)
    return groups


def exchange(value, masks):
    got = []
    for mask in masks:
        got.append(swap(value, mask))
    return got


def sum_stage(held, masks):
    got = exchange(held, masks)
    if len(got) == 1:
        return held + got[0]
    return (held + got[0]) + (got[1] + got[2])


def reduce_chips(held, n_bits):
    for masks in bit_groups(list(range(1, n_bits))):
        held = sum_stage(held, masks)
    return held


def swap_core(value):
    return swap(value, 1)


def aug_columns(first, second, rows):
    lane = lax.broadcasted_iota(jnp.int32, (rows, LANES), 1)
    out = jnp.zeros((rows, LANES), f32)
    for base, column in ((0, first), (3, second)):
        if column is None:
            out = jnp.where((lane >= base) & (lane < base + 3), 1.0, out)
        else:
            rest = column
            for piece in range(3):
                part = rest.astype(bf16).astype(f32)
                out = jnp.where(lane == base + piece, part, out)
                rest = rest - part
    return out.astype(bf16)


def row_sizes(value):
    return jnp.sum(value * value, axis=1, keepdims=True)


def eighth(value):
    square = value * value
    fourth = square * square
    return 1.0 / (fourth * fourth)


def label_kernel(na, me_ref, idx_ref, cls_ref, feat_ref, anch_ref, out_ref, x_ref, a_ref, rows, picked, sems, xsem, asem):
    docs_dev = feat_ref.shape[0]
    docs = x_ref.shape[0]
    base = (me_ref[0] // na) * docs_dev
    count = idx_ref.shape[0]
    copies = []
    for k in range(count):
        start = pl.multiple_of(((idx_ref[k] - base) >> 4) << 4, 16)
        copy = pltpu.make_async_copy(feat_ref.at[pl.ds(start, 16), :], rows.at[k], sems.at[k])
        copy.start()
        copies.append(copy)
    own = pl.ds(pl.multiple_of((me_ref[0] % na) * docs, docs), docs)
    bulk = pltpu.make_async_copy(feat_ref.at[own, :], x_ref, xsem)
    bulk.start()
    points = pltpu.make_async_copy(anch_ref, a_ref, asem)
    points.start()
    sub = lax.broadcasted_iota(jnp.int32, (16, LANES), 0)
    lane = lax.broadcasted_iota(jnp.int32, (1, LANES), 1)
    for k in range(count):
        picked[count + k : count + k + 1, :] = jnp.where(lane == cls_ref[k], 1.0, 0.0)
    for k in range(count):
        copies[k].wait()
        chosen = jnp.where(sub == ((idx_ref[k] - base) & 15), rows[k].astype(f32), 0.0)
        picked[k : k + 1, :] = jnp.sum(chosen, axis=0, keepdims=True)
    out_ref[...] = picked[...].astype(bf16)
    bulk.wait()
    points.wait()


def build_kernel(na, me_ref, a0, a1, a2, a3, x_ref, khi_ref, klo_ref, tinv_ref, aug_ref):
    docs, feat = x_ref.shape
    quarter = a0.shape[0]
    scale = 1.0 / (feat * width_h)
    me = me_ref[0] % na
    for mask, piece in enumerate((a0, a1, a2, a3)):
        at = pl.ds(pl.multiple_of((me ^ mask) * quarter, quarter), quarter)
        value = piece[...].astype(f32)
        aug_ref[at, 0:feat] = (value * (-2.0 * scale)).astype(bf16)
        aug_ref[at, feat:] = aug_columns(row_sizes(value) * scale + 1.0, None, quarter)
    tile = min(256, docs)
    for col in range(0, docs, tile):
        raw = x_ref[col : col + tile, :]
        right = jnp.concatenate([raw, aug_columns(None, row_sizes(raw.astype(f32)) * scale, tile)], axis=1)
        total = jnp.zeros((8, tile), f32)
        for at in range(0, aug_ref.shape[0], 256):
            kern = eighth(mm(aug_ref[at : at + 256, :], right, NT))
            high, low = split2(kern)
            khi_ref[at : at + 256, col : col + tile] = high
            klo_ref[at : at + 256, col : col + tile] = low
            total = total + jnp.sum(kern.reshape(32, 8, tile), axis=0)
        tinv_ref[:, col : col + tile] = 1.0 / jnp.sum(total, axis=0, keepdims=True)


def times(vec, khi, klo):
    one = mm(vec, khi)
    two = mm(vec[0 : 2 * CLASSES], klo)
    return one[0:CLASSES] + (one[CLASSES : 2 * CLASSES] + two[0:CLASSES] + (one[2 * CLASSES :] + two[CLASSES:]))


def times_back(value, khi, klo):
    vec = pieces(value)
    one = mm(vec, khi, NT)
    two = mm(vec[0 : 2 * CLASSES], klo, NT)
    return one[0:CLASSES] + (one[CLASSES : 2 * CLASSES] + two[0:CLASSES] + (one[2 * CLASSES :] + two[CLASSES:]))


def split3(value):
    high = value.astype(bf16)
    rest = value - high.astype(f32)
    middle = rest.astype(bf16)
    return high, middle, (rest - middle.astype(f32)).astype(bf16)


def pieces(value):
    return jnp.concatenate(split3(value), axis=0)


def halves(me_ref, size):
    core = me_ref[0] & 1
    return [pl.ds(pl.multiple_of(part * size, size), size) for part in (core, 1 - core)]


def put_weights(w_ref, spread, tinv):
    for k, part in enumerate(split3(spread * tinv)):
        w_ref[k * CLASSES : (k + 1) * CLASSES, :] = part


def back_rows(w_ref, khi, klo, dims):
    one = mm(w_ref[...], khi, dims)
    two = mm(w_ref[...], klo, dims)
    out = one[0:CLASSES] + (one[CLASSES : 2 * CLASSES] + two[0:CLASSES] + (one[2 * CLASSES : 3 * CLASSES] + two[CLASSES : 2 * CLASSES]))
    return out, one[3 * CLASSES :] + two[3 * CLASSES :]


def back_degree(w_ref, khi, klo, out_ref):
    out, deg = back_rows(w_ref, khi, klo, NT)
    size = out.shape[1]
    deg = deg[0:1] + (deg[1:2] + deg[2:3])
    out_ref[:, 0:size] = out
    out_ref[:, size:] = jnp.zeros((CLASSES, LANES), f32)
    for k in range(size // LANES):
        out_ref[k : k + 1, size:] = deg[:, k * LANES : (k + 1) * LANES]


def mean_of(value):
    return jnp.mean(value, axis=1, keepdims=True)


def total_of(value):
    return jnp.sum(jnp.sum(value, axis=1, keepdims=True), axis=0, keepdims=True)


def first_send(na, labs, slots, gain, me_ref, *refs):
    lab_refs = refs[: len(slots)]
    (aug_ref, khi_ref, klo_ref, tinv_ref, send_ref, w_ref, rhs_ref, mid_ref, zhi_ref, zlo_ref, spread_ref,
     laug, hot) = refs[len(slots) :]
    feat = laug.shape[1] - LANES
    docs = me_ref[0] // na
    for masks, ref in zip(slots, lab_refs):
        for k, mask in enumerate(masks):
            at = pl.ds(pl.multiple_of((docs ^ mask) * labs, labs), labs)
            laug[at, 0:feat] = ref[2 * labs * k : 2 * labs * k + labs, :]
            hot[at, :] = ref[2 * labs * k + labs : 2 * labs * (k + 1), :].astype(f32)
    size = row_sizes(laug[:, 0:feat].astype(f32)) * (1.0 / (feat * width_h))
    laug[:, feat:] = aug_columns(None, size, laug.shape[0])
    kern = eighth(mm(aug_ref[...], laug[...], NT))
    zhi, zlo = split2(kern / jnp.sum(kern, axis=0, keepdims=True))
    zhi_ref[...], zlo_ref[...] = zhi, zlo
    onehot = hot[...].T[0:CLASSES, :].astype(bf16)
    rhs = gain * (mm(onehot, zhi, NT) + mm(onehot, zlo, NT))
    rhs_ref[...] = rhs
    middle = rhs - mean_of(rhs)
    mid_ref[...] = middle
    tinv = tinv_ref[...]
    spread = times(pieces(middle), khi_ref[...], klo_ref[...]) * tinv
    spread_ref[...] = spread
    put_weights(w_ref, spread, tinv)
    row = lax.broadcasted_iota(jnp.int32, (CLASSES, tinv.shape[1]), 0)
    rest = tinv
    ones = jnp.zeros((CLASSES, tinv.shape[1]), f32)
    for k in range(3):
        part = rest.astype(bf16).astype(f32)
        ones = jnp.where(row == k, part, ones)
        rest = rest - part
    w_ref[3 * CLASSES :, :] = ones.astype(bf16)
    _, other = halves(me_ref, khi_ref.shape[0] // 2)
    back_degree(w_ref, khi_ref[other, :], klo_ref[other, :], send_ref)


def first_own(me_ref, w_ref, khi_ref, klo_ref, mine_ref):
    own, _ = halves(me_ref, khi_ref.shape[0] // 2)
    back_degree(w_ref, khi_ref[own, :], klo_ref[own, :], mine_ref)


def flip_kernel(in_ref, out_ref):
    for col in range(0, in_ref.shape[1], 256):
        out_ref[col : col + 256, :] = in_ref[:, col : col + 256].T


def product_own(me_ref, w_ref, thi_ref, tlo_ref, mine_ref):
    own, _ = halves(me_ref, thi_ref.shape[1] // 2)
    mine_ref[...] = back_rows(w_ref, thi_ref[:, own], tlo_ref[:, own], NN)[0]


def residual_part(sums_ref, mid_ref, at, dinv_ref):
    size = sums_ref.shape[1] - LANES
    for k in range(size // LANES):
        dinv_ref[:, k * LANES : (k + 1) * LANES] = 1.0 / sums_ref[k : k + 1, size:]
    return mid_ref[:, at] - sums_ref[:, 0:size] * dinv_ref[...]


def second_own(me_ref, held_ref, mid_ref, khi_ref, klo_ref, part_ref, dinv_ref):
    own, _ = halves(me_ref, khi_ref.shape[0] // 2)
    part_ref[...] = times(pieces(residual_part(held_ref, mid_ref, own, dinv_ref)), khi_ref[own, :], klo_ref[own, :])


def second_send(me_ref, got_ref, mid_ref, khi_ref, klo_ref, thi_ref, tlo_ref, tinv_ref, part_ref, dinv_own, send_ref, w_ref, dinv_ref, dinv_other):
    own, other = halves(me_ref, khi_ref.shape[0] // 2)
    rest = times(pieces(residual_part(got_ref, mid_ref, other, dinv_other)), khi_ref[other, :], klo_ref[other, :])
    dinv_ref[:, own] = dinv_own[...]
    dinv_ref[:, other] = dinv_other[...]
    tinv = tinv_ref[...]
    put_weights(w_ref, (part_ref[...] + rest) * tinv, tinv)
    send_ref[...] = back_rows(w_ref, thi_ref[:, other], tlo_ref[:, other], NN)[0]


def label_image(rhs_ref, zhi_ref, zlo_ref, lab_ref):
    zhi, zlo = zhi_ref[...], zlo_ref[...]
    lab_ref[...] = times_back(times(pieces(rhs_ref[...]), zhi, zlo), zhi, zlo)


def image_shift(lab_scale, lab, rhs):
    return lab_scale * mean_of(lab) + ridge * mean_of(rhs)


def third_own(lab_scale, graph_scale, me_ref, held_ref, rhs_ref, lab_ref, khi_ref, klo_ref, part_ref):
    own, _ = halves(me_ref, khi_ref.shape[0] // 2)
    shift = image_shift(lab_scale, lab_ref[...], rhs_ref[...])
    image = lab_scale * lab_ref[:, own] + graph_scale * held_ref[...] + ridge * rhs_ref[:, own]
    part_ref[...] = times(pieces(image - shift), khi_ref[own, :], klo_ref[own, :])


def third_send(lab_scale, graph_scale, me_ref, held_ref, got_ref, rhs_ref, lab_ref, part_ref, spread0_ref, khi_ref, klo_ref,
               thi_ref, tlo_ref, tinv_ref, send_ref, w_ref, spread_ref, direc_ref, mid_ref, first_ref, stats_ref, whole):
    own, other = halves(me_ref, khi_ref.shape[0] // 2)
    rhs, lab = rhs_ref[...], lab_ref[...]
    whole[:, own] = held_ref[...]
    whole[:, other] = got_ref[...]
    image = lab_scale * lab + graph_scale * whole[...] + ridge * rhs
    shift = image_shift(lab_scale, lab, rhs)
    whole[...] = image - shift
    rest = times(pieces(whole[:, other]), khi_ref[other, :], klo_ref[other, :])
    norm = total_of(rhs * rhs)
    alpha = norm / total_of(rhs * image)
    resid = rhs - alpha * image
    after = total_of(resid * resid)
    beta = after / norm
    direc = resid + beta * rhs
    base = mean_of(rhs)
    level = (1.0 + beta) * base - alpha * shift
    direc_ref[...] = direc
    mid_ref[...] = direc - level
    first_ref[...] = alpha * rhs
    tinv = tinv_ref[...]
    spread = (1.0 + beta) * spread0_ref[...] - alpha * ((part_ref[...] + rest) * tinv)
    put_weights(w_ref, spread, tinv)
    send_ref[...] = back_rows(w_ref, thi_ref[:, other], tlo_ref[:, other], NN)[0]
    spread_ref[...] = spread
    stats_ref[0:CLASSES, :] = jnp.broadcast_to(level, (CLASSES, LANES))
    stats_ref[CLASSES : 2 * CLASSES, :] = jnp.broadcast_to(alpha * base, (CLASSES, LANES))
    stats_ref[2 * CLASSES : 2 * CLASSES + 8, :] = jnp.broadcast_to(alpha, (8, LANES))
    stats_ref[2 * CLASSES + 8 :, :] = jnp.broadcast_to(after, (8, LANES))


def doc_parts(na, lab_scale, me_ref, spread0_ref, spread_ref, stats_ref, direc_ref, zhi_ref, zlo_ref, *refs):
    outs, (base_ref, slots) = refs[0:na], refs[na:]
    quarter = CLASSES // na
    part = stats_ref[2 * CLASSES : 2 * CLASSES + 1, 0:1] * spread0_ref[...] + stats_ref[CLASSES : 2 * CLASSES, 0:1]
    full = spread_ref[...] + stats_ref[0:CLASSES, 0:1]
    for k in range(na):
        slots[k, 0:quarter, :] = part[k * quarter : (k + 1) * quarter]
        slots[k, quarter : 2 * quarter, :] = full[k * quarter : (k + 1) * quarter]
    for mask in range(na):
        outs[mask][...] = slots[(me_ref[0] % na) ^ mask]
    direc = direc_ref[...]
    seen = times(pieces(direc), zhi_ref[...], zlo_ref[...])
    base_ref[...] = jnp.broadcast_to(lab_scale * total_of(seen * seen) + ridge * total_of(direc * direc), base_ref.shape)


def last_kernel(na, graph_scale, me_ref, held_ref, got_ref, direc_ref, mid_ref, first_ref, stats_ref, base_ref, dinv_ref, *refs):
    parts, (anchor_ref, doc_ref, whole) = refs[0:na], refs[na:]
    mine = me_ref[0] % na
    own, other = halves(me_ref, whole.shape[1] // 2)
    whole[:, own] = held_ref[...]
    whole[:, other] = got_ref[...]
    prod = whole[...]
    quad = total_of(prod * (mid_ref[...] - prod * dinv_ref[...]))
    alpha = stats_ref[2 * CLASSES + 8 : 2 * CLASSES + 9, 0:1] / (base_ref[0:1, 0:1] + graph_scale * quad)
    whole[...] = first_ref[...] + alpha * direc_ref[...]
    rows = anchor_ref.shape[1]
    anchor_ref[...] = whole[:, pl.ds(pl.multiple_of(mine * rows, rows), rows)]
    quarter, docs = doc_ref.shape[0], parts[0].shape[1]
    for mask in range(na):
        at = pl.ds(pl.multiple_of((mine ^ mask) * docs, docs), docs)
        doc_ref[:, at] = parts[mask][0:quarter, :] + alpha * parts[mask][quarter:, :]


VMEM = pl.BlockSpec(memory_space=pltpu.MemorySpace.VMEM)
SMEM = pl.BlockSpec(memory_space=pltpu.MemorySpace.SMEM)


def in_hbm(value):
    return pltpu.with_memory_space_constraint(value, pltpu.MemorySpace.HBM)


def call(kernel, in_specs, out_shape, scratch, flops=1 << 20, moved=1 << 18):
    return pl.pallas_call(
        kernel,
        in_specs=in_specs,
        out_specs=[VMEM] * len(out_shape),
        out_shape=out_shape,
        scratch_shapes=scratch,
        compiler_params=pltpu.CompilerParams(vmem_limit_bytes=24 << 20),
        cost_estimate=pl.CostEstimate(flops=flops, bytes_accessed=moved, transcendentals=0),
    )


def run(features, anchors, lab_index, lab_class):
    docs_dev, feat = features.shape
    nd, na = lax.axis_size("docs"), lax.axis_size("anch")
    n_bits = (nd * na).bit_length() - 1
    a_bits = na.bit_length() - 1
    labs = lab_index.shape[0]
    labeled = labs * nd
    quarter = anchors.shape[0]
    total = quarter * na
    docs = docs_dev // na
    lab_scale = total / labeled
    graph_scale = total * total / (docs_dev * nd)
    assert na == 4 and nd * na == 1 << n_bits and total // LANES <= CLASSES and feat == LANES
    sds = jax.ShapeDtypeStruct

    me = lax.axis_index(EVERY).astype(jnp.int32).reshape(1)

    own, mine_x, near = pl.pallas_call(
        functools.partial(label_kernel, na),
        grid_spec=pltpu.PrefetchScalarGridSpec(
            num_scalar_prefetch=3,
            grid=(1,),
            in_specs=[pl.BlockSpec(memory_space=pltpu.MemorySpace.HBM)] * 2,
            out_specs=[VMEM] * 3,
            scratch_shapes=[
                pltpu.VMEM((labs, 16, LANES), bf16),
                pltpu.VMEM((2 * labs, LANES), f32),
                pltpu.SemaphoreType.DMA((labs,)),
                pltpu.SemaphoreType.DMA,
                pltpu.SemaphoreType.DMA,
            ],
        ),
        out_shape=[sds((2 * labs, feat), bf16), sds((docs, feat), bf16), sds((quarter, feat), bf16)],
        name="label_rows",
        compiler_params=pltpu.CompilerParams(vmem_limit_bytes=4 << 20),
    )(me, in_hbm(lab_index), in_hbm(lab_class), in_hbm(features), in_hbm(anchors))

    piece = [near, swap_core(anchors), None, None]
    piece[2] = swap(anchors, 2)
    piece[3] = swap(anchors, 3)

    held, masks = own, [0]
    bits = list(range(a_bits, n_bits))
    stages = bit_groups(bits[:1]) + bit_groups(bits[1:])
    for at, stage in enumerate(stages):
        got = exchange(held, stage)
        if at < len(stages) - 1:
            masks = masks + [m ^ mask for mask in stage for m in masks]
            held = jnp.concatenate([held] + got, axis=0)
    lab_arrays = [held] + got
    slots = [[m >> a_bits for m in masks]] + [[(m ^ mask) >> a_bits for m in masks] for mask in stages[-1]]

    k_sds = sds((total, docs), bf16)
    khi, klo, tinv, aug = call(
        functools.partial(build_kernel, na),
        [SMEM] + [VMEM] * 5,
        [k_sds, k_sds, sds((1, docs), f32), sds((total, feat + LANES), bf16)],
        [],
        flops=2 * total * docs * 256,
        moved=4 * total * docs,
    )(me, *piece, mine_x)

    half = total // 2
    flat_sds = sds((CLASSES, total), f32)
    half_sds = sds((CLASSES, half), f32)
    long_sds = sds((CLASSES, half + LANES), f32)
    docs_sds = sds((CLASSES, docs), f32)
    z_sds = sds((total, labeled), bf16)
    w_sds = sds((3 * CLASSES, docs), bf16)
    work = dict(flops=4 * total * docs * 64, moved=2 * total * docs)

    send, w, rhs, middle, zhi, zlo, spread0 = call(
        functools.partial(first_send, na, labs, slots, CLASSES * lab_scale),
        [SMEM] + [VMEM] * (len(lab_arrays) + 4),
        [long_sds, sds((4 * CLASSES, docs), bf16), flat_sds, flat_sds, z_sds, z_sds, docs_sds],
        [pltpu.VMEM((labeled, feat + LANES), bf16), pltpu.VMEM((labeled, LANES), f32)],
        **work,
    )(me, *lab_arrays, aug, khi, klo, tinv)
    got = swap_core(send)
    mine = call(first_own, [SMEM] + [VMEM] * 3, [long_sds], [], **work)(me, w, khi, klo)[0]
    held = reduce_chips(mine + got, n_bits)
    thi = call(flip_kernel, [VMEM], [sds((docs, total), bf16)], [])(khi)[0]
    tlo = call(flip_kernel, [VMEM], [sds((docs, total), bf16)], [])(klo)[0]
    lab = call(label_image, [VMEM] * 3, [flat_sds], [])(rhs, zhi, zlo)[0]

    got = swap_core(held)
    part, dinv_own = call(
        second_own, [SMEM] + [VMEM] * 4, [docs_sds, sds((1, half), f32)], [], **work
    )(me, held, middle, khi, klo)
    send, w, dinv = call(
        second_send, [SMEM] + [VMEM] * 9, [half_sds, w_sds, sds((1, total), f32)], [pltpu.VMEM((1, half), f32)], **work
    )(me, got, middle, khi, klo, thi, tlo, tinv, part, dinv_own)
    got = swap_core(send)
    mine = call(product_own, [SMEM] + [VMEM] * 3, [half_sds], [], **work)(me, w, thi, tlo)[0]
    held = reduce_chips(mine + got, n_bits)

    got = swap_core(held)
    part = call(
        functools.partial(third_own, lab_scale, graph_scale), [SMEM] + [VMEM] * 5, [docs_sds], [], **work
    )(me, held, rhs, lab, khi, klo)[0]
    send, w, spread, direc, middle, first, stats = call(
        functools.partial(third_send, lab_scale, graph_scale),
        [SMEM] + [VMEM] * 11,
        [half_sds, w_sds, docs_sds, flat_sds, flat_sds, flat_sds, sds((2 * CLASSES + 16, LANES), f32)],
        [pltpu.VMEM((CLASSES, total), f32)],
        **work,
    )(me, held, got, rhs, lab, part, spread0, khi, klo, thi, tlo, tinv)
    got = swap_core(send)
    mine = call(product_own, [SMEM] + [VMEM] * 3, [half_sds], [], **work)(me, w, thi, tlo)[0]
    part_rows = 2 * CLASSES // na
    *docs_out, base = call(
        functools.partial(doc_parts, na, lab_scale),
        [SMEM] + [VMEM] * 6,
        [sds((part_rows, docs), f32)] * na + [sds((8, LANES), f32)],
        [pltpu.VMEM((na, part_rows, docs), f32)],
    )(me, spread0, spread, stats, direc, zhi, zlo)
    held = reduce_chips(mine + got, n_bits)
    got = swap_core(held)

    parts = [docs_out[0]]
    for mask in range(1, na):
        parts.append(swap(docs_out[mask], mask))
    anchor_scores, doc_scores = call(
        functools.partial(last_kernel, na, graph_scale),
        [SMEM] + [VMEM] * (8 + na),
        [sds((CLASSES, quarter), f32), sds((CLASSES // na, docs_dev), f32)],
        [pltpu.VMEM((CLASSES, total), f32)],
    )(me, held, got, direc, middle, first, stats, base, dinv, *parts)
    return anchor_scores.T, doc_scores


def solution(mesh):
    in_specs = (P("docs", None), P("anch", None), P("docs"), P("docs"))
    out_specs = (P("anch", None), P("anch", "docs"))
    return jax.shard_map(run, mesh=mesh, in_specs=in_specs, out_specs=out_specs, check_vma=False)
```

```python
import functools

import jax
import jax.numpy as jnp
from jax import lax
from jax.experimental import pallas as pl
from jax.experimental.pallas import tpu as pltpu
from jax.sharding import PartitionSpec as P


CLASSES = 16

width_h = 0.25
ridge = 0.1
f32 = jnp.float32
bf16 = jnp.bfloat16
EVERY = ("docs", "anch")
LANES = 128

NT = (((1,), (1,)), ((), ()))
NN = (((1,), (0,)), ((), ()))


def mm(left, right, dims=NN, precision=None):
    return lax.dot_general(left, right, dims, precision=precision, preferred_element_type=f32)


def split2(value):
    high = value.astype(bf16)
    return high, (value - high.astype(f32)).astype(bf16)


def swap(value, mask):
    count = lax.axis_size("docs") * lax.axis_size("anch")
    return lax.ppermute(value, EVERY, [(i, i ^ mask) for i in range(count)])


def bit_groups(bits):
    groups = []
    while bits:
        part, bits = bits[:2], bits[2:]
        masks = [1 << part[0]]
        if len(part) == 2:
            masks += [1 << part[1], (1 << part[0]) | (1 << part[1])]
        groups.append(masks)
    return groups


def exchange(value, masks):
    got = []
    for mask in masks:
        got.append(swap(value, mask))
    return got


def sum_stage(held, masks):
    got = exchange(held, masks)
    if len(got) == 1:
        return held + got[0]
    return (held + got[0]) + (got[1] + got[2])


def reduce_chips(held, n_bits):
    for masks in bit_groups(list(range(1, n_bits))):
        held = sum_stage(held, masks)
    return held


def swap_core(value):
    return swap(value, 1)


def aug_columns(first, second, rows):
    lane = lax.broadcasted_iota(jnp.int32, (rows, LANES), 1)
    out = jnp.zeros((rows, LANES), f32)
    for base, column in ((0, first), (3, second)):
        if column is None:
            out = jnp.where((lane >= base) & (lane < base + 3), 1.0, out)
        else:
            rest = column
            for piece in range(3):
                part = rest.astype(bf16).astype(f32)
                out = jnp.where(lane == base + piece, part, out)
                rest = rest - part
    return out.astype(bf16)


def row_sizes(value):
    return jnp.sum(value * value, axis=1, keepdims=True)


def eighth(value):
    square = value * value
    fourth = square * square
    return 1.0 / (fourth * fourth)


def label_kernel(na, me_ref, idx_ref, cls_ref, feat_ref, anch_ref, out_ref, x_ref, a_ref, rows, picked, sems, xsem, asem):
    docs_dev = feat_ref.shape[0]
    docs = x_ref.shape[0]
    base = (me_ref[0] // na) * docs_dev
    count = idx_ref.shape[0]
    copies = []
    for k in range(count):
        start = pl.multiple_of(((idx_ref[k] - base) >> 4) << 4, 16)
        copy = pltpu.make_async_copy(feat_ref.at[pl.ds(start, 16), :], rows.at[k], sems.at[k])
        copy.start()
        copies.append(copy)
    own = pl.ds(pl.multiple_of((me_ref[0] % na) * docs, docs), docs)
    bulk = pltpu.make_async_copy(feat_ref.at[own, :], x_ref, xsem)
    bulk.start()
    points = pltpu.make_async_copy(anch_ref, a_ref, asem)
    points.start()
    sub = lax.broadcasted_iota(jnp.int32, (16, LANES), 0)
    lane = lax.broadcasted_iota(jnp.int32, (1, LANES), 1)
    for k in range(count):
        picked[count + k : count + k + 1, :] = jnp.where(lane == cls_ref[k], 1.0, 0.0)
    for k in range(count):
        copies[k].wait()
        chosen = jnp.where(sub == ((idx_ref[k] - base) & 15), rows[k].astype(f32), 0.0)
        picked[k : k + 1, :] = jnp.sum(chosen, axis=0, keepdims=True)
    out_ref[...] = picked[...].astype(bf16)
    bulk.wait()
    points.wait()


def build_kernel(na, me_ref, a0, a1, a2, a3, x_ref, khi_ref, klo_ref, aug_ref):
    docs, feat = x_ref.shape
    quarter = a0.shape[0]
    scale = 1.0 / (feat * width_h)
    me = me_ref[0] % na
    for mask, piece in enumerate((a0, a1, a2, a3)):
        at = pl.ds(pl.multiple_of((me ^ mask) * quarter, quarter), quarter)
        value = piece[...].astype(f32)
        aug_ref[at, 0:feat] = (value * (-2.0 * scale)).astype(bf16)
        aug_ref[at, feat:] = aug_columns(row_sizes(value) * scale + 1.0, None, quarter)
    tile = min(256, docs)
    row = lax.broadcasted_iota(jnp.int32, (16, tile), 0)
    rest = jnp.zeros((aug_ref.shape[1] - feat - 16, tile), bf16)
    for col in range(0, docs, tile):
        turned = x_ref[col : col + tile, :].T
        wide = turned.astype(f32)
        size = jnp.sum(wide * wide, axis=0, keepdims=True) * scale
        extra = jnp.where(row < 3, 1.0, 0.0)
        for k, part in enumerate(split3(size)):
            extra = jnp.where(row == 3 + k, part.astype(f32), extra)
        right = jnp.concatenate([turned, extra.astype(bf16), rest], axis=0)
        for at in range(0, aug_ref.shape[0], 256):
            kern = eighth(mm(aug_ref[at : at + 256, :], right))
            high, low = split2(kern)
            khi_ref[at : at + 256, col : col + tile] = high
            klo_ref[at : at + 256, col : col + tile] = low


def times(vec, khi, klo):
    more = vec.shape[0] > 3 * CLASSES
    one = mm(vec, khi)
    two = mm(vec if more else vec[0 : 2 * CLASSES], klo)
    out = one[0:CLASSES] + (one[CLASSES : 2 * CLASSES] + two[0:CLASSES] + (one[2 * CLASSES : 3 * CLASSES] + two[CLASSES : 2 * CLASSES]))
    return (out, one[3 * CLASSES :] + two[3 * CLASSES :]) if more else out


def times_back(value, khi, klo):
    vec = pieces(value)
    one = mm(vec, khi, NT)
    two = mm(vec[0 : 2 * CLASSES], klo, NT)
    return one[0:CLASSES] + (one[CLASSES : 2 * CLASSES] + two[0:CLASSES] + (one[2 * CLASSES :] + two[CLASSES:]))


def split3(value):
    high = value.astype(bf16)
    rest = value - high.astype(f32)
    middle = rest.astype(bf16)
    return high, middle, (rest - middle.astype(f32)).astype(bf16)


def pieces(value):
    return jnp.concatenate(split3(value), axis=0)


def halves(me_ref, size):
    core = me_ref[0] & 1
    return [pl.ds(pl.multiple_of(part * size, size), size) for part in (core, 1 - core)]


def put_weights(w_ref, spread, tinv):
    for k, part in enumerate(split3(spread * tinv)):
        w_ref[k * CLASSES : (k + 1) * CLASSES, :] = part


def back_rows(w_ref, khi, klo, dims):
    one = mm(w_ref[...], khi, dims)
    rows = w_ref.shape[0]
    two = mm(w_ref[0 : 2 * CLASSES, :] if rows == 3 * CLASSES else w_ref[...], klo, dims)
    out = one[0:CLASSES] + (one[CLASSES : 2 * CLASSES] + two[0:CLASSES] + (one[2 * CLASSES : 3 * CLASSES] + two[CLASSES : 2 * CLASSES]))
    return out, one[3 * CLASSES :] + two[3 * CLASSES :] if rows > 3 * CLASSES else None


def back_degree(w_ref, khi, klo, out_ref):
    out, deg = back_rows(w_ref, khi, klo, NT)
    size = out.shape[1]
    deg = deg[0:1] + (deg[1:2] + deg[2:3])
    out_ref[:, 0:size] = out
    out_ref[:, size:] = jnp.zeros((CLASSES, LANES), f32)
    for k in range(size // LANES):
        out_ref[k : k + 1, size:] = deg[:, k * LANES : (k + 1) * LANES]


def mean_of(value):
    return jnp.mean(value, axis=1, keepdims=True)


def total_of(value):
    return jnp.sum(jnp.sum(value, axis=1, keepdims=True), axis=0, keepdims=True)


def first_send(na, labs, slots, gain, me_ref, *refs):
    lab_refs = refs[: len(slots)]
    (aug_ref, khi_ref, klo_ref, send_ref, w_ref, rhs_ref, mid_ref, zhi_ref, zlo_ref, spread_ref, tinv_ref,
     laug, hot) = refs[len(slots) :]
    feat = laug.shape[1] - LANES
    docs = me_ref[0] // na
    for masks, ref in zip(slots, lab_refs):
        for k, mask in enumerate(masks):
            at = pl.ds(pl.multiple_of((docs ^ mask) * labs, labs), labs)
            laug[at, 0:feat] = ref[2 * labs * k : 2 * labs * k + labs, :]
            hot[at, :] = ref[2 * labs * k + labs : 2 * labs * (k + 1), :].astype(f32)
    size = row_sizes(laug[:, 0:feat].astype(f32)) * (1.0 / (feat * width_h))
    laug[:, feat:] = aug_columns(None, size, laug.shape[0])
    kern = eighth(mm(aug_ref[...], laug[...], NT))
    zhi, zlo = split2(kern / jnp.sum(kern, axis=0, keepdims=True))
    zhi_ref[...], zlo_ref[...] = zhi, zlo
    onehot = hot[...].T[0:CLASSES, :].astype(bf16)
    rhs = gain * (mm(onehot, zhi, NT) + mm(onehot, zlo, NT))
    rhs_ref[...] = rhs
    middle = rhs - mean_of(rhs)
    mid_ref[...] = middle
    vec = jnp.concatenate([*split3(middle), jnp.ones(middle.shape, bf16)], axis=0)
    spread, sums = times(vec, khi_ref[...], klo_ref[...])
    tinv = 1.0 / sums[0:1]
    tinv_ref[...] = tinv
    spread = spread * tinv
    spread_ref[...] = spread
    put_weights(w_ref, spread, tinv)
    row = lax.broadcasted_iota(jnp.int32, (CLASSES, tinv.shape[1]), 0)
    rest = tinv
    ones = jnp.zeros((CLASSES, tinv.shape[1]), f32)
    for k in range(3):
        part = rest.astype(bf16).astype(f32)
        ones = jnp.where(row == k, part, ones)
        rest = rest - part
    w_ref[3 * CLASSES :, :] = ones.astype(bf16)
    _, other = halves(me_ref, khi_ref.shape[0] // 2)
    back_degree(w_ref, khi_ref[other, :], klo_ref[other, :], send_ref)


def first_own(me_ref, w_ref, khi_ref, klo_ref, mine_ref):
    own, _ = halves(me_ref, khi_ref.shape[0] // 2)
    back_degree(w_ref, khi_ref[own, :], klo_ref[own, :], mine_ref)


def flip_kernel(in_ref, out_ref):
    for col in range(0, in_ref.shape[1], 256):
        out_ref[col : col + 256, :] = in_ref[:, col : col + 256].T


def product_own(me_ref, w_ref, thi_ref, tlo_ref, mine_ref):
    own, _ = halves(me_ref, thi_ref.shape[1] // 2)
    mine_ref[...] = back_rows(w_ref, thi_ref[:, own], tlo_ref[:, own], NN)[0]


def residual_part(sums_ref, mid_ref, at, dinv_ref):
    size = sums_ref.shape[1] - LANES
    for k in range(size // LANES):
        dinv_ref[:, k * LANES : (k + 1) * LANES] = 1.0 / sums_ref[k : k + 1, size:]
    return mid_ref[:, at] - sums_ref[:, 0:size] * dinv_ref[...]


def second_own(me_ref, held_ref, mid_ref, khi_ref, klo_ref, part_ref, dinv_ref):
    own, _ = halves(me_ref, khi_ref.shape[0] // 2)
    part_ref[...] = times(pieces(residual_part(held_ref, mid_ref, own, dinv_ref)), khi_ref[own, :], klo_ref[own, :])


def second_send(me_ref, got_ref, mid_ref, khi_ref, klo_ref, thi_ref, tlo_ref, tinv_ref, part_ref, dinv_own, send_ref, w_ref, dinv_ref, dinv_other):
    own, other = halves(me_ref, khi_ref.shape[0] // 2)
    rest = times(pieces(residual_part(got_ref, mid_ref, other, dinv_other)), khi_ref[other, :], klo_ref[other, :])
    dinv_ref[:, own] = dinv_own[...]
    dinv_ref[:, other] = dinv_other[...]
    tinv = tinv_ref[...]
    put_weights(w_ref, (part_ref[...] + rest) * tinv, tinv)
    send_ref[...] = back_rows(w_ref, thi_ref[:, other], tlo_ref[:, other], NN)[0]


def label_image(rhs_ref, zhi_ref, zlo_ref, lab_ref):
    zhi, zlo = zhi_ref[...], zlo_ref[...]
    lab_ref[...] = times_back(times(pieces(rhs_ref[...]), zhi, zlo), zhi, zlo)


def image_shift(lab_scale, lab, rhs):
    return lab_scale * mean_of(lab) + ridge * mean_of(rhs)


def third_own(lab_scale, graph_scale, me_ref, held_ref, rhs_ref, lab_ref, khi_ref, klo_ref, part_ref):
    own, _ = halves(me_ref, khi_ref.shape[0] // 2)
    shift = image_shift(lab_scale, lab_ref[...], rhs_ref[...])
    image = lab_scale * lab_ref[:, own] + graph_scale * held_ref[...] + ridge * rhs_ref[:, own]
    part_ref[...] = times(pieces(image - shift), khi_ref[own, :], klo_ref[own, :])


def third_send(lab_scale, graph_scale, me_ref, held_ref, got_ref, rhs_ref, lab_ref, part_ref, spread0_ref, khi_ref, klo_ref,
               thi_ref, tlo_ref, tinv_ref, send_ref, w_ref, spread_ref, direc_ref, mid_ref, first_ref, stats_ref, whole):
    own, other = halves(me_ref, khi_ref.shape[0] // 2)
    rhs, lab = rhs_ref[...], lab_ref[...]
    whole[:, own] = held_ref[...]
    whole[:, other] = got_ref[...]
    image = lab_scale * lab + graph_scale * whole[...] + ridge * rhs
    shift = image_shift(lab_scale, lab, rhs)
    whole[...] = image - shift
    rest = times(pieces(whole[:, other]), khi_ref[other, :], klo_ref[other, :])
    norm = total_of(rhs * rhs)
    alpha = norm / total_of(rhs * image)
    resid = rhs - alpha * image
    after = total_of(resid * resid)
    beta = after / norm
    direc = resid + beta * rhs
    base = mean_of(rhs)
    level = (1.0 + beta) * base - alpha * shift
    direc_ref[...] = direc
    mid_ref[...] = direc - level
    first_ref[...] = alpha * rhs
    tinv = tinv_ref[...]
    spread = (1.0 + beta) * spread0_ref[...] - alpha * ((part_ref[...] + rest) * tinv)
    put_weights(w_ref, spread, tinv)
    send_ref[...] = back_rows(w_ref, thi_ref[:, other], tlo_ref[:, other], NN)[0]
    spread_ref[...] = spread
    stats_ref[0:CLASSES, :] = jnp.broadcast_to(level, (CLASSES, LANES))
    stats_ref[CLASSES : 2 * CLASSES, :] = jnp.broadcast_to(alpha * base, (CLASSES, LANES))
    stats_ref[2 * CLASSES : 2 * CLASSES + 8, :] = jnp.broadcast_to(alpha, (8, LANES))
    stats_ref[2 * CLASSES + 8 :, :] = jnp.broadcast_to(after, (8, LANES))


def doc_parts(na, lab_scale, me_ref, spread0_ref, spread_ref, stats_ref, direc_ref, zhi_ref, zlo_ref, *refs):
    outs, (base_ref, slots) = refs[0:na], refs[na:]
    quarter = CLASSES // na
    part = stats_ref[2 * CLASSES : 2 * CLASSES + 1, 0:1] * spread0_ref[...] + stats_ref[CLASSES : 2 * CLASSES, 0:1]
    full = spread_ref[...] + stats_ref[0:CLASSES, 0:1]
    for k in range(na):
        slots[k, 0:quarter, :] = part[k * quarter : (k + 1) * quarter]
        slots[k, quarter : 2 * quarter, :] = full[k * quarter : (k + 1) * quarter]
    for mask in range(na):
        outs[mask][...] = slots[(me_ref[0] % na) ^ mask]
    direc = direc_ref[...]
    seen = times(pieces(direc), zhi_ref[...], zlo_ref[...])
    base_ref[...] = jnp.broadcast_to(lab_scale * total_of(seen * seen) + ridge * total_of(direc * direc), base_ref.shape)


def last_kernel(na, graph_scale, me_ref, held_ref, got_ref, direc_ref, mid_ref, first_ref, stats_ref, base_ref, dinv_ref, *refs):
    parts, (anchor_ref, doc_ref, whole) = refs[0:na], refs[na:]
    mine = me_ref[0] % na
    own, other = halves(me_ref, whole.shape[1] // 2)
    whole[:, own] = held_ref[...]
    whole[:, other] = got_ref[...]
    prod = whole[...]
    quad = total_of(prod * (mid_ref[...] - prod * dinv_ref[...]))
    alpha = stats_ref[2 * CLASSES + 8 : 2 * CLASSES + 9, 0:1] / (base_ref[0:1, 0:1] + graph_scale * quad)
    whole[...] = first_ref[...] + alpha * direc_ref[...]
    rows = anchor_ref.shape[1]
    anchor_ref[...] = whole[:, pl.ds(pl.multiple_of(mine * rows, rows), rows)]
    quarter, docs = doc_ref.shape[0], parts[0].shape[1]
    for mask in range(na):
        at = pl.ds(pl.multiple_of((mine ^ mask) * docs, docs), docs)
        doc_ref[:, at] = parts[mask][0:quarter, :] + alpha * parts[mask][quarter:, :]


VMEM = pl.BlockSpec(memory_space=pltpu.MemorySpace.VMEM)
SMEM = pl.BlockSpec(memory_space=pltpu.MemorySpace.SMEM)


def in_hbm(value):
    return pltpu.with_memory_space_constraint(value, pltpu.MemorySpace.HBM)


def call(kernel, in_specs, out_shape, scratch, flops=1 << 20, moved=1 << 18):
    return pl.pallas_call(
        kernel,
        in_specs=in_specs,
        out_specs=[VMEM] * len(out_shape),
        out_shape=out_shape,
        scratch_shapes=scratch,
        compiler_params=pltpu.CompilerParams(vmem_limit_bytes=24 << 20),
        cost_estimate=pl.CostEstimate(flops=flops, bytes_accessed=moved, transcendentals=0),
    )


def run(features, anchors, lab_index, lab_class):
    docs_dev, feat = features.shape
    nd, na = lax.axis_size("docs"), lax.axis_size("anch")
    n_bits = (nd * na).bit_length() - 1
    a_bits = na.bit_length() - 1
    labs = lab_index.shape[0]
    labeled = labs * nd
    quarter = anchors.shape[0]
    total = quarter * na
    docs = docs_dev // na
    lab_scale = total / labeled
    graph_scale = total * total / (docs_dev * nd)
    assert na == 4 and nd * na == 1 << n_bits and total // LANES <= CLASSES and feat == LANES
    sds = jax.ShapeDtypeStruct

    me = lax.axis_index(EVERY).astype(jnp.int32).reshape(1)

    own, mine_x, near = pl.pallas_call(
        functools.partial(label_kernel, na),
        grid_spec=pltpu.PrefetchScalarGridSpec(
            num_scalar_prefetch=3,
            grid=(1,),
            in_specs=[pl.BlockSpec(memory_space=pltpu.MemorySpace.HBM)] * 2,
            out_specs=[VMEM] * 3,
            scratch_shapes=[
                pltpu.VMEM((labs, 16, LANES), bf16),
                pltpu.VMEM((2 * labs, LANES), f32),
                pltpu.SemaphoreType.DMA((labs,)),
                pltpu.SemaphoreType.DMA,
                pltpu.SemaphoreType.DMA,
            ],
        ),
        out_shape=[sds((2 * labs, feat), bf16), sds((docs, feat), bf16), sds((quarter, feat), bf16)],
        name="label_rows",
        compiler_params=pltpu.CompilerParams(vmem_limit_bytes=4 << 20),
    )(me, in_hbm(lab_index), in_hbm(lab_class), in_hbm(features), in_hbm(anchors))

    piece = [near, swap_core(anchors), None, None]
    piece[2] = swap(anchors, 2)
    piece[3] = swap(anchors, 3)

    held, masks = own, [0]
    bits = list(range(a_bits, n_bits))
    stages = bit_groups(bits[:1]) + bit_groups(bits[1:])
    for at, stage in enumerate(stages):
        got = exchange(held, stage)
        if at < len(stages) - 1:
            masks = masks + [m ^ mask for mask in stage for m in masks]
            held = jnp.concatenate([held] + got, axis=0)
    lab_arrays = [held] + got
    slots = [[m >> a_bits for m in masks]] + [[(m ^ mask) >> a_bits for m in masks] for mask in stages[-1]]

    k_sds = sds((total, docs), bf16)
    khi, klo, aug = call(
        functools.partial(build_kernel, na),
        [SMEM] + [VMEM] * 5,
        [k_sds, k_sds, sds((total, feat + LANES), bf16)],
        [],
        flops=2 * total * docs * 256,
        moved=4 * total * docs,
    )(me, *piece, mine_x)

    half = total // 2
    flat_sds = sds((CLASSES, total), f32)
    half_sds = sds((CLASSES, half), f32)
    long_sds = sds((CLASSES, half + LANES), f32)
    docs_sds = sds((CLASSES, docs), f32)
    z_sds = sds((total, labeled), bf16)
    w_sds = sds((3 * CLASSES, docs), bf16)
    work = dict(flops=4 * total * docs * 64, moved=2 * total * docs)

    send, w, rhs, middle, zhi, zlo, spread0, tinv = call(
        functools.partial(first_send, na, labs, slots, CLASSES * lab_scale),
        [SMEM] + [VMEM] * (len(lab_arrays) + 3),
        [long_sds, sds((4 * CLASSES, docs), bf16), flat_sds, flat_sds, z_sds, z_sds, docs_sds, sds((1, docs), f32)],
        [pltpu.VMEM((labeled, feat + LANES), bf16), pltpu.VMEM((labeled, LANES), f32)],
        **work,
    )(me, *lab_arrays, aug, khi, klo)
    got = swap_core(send)
    mine = call(first_own, [SMEM] + [VMEM] * 3, [long_sds], [], **work)(me, w, khi, klo)[0]
    held = reduce_chips(mine + got, n_bits)
    thi = call(flip_kernel, [VMEM], [sds((docs, total), bf16)], [])(khi)[0]
    tlo = call(flip_kernel, [VMEM], [sds((docs, total), bf16)], [])(klo)[0]
    lab = call(label_image, [VMEM] * 3, [flat_sds], [])(rhs, zhi, zlo)[0]

    got = swap_core(held)
    part, dinv_own = call(
        second_own, [SMEM] + [VMEM] * 4, [docs_sds, sds((1, half), f32)], [], **work
    )(me, held, middle, khi, klo)
    send, w, dinv = call(
        second_send, [SMEM] + [VMEM] * 9, [half_sds, w_sds, sds((1, total), f32)], [pltpu.VMEM((1, half), f32)], **work
    )(me, got, middle, khi, klo, thi, tlo, tinv, part, dinv_own)
    got = swap_core(send)
    mine = call(product_own, [SMEM] + [VMEM] * 3, [half_sds], [], **work)(me, w, thi, tlo)[0]
    held = reduce_chips(mine + got, n_bits)

    got = swap_core(held)
    part = call(
        functools.partial(third_own, lab_scale, graph_scale), [SMEM] + [VMEM] * 5, [docs_sds], [], **work
    )(me, held, rhs, lab, khi, klo)[0]
    send, w, spread, direc, middle, first, stats = call(
        functools.partial(third_send, lab_scale, graph_scale),
        [SMEM] + [VMEM] * 11,
        [half_sds, w_sds, docs_sds, flat_sds, flat_sds, flat_sds, sds((2 * CLASSES + 16, LANES), f32)],
        [pltpu.VMEM((CLASSES, total), f32)],
        **work,
    )(me, held, got, rhs, lab, part, spread0, khi, klo, thi, tlo, tinv)
    got = swap_core(send)
    mine = call(product_own, [SMEM] + [VMEM] * 3, [half_sds], [], **work)(me, w, thi, tlo)[0]
    part_rows = 2 * CLASSES // na
    *docs_out, base = call(
        functools.partial(doc_parts, na, lab_scale),
        [SMEM] + [VMEM] * 6,
        [sds((part_rows, docs), f32)] * na + [sds((8, LANES), f32)],
        [pltpu.VMEM((na, part_rows, docs), f32)],
    )(me, spread0, spread, stats, direc, zhi, zlo)
    held = reduce_chips(mine + got, n_bits)
    got = swap_core(held)

    parts = [docs_out[0]]
    for mask in range(1, na):
        parts.append(swap(docs_out[mask], mask))
    anchor_scores, doc_scores = call(
        functools.partial(last_kernel, na, graph_scale),
        [SMEM] + [VMEM] * (8 + na),
        [sds((CLASSES, quarter), f32), sds((CLASSES // na, docs_dev), f32)],
        [pltpu.VMEM((CLASSES, total), f32)],
    )(me, held, got, direc, middle, first, stats, base, dinv, *parts)
    return anchor_scores.T, doc_scores


def solution(mesh):
    in_specs = (P("docs", None), P("anch", None), P("docs"), P("docs"))
    out_specs = (P("anch", None), P("anch", "docs"))
    return jax.shard_map(run, mesh=mesh, in_specs=in_specs, out_specs=out_specs, check_vma=False)
```

```python
import functools

import jax
import jax.numpy as jnp
from jax import lax
from jax.experimental import pallas as pl
from jax.experimental.pallas import tpu as pltpu
from jax.sharding import PartitionSpec as P


CLASSES = 16

width_h = 0.25
ridge = 0.1
f32 = jnp.float32
bf16 = jnp.bfloat16
EVERY = ("docs", "anch")
LANES = 128

NT = (((1,), (1,)), ((), ()))
NN = (((1,), (0,)), ((), ()))


def mm(left, right, dims=NN, precision=None):
    return lax.dot_general(left, right, dims, precision=precision, preferred_element_type=f32)


def split2(value):
    high = value.astype(bf16)
    return high, (value - high.astype(f32)).astype(bf16)


def swap(value, mask):
    count = lax.axis_size("docs") * lax.axis_size("anch")
    return lax.ppermute(value, EVERY, [(i, i ^ mask) for i in range(count)])


def bit_groups(bits):
    groups = []
    while bits:
        part, bits = bits[:2], bits[2:]
        masks = [1 << part[0]]
        if len(part) == 2:
            masks += [1 << part[1], (1 << part[0]) | (1 << part[1])]
        groups.append(masks)
    return groups


def exchange(value, masks):
    got = []
    for mask in masks:
        got.append(swap(value, mask))
    return got


def sum_stage(held, masks):
    got = exchange(held, masks)
    if len(got) == 1:
        return held + got[0]
    return (held + got[0]) + (got[1] + got[2])


def reduce_chips(held, n_bits):
    for masks in bit_groups(list(range(1, n_bits))):
        held = sum_stage(held, masks)
    return held


def swap_core(value):
    return swap(value, 1)


def side_rows(turned, scale, shift, first, size):
    wide = turned.astype(f32)
    norms = jnp.sum(wide * wide, axis=0, keepdims=True) * scale + shift
    row = lax.broadcasted_iota(jnp.int32, (16, turned.shape[1]), 0)
    out = jnp.where(row < 6, 1.0, 0.0)
    for k, part in enumerate(split3(norms)):
        out = jnp.where(row == first + k, part.astype(f32), out)
    return jnp.concatenate([out.astype(bf16), jnp.zeros((size - 16, turned.shape[1]), bf16)], axis=0)


def eighth(value):
    square = value * value
    fourth = square * square
    return 1.0 / (fourth * fourth)


def label_kernel(na, me_ref, idx_ref, cls_ref, feat_ref, anch_ref, out_ref, x_ref, a_ref, rows, picked, sems, xsem, asem):
    docs_dev = feat_ref.shape[0]
    docs = x_ref.shape[0]
    base = (me_ref[0] // na) * docs_dev
    count = idx_ref.shape[0]
    copies = []
    for k in range(count):
        start = pl.multiple_of(((idx_ref[k] - base) >> 4) << 4, 16)
        copy = pltpu.make_async_copy(feat_ref.at[pl.ds(start, 16), :], rows.at[k], sems.at[k])
        copy.start()
        copies.append(copy)
    own = pl.ds(pl.multiple_of((me_ref[0] % na) * docs, docs), docs)
    bulk = pltpu.make_async_copy(feat_ref.at[own, :], x_ref, xsem)
    bulk.start()
    points = pltpu.make_async_copy(anch_ref, a_ref, asem)
    points.start()
    sub = lax.broadcasted_iota(jnp.int32, (16, LANES), 0)
    lane = lax.broadcasted_iota(jnp.int32, (1, LANES), 1)
    for k in range(count):
        picked[count + k : count + k + 1, :] = jnp.where(lane == cls_ref[k], 1.0, 0.0)
    for copy in copies:
        copy.wait()
    for k in range(count):
        chosen = jnp.where(sub == ((idx_ref[k] - base) & 15), rows[k].astype(f32), 0.0)
        picked[k : k + 1, :] = jnp.sum(chosen, axis=0, keepdims=True)
    out_ref[...] = picked[...].astype(bf16)
    bulk.wait()
    points.wait()


def build_kernel(na, me_ref, a0, a1, a2, a3, x_ref, khi_ref, klo_ref, aug_ref):
    docs, feat = x_ref.shape
    quarter = a0.shape[0]
    scale = 1.0 / (feat * width_h)
    me = me_ref[0] % na
    for mask, piece in enumerate((a0, a1, a2, a3)):
        at = pl.ds(pl.multiple_of((me ^ mask) * quarter, quarter), quarter)
        aug_ref[at, 0:feat] = (piece[...].astype(f32) * (-2.0 * scale)).astype(bf16)
        aug_ref[at, feat:] = side_rows(piece[...].T, scale, 1.0, 0, LANES).T
    tile = min(256, docs)
    for col in range(0, docs, tile):
        turned = x_ref[col : col + tile, :].T
        right = jnp.concatenate([turned, side_rows(turned, scale, 0.0, 3, LANES)], axis=0)
        for at in range(0, aug_ref.shape[0], 256):
            kern = eighth(mm(aug_ref[at : at + 256, :], right))
            high, low = split2(kern)
            khi_ref[at : at + 256, col : col + tile] = high
            klo_ref[at : at + 256, col : col + tile] = low


def times(vec, khi, klo):
    more = vec.shape[0] > 3 * CLASSES
    one = mm(vec, khi)
    two = mm(vec if more else vec[0 : 2 * CLASSES], klo)
    out = one[0:CLASSES] + (one[CLASSES : 2 * CLASSES] + two[0:CLASSES] + (one[2 * CLASSES : 3 * CLASSES] + two[CLASSES : 2 * CLASSES]))
    return (out, one[3 * CLASSES :] + two[3 * CLASSES :]) if more else out


def times_back(value, khi, klo):
    vec = pieces(value)
    one = mm(vec, khi, NT)
    two = mm(vec[0 : 2 * CLASSES], klo, NT)
    return one[0:CLASSES] + (one[CLASSES : 2 * CLASSES] + two[0:CLASSES] + (one[2 * CLASSES :] + two[CLASSES:]))


def split3(value):
    high = value.astype(bf16)
    rest = value - high.astype(f32)
    middle = rest.astype(bf16)
    return high, middle, (rest - middle.astype(f32)).astype(bf16)


def pieces(value):
    return jnp.concatenate(split3(value), axis=0)


def halves(me_ref, size):
    core = me_ref[0] & 1
    return [pl.ds(pl.multiple_of(part * size, size), size) for part in (core, 1 - core)]


def put_weights(w_ref, spread, tinv):
    for k, part in enumerate(split3(spread * tinv)):
        w_ref[k * CLASSES : (k + 1) * CLASSES, :] = part


def back_rows(w_ref, khi, klo, dims):
    one = mm(w_ref[...], khi, dims)
    rows = w_ref.shape[0]
    two = mm(w_ref[0 : 2 * CLASSES, :] if rows == 3 * CLASSES else w_ref[...], klo, dims)
    out = one[0:CLASSES] + (one[CLASSES : 2 * CLASSES] + two[0:CLASSES] + (one[2 * CLASSES : 3 * CLASSES] + two[CLASSES : 2 * CLASSES]))
    return out, one[3 * CLASSES :] + two[3 * CLASSES :] if rows > 3 * CLASSES else None


def back_degree(w_ref, khi, klo, out_ref):
    out, deg = back_rows(w_ref, khi, klo, NT)
    size = out.shape[1]
    deg = deg[0:1] + (deg[1:2] + deg[2:3])
    out_ref[:, 0:size] = out
    out_ref[:, size:] = jnp.zeros((CLASSES, LANES), f32)
    for k in range(size // LANES):
        out_ref[k : k + 1, size:] = deg[:, k * LANES : (k + 1) * LANES]


def mean_of(value):
    return jnp.mean(value, axis=1, keepdims=True)


def total_of(value):
    return jnp.sum(jnp.sum(value, axis=1, keepdims=True), axis=0, keepdims=True)


def first_send(na, labs, slots, gain, me_ref, *refs):
    lab_refs = refs[: len(slots)]
    (aug_ref, khi_ref, klo_ref, send_ref, w_ref, rhs_ref, mid_ref, zhi_ref, zlo_ref, spread_ref, tinv_ref,
     laug, hot) = refs[len(slots) :]
    feat = laug.shape[1]
    docs = me_ref[0] // na
    for masks, ref in zip(slots, lab_refs):
        for k, mask in enumerate(masks):
            at = pl.ds(pl.multiple_of((docs ^ mask) * labs, labs), labs)
            laug[at, :] = ref[2 * labs * k : 2 * labs * k + labs, :]
            hot[at, :] = ref[2 * labs * k + labs : 2 * labs * (k + 1), :].astype(f32)
    turned = laug[...].T
    right = jnp.concatenate([turned, side_rows(turned, 1.0 / (feat * width_h), 0.0, 3, LANES)], axis=0)
    kern = eighth(mm(aug_ref[...], right))
    zhi, zlo = split2(kern / jnp.sum(kern, axis=0, keepdims=True))
    zhi_ref[...], zlo_ref[...] = zhi, zlo
    onehot = hot[...].T[0:CLASSES, :].astype(bf16)
    rhs = gain * (mm(onehot, zhi, NT) + mm(onehot, zlo, NT))
    rhs_ref[...] = rhs
    middle = rhs - mean_of(rhs)
    mid_ref[...] = middle
    vec = jnp.concatenate([*split3(middle), jnp.ones(middle.shape, bf16)], axis=0)
    spread, sums = times(vec, khi_ref[...], klo_ref[...])
    tinv = 1.0 / sums[0:1]
    tinv_ref[...] = tinv
    spread = spread * tinv
    spread_ref[...] = spread
    put_weights(w_ref, spread, tinv)
    row = lax.broadcasted_iota(jnp.int32, (CLASSES, tinv.shape[1]), 0)
    rest = tinv
    ones = jnp.zeros((CLASSES, tinv.shape[1]), f32)
    for k in range(3):
        part = rest.astype(bf16).astype(f32)
        ones = jnp.where(row == k, part, ones)
        rest = rest - part
    w_ref[3 * CLASSES :, :] = ones.astype(bf16)
    _, other = halves(me_ref, khi_ref.shape[0] // 2)
    back_degree(w_ref, khi_ref[other, :], klo_ref[other, :], send_ref)


def first_own(me_ref, w_ref, khi_ref, klo_ref, mine_ref):
    own, _ = halves(me_ref, khi_ref.shape[0] // 2)
    back_degree(w_ref, khi_ref[own, :], klo_ref[own, :], mine_ref)


def flip_kernel(in_ref, out_ref):
    for col in range(0, in_ref.shape[1], 256):
        out_ref[col : col + 256, :] = in_ref[:, col : col + 256].T


def product_own(me_ref, w_ref, thi_ref, tlo_ref, mine_ref):
    own, _ = halves(me_ref, thi_ref.shape[1] // 2)
    mine_ref[...] = back_rows(w_ref, thi_ref[:, own], tlo_ref[:, own], NN)[0]


def residual_part(sums_ref, mid_ref, at, dinv_ref):
    size = sums_ref.shape[1] - LANES
    for k in range(size // LANES):
        dinv_ref[:, k * LANES : (k + 1) * LANES] = 1.0 / sums_ref[k : k + 1, size:]
    return mid_ref[:, at] - sums_ref[:, 0:size] * dinv_ref[...]


def second_own(me_ref, held_ref, mid_ref, khi_ref, klo_ref, part_ref, dinv_ref):
    own, _ = halves(me_ref, khi_ref.shape[0] // 2)
    part_ref[...] = times(pieces(residual_part(held_ref, mid_ref, own, dinv_ref)), khi_ref[own, :], klo_ref[own, :])


def second_send(me_ref, got_ref, mid_ref, khi_ref, klo_ref, thi_ref, tlo_ref, tinv_ref, part_ref, dinv_own, send_ref, w_ref, dinv_ref, dinv_other):
    own, other = halves(me_ref, khi_ref.shape[0] // 2)
    rest = times(pieces(residual_part(got_ref, mid_ref, other, dinv_other)), khi_ref[other, :], klo_ref[other, :])
    dinv_ref[:, own] = dinv_own[...]
    dinv_ref[:, other] = dinv_other[...]
    tinv = tinv_ref[...]
    put_weights(w_ref, (part_ref[...] + rest) * tinv, tinv)
    send_ref[...] = back_rows(w_ref, thi_ref[:, other], tlo_ref[:, other], NN)[0]


def label_image(rhs_ref, zhi_ref, zlo_ref, lab_ref):
    zhi, zlo = zhi_ref[...], zlo_ref[...]
    lab_ref[...] = times_back(times(pieces(rhs_ref[...]), zhi, zlo), zhi, zlo)


def image_shift(lab_scale, lab, rhs):
    return lab_scale * mean_of(lab) + ridge * mean_of(rhs)


def third_own(lab_scale, graph_scale, me_ref, held_ref, rhs_ref, lab_ref, khi_ref, klo_ref, part_ref):
    own, _ = halves(me_ref, khi_ref.shape[0] // 2)
    shift = image_shift(lab_scale, lab_ref[...], rhs_ref[...])
    image = lab_scale * lab_ref[:, own] + graph_scale * held_ref[...] + ridge * rhs_ref[:, own]
    part_ref[...] = times(pieces(image - shift), khi_ref[own, :], klo_ref[own, :])


def third_send(lab_scale, graph_scale, me_ref, held_ref, got_ref, rhs_ref, lab_ref, part_ref, spread0_ref, khi_ref, klo_ref,
               thi_ref, tlo_ref, tinv_ref, send_ref, w_ref, spread_ref, direc_ref, mid_ref, first_ref, stats_ref, whole):
    own, other = halves(me_ref, khi_ref.shape[0] // 2)
    rhs, lab = rhs_ref[...], lab_ref[...]
    whole[:, own] = held_ref[...]
    whole[:, other] = got_ref[...]
    image = lab_scale * lab + graph_scale * whole[...] + ridge * rhs
    shift = image_shift(lab_scale, lab, rhs)
    whole[...] = image - shift
    rest = times(pieces(whole[:, other]), khi_ref[other, :], klo_ref[other, :])
    norm = total_of(rhs * rhs)
    alpha = norm / total_of(rhs * image)
    resid = rhs - alpha * image
    after = total_of(resid * resid)
    beta = after / norm
    direc = resid + beta * rhs
    base = mean_of(rhs)
    level = (1.0 + beta) * base - alpha * shift
    direc_ref[...] = direc
    mid_ref[...] = direc - level
    first_ref[...] = alpha * rhs
    tinv = tinv_ref[...]
    spread = (1.0 + beta) * spread0_ref[...] - alpha * ((part_ref[...] + rest) * tinv)
    put_weights(w_ref, spread, tinv)
    send_ref[...] = back_rows(w_ref, thi_ref[:, other], tlo_ref[:, other], NN)[0]
    spread_ref[...] = spread
    stats_ref[0:CLASSES, :] = jnp.broadcast_to(level, (CLASSES, LANES))
    stats_ref[CLASSES : 2 * CLASSES, :] = jnp.broadcast_to(alpha * base, (CLASSES, LANES))
    stats_ref[2 * CLASSES : 2 * CLASSES + 8, :] = jnp.broadcast_to(alpha, (8, LANES))
    stats_ref[2 * CLASSES + 8 :, :] = jnp.broadcast_to(after, (8, LANES))


def doc_parts(na, lab_scale, me_ref, spread0_ref, spread_ref, stats_ref, direc_ref, zhi_ref, zlo_ref, *refs):
    outs, (base_ref, slots) = refs[0:na], refs[na:]
    quarter = CLASSES // na
    part = stats_ref[2 * CLASSES : 2 * CLASSES + 1, 0:1] * spread0_ref[...] + stats_ref[CLASSES : 2 * CLASSES, 0:1]
    full = spread_ref[...] + stats_ref[0:CLASSES, 0:1]
    for k in range(na):
        slots[k, 0:quarter, :] = part[k * quarter : (k + 1) * quarter]
        slots[k, quarter : 2 * quarter, :] = full[k * quarter : (k + 1) * quarter]
    for mask in range(na):
        outs[mask][...] = slots[(me_ref[0] % na) ^ mask]
    direc = direc_ref[...]
    seen = times(pieces(direc), zhi_ref[...], zlo_ref[...])
    base_ref[...] = jnp.broadcast_to(lab_scale * total_of(seen * seen) + ridge * total_of(direc * direc), base_ref.shape)


def last_kernel(na, graph_scale, me_ref, held_ref, got_ref, direc_ref, mid_ref, first_ref, stats_ref, base_ref, dinv_ref, *refs):
    parts, (anchor_ref, doc_ref, whole) = refs[0:na], refs[na:]
    mine = me_ref[0] % na
    own, other = halves(me_ref, whole.shape[1] // 2)
    whole[:, own] = held_ref[...]
    whole[:, other] = got_ref[...]
    prod = whole[...]
    quad = total_of(prod * (mid_ref[...] - prod * dinv_ref[...]))
    alpha = stats_ref[2 * CLASSES + 8 : 2 * CLASSES + 9, 0:1] / (base_ref[0:1, 0:1] + graph_scale * quad)
    whole[...] = first_ref[...] + alpha * direc_ref[...]
    rows = anchor_ref.shape[1]
    anchor_ref[...] = whole[:, pl.ds(pl.multiple_of(mine * rows, rows), rows)]
    quarter, docs = doc_ref.shape[0], parts[0].shape[1]
    for mask in range(na):
        at = pl.ds(pl.multiple_of((mine ^ mask) * docs, docs), docs)
        doc_ref[:, at] = parts[mask][0:quarter, :] + alpha * parts[mask][quarter:, :]


VMEM = pl.BlockSpec(memory_space=pltpu.MemorySpace.VMEM)
SMEM = pl.BlockSpec(memory_space=pltpu.MemorySpace.SMEM)


def in_hbm(value):
    return pltpu.with_memory_space_constraint(value, pltpu.MemorySpace.HBM)


def call(kernel, in_specs, out_shape, scratch, flops=1 << 20, moved=1 << 18):
    return pl.pallas_call(
        kernel,
        in_specs=in_specs,
        out_specs=[VMEM] * len(out_shape),
        out_shape=out_shape,
        scratch_shapes=scratch,
        compiler_params=pltpu.CompilerParams(vmem_limit_bytes=24 << 20),
        cost_estimate=pl.CostEstimate(flops=flops, bytes_accessed=moved, transcendentals=0),
    )


def run(features, anchors, lab_index, lab_class):
    docs_dev, feat = features.shape
    nd, na = lax.axis_size("docs"), lax.axis_size("anch")
    n_bits = (nd * na).bit_length() - 1
    a_bits = na.bit_length() - 1
    labs = lab_index.shape[0]
    labeled = labs * nd
    quarter = anchors.shape[0]
    total = quarter * na
    docs = docs_dev // na
    lab_scale = total / labeled
    graph_scale = total * total / (docs_dev * nd)
    assert na == 4 and nd * na == 1 << n_bits and total // LANES <= CLASSES and feat == LANES
    sds = jax.ShapeDtypeStruct

    me = lax.axis_index(EVERY).astype(jnp.int32).reshape(1)

    own, mine_x, near = pl.pallas_call(
        functools.partial(label_kernel, na),
        grid_spec=pltpu.PrefetchScalarGridSpec(
            num_scalar_prefetch=3,
            grid=(1,),
            in_specs=[pl.BlockSpec(memory_space=pltpu.MemorySpace.HBM)] * 2,
            out_specs=[VMEM] * 3,
            scratch_shapes=[
                pltpu.VMEM((labs, 16, LANES), bf16),
                pltpu.VMEM((2 * labs, LANES), f32),
                pltpu.SemaphoreType.DMA((labs,)),
                pltpu.SemaphoreType.DMA,
                pltpu.SemaphoreType.DMA,
            ],
        ),
        out_shape=[sds((2 * labs, feat), bf16), sds((docs, feat), bf16), sds((quarter, feat), bf16)],
        name="label_rows",
        compiler_params=pltpu.CompilerParams(vmem_limit_bytes=4 << 20),
    )(me, in_hbm(lab_index), in_hbm(lab_class), in_hbm(features), in_hbm(anchors))

    piece = [near, swap_core(anchors), None, None]
    piece[2] = swap(anchors, 2)
    piece[3] = swap(anchors, 3)

    held, masks = own, [0]
    bits = list(range(a_bits, n_bits))
    stages = bit_groups(bits[:1]) + bit_groups(bits[1:])
    for at, stage in enumerate(stages):
        got = exchange(held, stage)
        if at < len(stages) - 1:
            masks = masks + [m ^ mask for mask in stage for m in masks]
            held = jnp.concatenate([held] + got, axis=0)
    lab_arrays = [held] + got
    slots = [[m >> a_bits for m in masks]] + [[(m ^ mask) >> a_bits for m in masks] for mask in stages[-1]]

    k_sds = sds((total, docs), bf16)
    khi, klo, aug = call(
        functools.partial(build_kernel, na),
        [SMEM] + [VMEM] * 5,
        [k_sds, k_sds, sds((total, feat + LANES), bf16)],
        [],
        flops=2 * total * docs * 256,
        moved=4 * total * docs,
    )(me, *piece, mine_x)

    half = total // 2
    flat_sds = sds((CLASSES, total), f32)
    half_sds = sds((CLASSES, half), f32)
    long_sds = sds((CLASSES, half + LANES), f32)
    docs_sds = sds((CLASSES, docs), f32)
    z_sds = sds((total, labeled), bf16)
    w_sds = sds((3 * CLASSES, docs), bf16)
    work = dict(flops=4 * total * docs * 64, moved=2 * total * docs)

    send, w, rhs, middle, zhi, zlo, spread0, tinv = call(
        functools.partial(first_send, na, labs, slots, CLASSES * lab_scale),
        [SMEM] + [VMEM] * (len(lab_arrays) + 3),
        [long_sds, sds((4 * CLASSES, docs), bf16), flat_sds, flat_sds, z_sds, z_sds, docs_sds, sds((1, docs), f32)],
        [pltpu.VMEM((labeled, feat), bf16), pltpu.VMEM((labeled, LANES), f32)],
        **work,
    )(me, *lab_arrays, aug, khi, klo)
    got = swap_core(send)
    mine = call(first_own, [SMEM] + [VMEM] * 3, [long_sds], [], **work)(me, w, khi, klo)[0]
    held = reduce_chips(mine + got, n_bits)
    thi = call(flip_kernel, [VMEM], [sds((docs, total), bf16)], [])(khi)[0]
    tlo = call(flip_kernel, [VMEM], [sds((docs, total), bf16)], [])(klo)[0]
    lab = call(label_image, [VMEM] * 3, [flat_sds], [])(rhs, zhi, zlo)[0]

    got = swap_core(held)
    part, dinv_own = call(
        second_own, [SMEM] + [VMEM] * 4, [docs_sds, sds((1, half), f32)], [], **work
    )(me, held, middle, khi, klo)
    send, w, dinv = call(
        second_send, [SMEM] + [VMEM] * 9, [half_sds, w_sds, sds((1, total), f32)], [pltpu.VMEM((1, half), f32)], **work
    )(me, got, middle, khi, klo, thi, tlo, tinv, part, dinv_own)
    got = swap_core(send)
    mine = call(product_own, [SMEM] + [VMEM] * 3, [half_sds], [], **work)(me, w, thi, tlo)[0]
    held = reduce_chips(mine + got, n_bits)

    got = swap_core(held)
    part = call(
        functools.partial(third_own, lab_scale, graph_scale), [SMEM] + [VMEM] * 5, [docs_sds], [], **work
    )(me, held, rhs, lab, khi, klo)[0]
    send, w, spread, direc, middle, first, stats = call(
        functools.partial(third_send, lab_scale, graph_scale),
        [SMEM] + [VMEM] * 11,
        [half_sds, w_sds, docs_sds, flat_sds, flat_sds, flat_sds, sds((2 * CLASSES + 16, LANES), f32)],
        [pltpu.VMEM((CLASSES, total), f32)],
        **work,
    )(me, held, got, rhs, lab, part, spread0, khi, klo, thi, tlo, tinv)
    got = swap_core(send)
    mine = call(product_own, [SMEM] + [VMEM] * 3, [half_sds], [], **work)(me, w, thi, tlo)[0]
    part_rows = 2 * CLASSES // na
    *docs_out, base = call(
        functools.partial(doc_parts, na, lab_scale),
        [SMEM] + [VMEM] * 6,
        [sds((part_rows, docs), f32)] * na + [sds((8, LANES), f32)],
        [pltpu.VMEM((na, part_rows, docs), f32)],
    )(me, spread0, spread, stats, direc, zhi, zlo)
    held = reduce_chips(mine + got, n_bits)
    got = swap_core(held)

    parts = [docs_out[0]]
    for mask in range(1, na):
        parts.append(swap(docs_out[mask], mask))
    anchor_scores, doc_scores = call(
        functools.partial(last_kernel, na, graph_scale),
        [SMEM] + [VMEM] * (8 + na),
        [sds((CLASSES, quarter), f32), sds((CLASSES // na, docs_dev), f32)],
        [pltpu.VMEM((CLASSES, total), f32)],
    )(me, held, got, direc, middle, first, stats, base, dinv, *parts)
    return anchor_scores.T, doc_scores


def solution(mesh):
    in_specs = (P("docs", None), P("anch", None), P("docs"), P("docs"))
    out_specs = (P("anch", None), P("anch", "docs"))
    return jax.shard_map(run, mesh=mesh, in_specs=in_specs, out_specs=out_specs, check_vma=False)
```
